32 devices in a mesh: fsdp: 16 (over z, x, core), tensor: 2 (over y).
Axes of the slice: x: 2, y: 2, z: 4, core: 2. Of those that a mesh axis runs over, the one named last changes fastest.
Arguments:
- tokens: bfloat16 [2, 1024, 16, 1024], P(None, 'tensor', 'fsdp'), may hold values from -6 to 6
- piece_starts: int32 [2, 16, 3], P(None, 'fsdp'), may hold values from 0 to 1024, as said below
- gain_attn: float32 [1024], P(('fsdp', 'tensor')), may hold values from 0.25 to 1.75
- w_qkv: bfloat16 [3, 1024, 1024], P(None, 'fsdp', 'tensor'), may hold values from -0.1875 to 0.1875
- w_out: bfloat16 [1024, 1024], P('tensor', 'fsdp'), may hold values from -1.5 to 1.5
- gain_mlp: float32 [1024], P(('fsdp', 'tensor')), may hold values from 0.25 to 1.75
- w_gate_up: bfloat16 [2, 1024, 4096], P(None, 'fsdp', 'tensor'), may hold values from -0.1875 to 0.1875
- w_down: bfloat16 [4096, 1024], P('tensor', 'fsdp'), may hold values from -0.09375 to 0.09375
- out_grad: bfloat16 [2, 1024, 16, 1024], P(None, 'tensor', 'fsdp'), may hold values from -6 to 6
Outputs:
- layer_out: bfloat16 [2, 1024, 16, 1024], P(None, 'tensor', 'fsdp')
- input_grad: float32 [2, 1024, 16, 1024], P(None, 'tensor', 'fsdp')
- grad_gain_attn: float32 [1024], P(('fsdp', 'tensor'))
- grad_qkv: float32 [3, 1024, 1024], P(None, 'fsdp', 'tensor')
- grad_out: float32 [1024, 1024], P('tensor', 'fsdp')
- feedforward_gain_gradient: float32 [1024], P(('fsdp', 'tensor'))
- grad_gate_up: float32 [2, 1024, 4096], P(None, 'fsdp', 'tensor')
- grad_down: float32 [4096, 1024], P('tensor', 'fsdp')
The draws below stay inside these ranges and needn't reach their ends.
Inputs may be any that keep to these rules, and one draw needn't show every extreme that they name: `piece_starts`: entry p of a row is the first position of picture piece p of that sequence; each piece covers 256 positions inside the sequence, pieces do not intersect and come in rising order; an entry equal to 1024 marks an unused slot, and unused slots follow the used ones.
All inputs are finite; a program needn't handle non-finite values.
Results may differ from the reference program's by a relative error of at most 0.022.
Values may be sent and summed in bfloat16 or wider, within the bound.
No kernel may reach another device: no remote copies, remote signals or barrier semaphores. Data moves between devices by JAX's collectives and lax.ppermute only.
A program may use at most 384 MiB of HBM per device.

```python
import jax
import jax.numpy as jnp
from jax import lax

D = 1024
HEADS = 16
HEAD_DIM = 64
FF = 4096
MICRO = 2
QBLOCK = 512
PIECE = 256
PIECES = 3
LENGTH = 1024
SEQS = 16


def draw_piece_starts(key, part):
    spacing = LENGTH // PIECES
    split_keys = jax.random.split(key, 2)
    offsets = jax.random.randint(split_keys[0], (MICRO, SEQS, PIECES), 0, spacing - PIECE + 1, dtype=jnp.int32)
    offsets = offsets.at[0, 0, 0].set(0)
    counts = jax.random.randint(split_keys[1], (MICRO, SEQS), 0, PIECES + 1, dtype=jnp.int32)
    counts = counts.at[0, 0].set(PIECES).at[MICRO - 1, SEQS - 1].set(0)
    slot_index = jnp.arange(PIECES, dtype=jnp.int32)
    starts = slot_index[None, None, :] * spacing + offsets
    return jnp.where(slot_index[None, None, :] < counts[:, :, None], starts, LENGTH).astype(jnp.int32)


def strengthened(values, own_key, source, target, parts, factor):
    def block_of(dim):
        return (jnp.arange(values.shape[dim]) // (values.shape[dim] // parts)).reshape((-1,) + (1,) * (values.ndim - 1 - dim))

    one_side = jax.random.permutation(own_key, parts)[block_of(target)]
    other_side = (block_of(target) + parts // 2) % parts
    return jnp.where((block_of(source) == one_side) | (block_of(source) == other_side), factor * values, values)


def steps_of(stream_key, shape, pieces, least, high):
    factor_of = 1.0
    for axis_at, shards_of in pieces:
        draws = jax.random.uniform(jax.random.fold_in(jax.random.fold_in(stream_key, 6), axis_at), (shards_of,), jnp.float32, least / len(pieces), high / len(pieces))
        factor_of = factor_of * jnp.repeat(jnp.exp(draws), shape[axis_at] // shards_of).reshape((-1,) + (1,) * (len(shape) - 1 - axis_at))
    return factor_of


def gaussian(own_key, extent, scale, bound, cuts=(), kind=jnp.bfloat16):
    entries = jax.random.normal(own_key, extent, jnp.float32) * scale
    if len(cuts) > 0:
        entries = steps_of(own_key, extent, cuts, -0.22, 0.18) * entries
    return jnp.clip(entries, min=-bound, max=bound).astype(kind)


def noise_with(own_key, extent, deviation, most, cuts, heavy, kind=jnp.bfloat16):
    drawn = deviation * jax.random.normal(own_key, extent, jnp.float32)
    if cuts:
        drawn = drawn * steps_of(own_key, extent, cuts, -0.22, 0.18)
    return jnp.clip(strengthened(drawn, jax.random.fold_in(own_key, 3), *heavy), -most, most).astype(kind)


def setup_inputs(seed: int = 0) -> dict:
    splits = jax.random.split(jax.random.key(seed), 10)
    return {
        "tokens": gaussian(splits[0], (MICRO, LENGTH, SEQS, D), 1.0, 6.0, ((1, 2), (2, 16))),
        "piece_starts": draw_piece_starts(jax.random.fold_in(splits[9], 71), 0),
        "gain_attn": jnp.clip(1.0 + 0.15 * jax.random.normal(splits[2], (D,), jnp.float32), 0.25, 1.75),
        "w_qkv": gaussian(splits[3], (3, D, D), D ** -0.5, 0.1875, ((1, 16), (2, 2))),
        "w_out": gaussian(splits[4], (D, D), (max(1, D // 64)) ** -0.5, 1.5, ((0, 2), (1, 16))),
        "gain_mlp": jnp.clip(1.0 + 0.15 * jax.random.normal(splits[5], (D,), jnp.float32), 0.25, 1.75),
        "w_gate_up": gaussian(splits[6], (2, D, FF), D ** -0.5, 0.1875, ((1, 16), (2, 2))),
        "w_down": gaussian(splits[7], (FF, D), FF ** -0.5, 0.09375, ((0, 2), (1, 16))),
        "out_grad": noise_with(splits[8], (MICRO, LENGTH, SEQS, D), 1.0, 6.0, ((1, 2), (2, 16)), (2, 3, 16, 2.0)),
    }


@jax.custom_vjp
def low(v):
    return lax.optimization_barrier(v.astype(jnp.bfloat16)).astype(jnp.float32)

@jax.custom_vjp
def low_back(v):
    return v

def low_keep(v):
    return (low(v), None)

def low_pass(kept, grad):
    return (grad,)

def back_keep(v):
    return (v, None)

def back_low(kept, grad):
    return (low(grad),)
low.defvjp(low_keep, low_pass)
low_back.defvjp(back_keep, back_low)
norm_eps = 1e-05
masked_score = -1e+30
highest = lax.Precision.HIGHEST

def rms_scale(values_float_rows):
    return lax.rsqrt(lax.optimization_barrier(jnp.mean(values_float_rows * values_float_rows, axis=-1, keepdims=True)) + norm_eps)

def piece_index_labels(starts_row):
    positions = jnp.arange(LENGTH, dtype=jnp.int32)[:, None]
    inside = (positions >= starts_row[None, :]) & (positions < starts_row[None, :] + PIECE)
    numbers = jnp.arange(1, PIECES + 1, dtype=jnp.int32)
    return lax.optimization_barrier(jnp.sum(jnp.where(inside, numbers[None, :], 0), axis=1)).astype(jnp.int32)

def attention_block(first_row, queries, keys_all, values_all, labels):
    block_q = lax.dynamic_slice_in_dim(queries, first_row, QBLOCK, 0)
    row_labels = lax.dynamic_slice_in_dim(labels, first_row, QBLOCK, 0)
    row_ids = first_row + jnp.arange(QBLOCK, dtype=jnp.int32)
    col_ids = jnp.arange(labels.shape[0], dtype=jnp.int32)
    causal = col_ids[None, :] <= row_ids[:, None]
    same_piece = (row_labels[:, None] == labels[None, :]) & (row_labels[:, None] > 0)
    allowed = causal | same_piece
    scores = low_back(jnp.einsum('qhd,khd->hqk', block_q, keys_all, precision=highest) * HEAD_DIM ** (-0.5))
    scores = jnp.where(allowed[None], scores, masked_score)
    row_max = lax.optimization_barrier(jnp.max(scores, axis=-1, keepdims=True))
    exp_scores = jnp.exp(scores - row_max)
    attn_probs = low(exp_scores / lax.optimization_barrier(jnp.sum(exp_scores, axis=-1, keepdims=True)))
    return jnp.einsum('hqk,khd->qhd', attn_probs, values_all, precision=highest)

def layer(rows_f32, gain_attn, w_qkv, w_out, gain_mlp, w_gate_up, w_down, labels):
    length = rows_f32.shape[0]
    pre_attn = rows_f32 * rms_scale(rows_f32)
    normed = low(pre_attn * gain_attn)
    qkv_low = low(low_back(jnp.einsum('ld,cde->lce', normed, w_qkv, precision=highest)))
    head_view = qkv_low.reshape(length, 3, HEADS, HEAD_DIM)
    checked = jax.checkpoint(attention_block)
    firsts = jnp.arange(length // QBLOCK, dtype=jnp.int32) * QBLOCK
    blocks = lax.map(lambda first_row: checked(first_row, head_view[:, 0], head_view[:, 1], head_view[:, 2], labels), firsts)
    attended = low(low_back(blocks.reshape(length, D)))
    attn_part = low_back(jnp.dot(attended, w_out, precision=highest))
    hidden = rows_f32 + attn_part
    pre_mlp = hidden * rms_scale(hidden)
    normed_mlp = low(pre_mlp * gain_mlp)
    gate_up = low_back(jnp.einsum('ld,cdf->lcf', normed_mlp, w_gate_up, precision=highest))
    gate_part = gate_up[:, 0]
    mixed_lowp_rows = low(gate_part * jax.nn.sigmoid(gate_part) * gate_up[:, 1])
    return hidden + low_back(jnp.dot(mixed_lowp_rows, w_down, precision=highest))

def reference(tokens, piece_starts, gain_attn, w_qkv, w_out, gain_mlp, w_gate_up, w_down, out_grad):
    weights = (gain_attn.astype(jnp.float32), w_qkv.astype(jnp.float32), w_out.astype(jnp.float32), gain_mlp.astype(jnp.float32), w_gate_up.astype(jnp.float32), w_down.astype(jnp.float32))
    rows_in = jnp.transpose(tokens.astype(jnp.float32), (0, 2, 1, 3)).reshape(MICRO * SEQS, LENGTH, D)
    grads_in = jnp.transpose(out_grad.astype(jnp.float32), (0, 2, 1, 3)).reshape(MICRO * SEQS, LENGTH, D)
    starts_in = piece_starts.reshape(MICRO * SEQS, PIECES).astype(jnp.int32)

    def one_seq(totals, seq_items):
        rows_f32, cotangent, starts_row = seq_items
        labels = piece_index_labels(starts_row)

        def forward(rows_now, gain_one, qkv_w, out_w, gain_two, gate_up_w, down_w):
            return layer(rows_now, gain_one, qkv_w, out_w, gain_two, gate_up_w, down_w, labels)
        result, pullback = jax.vjp(forward, rows_f32, *weights)
        grad_list = pullback(cotangent)
        new_totals = tuple((total_now + grad_now for total_now, grad_now in zip(totals, grad_list[1:])))
        return (new_totals, (result.astype(jnp.bfloat16), grad_list[0]))
    zero_sums = tuple((jnp.zeros(weight.shape, jnp.float32) for weight in weights))
    totals, (seq_outs, seq_grads) = lax.scan(one_seq, zero_sums, (rows_in, grads_in, starts_in))
    layer_out = jnp.transpose(seq_outs.reshape(MICRO, SEQS, LENGTH, D), (0, 2, 1, 3))
    input_grad = jnp.transpose(seq_grads.reshape(MICRO, SEQS, LENGTH, D), (0, 2, 1, 3))
    return (layer_out, input_grad, totals[0], totals[1], totals[2], totals[3], totals[4], totals[5])
```

```python
import jax
import jax.numpy as jnp
from jax import lax
from jax.experimental import pallas as pl
from jax.experimental.pallas import tpu as pltpu
from jax.sharding import PartitionSpec as P

D = 1024
HEAD_DIM = 64
QBLOCK = 512
PIECE = 256


norm_eps = 1e-05
masked_score = -1e30


def rms_scale(values_float_rows):
    return lax.rsqrt(
        jnp.mean(values_float_rows * values_float_rows, axis=-1, keepdims=True) + norm_eps
    )


def norm_backward_pass(d_normed, normed_pre, scale_rows, gain_vector_row):
    d_scaled = d_normed * gain_vector_row
    return scale_rows * (
        d_scaled - normed_pre * jnp.mean(d_scaled * normed_pre, axis=-1, keepdims=True)
    )


def piece_index_labels(starts_row, length):
    positions = jnp.arange(length, dtype=jnp.int32)[:, None]
    inside = (positions >= starts_row[None, :]) & (positions < starts_row[None, :] + PIECE)
    numbers = jnp.arange(1, starts_row.shape[0] + 1, dtype=jnp.int32)
    return jnp.sum(jnp.where(inside, numbers[None, :], 0), axis=1)


def allowed_block(labels, first_row, key_count):
    row_ids = first_row + jnp.arange(QBLOCK, dtype=jnp.int32)
    col_ids = jnp.arange(key_count, dtype=jnp.int32)
    row_labels = labels[first_row : first_row + QBLOCK]
    causal = col_ids[None, :] <= row_ids[:, None]
    same_piece = (row_labels[:, None] == labels[None, :]) & (row_labels[:, None] > 0)
    return causal | same_piece


def attend_forward(queries, keys_all, values_all, labels, key_spans):
    score_scale = HEAD_DIM ** (-0.5)
    outputs = []
    totals = []
    for first_row, key_count in key_spans:
        block_q = queries[first_row : first_row + QBLOCK]
        scores = (
            jnp.einsum("qhd,khd->hqk", block_q, keys_all, preferred_element_type=jnp.float32)
            * score_scale
        )
        scores = jnp.where(allowed_block(labels, first_row, key_count)[None], scores, masked_score)
        row_max = jnp.max(scores, axis=-1, keepdims=True)
        exp_scores = jnp.exp(scores - row_max)
        row_total = jnp.sum(exp_scores, axis=-1, keepdims=True)
        attn_probs = (exp_scores / row_total).astype(jnp.bfloat16)
        block_out = jnp.einsum(
            "hqk,khd->qhd", attn_probs, values_all, preferred_element_type=jnp.float32
        )
        outputs.append(block_out.astype(jnp.bfloat16))
        totals.append((row_max + jnp.log(row_total))[..., 0])
    return (jnp.concatenate(outputs, 0), jnp.concatenate(totals, 1))


def attend_backward(queries, keys_all, values_all, labels, log_total, d_heads, key_spans):
    score_scale = HEAD_DIM ** (-0.5)
    query_parts = []
    d_keys = jnp.zeros(keys_all.shape, jnp.float32)
    d_values = jnp.zeros(values_all.shape, jnp.float32)
    for first_row, key_count in key_spans:
        block_q = queries[first_row : first_row + QBLOCK]
        block_d = d_heads[first_row : first_row + QBLOCK]
        scores = (
            jnp.einsum("qhd,khd->hqk", block_q, keys_all, preferred_element_type=jnp.float32)
            * score_scale
        )
        mask_now = allowed_block(labels, first_row, key_count)[None]
        attn_probs = jnp.where(
            mask_now, jnp.exp(scores - log_total[:, first_row : first_row + QBLOCK, None]), 0.0
        )
        probs_low = attn_probs.astype(jnp.bfloat16)
        d_probs = jnp.einsum(
            "qhd,khd->hqk", block_d, values_all, preferred_element_type=jnp.float32
        )
        row_dot = jnp.sum(attn_probs * d_probs, axis=-1, keepdims=True)
        d_scores = (attn_probs * (d_probs - row_dot)).astype(jnp.bfloat16)
        query_parts.append(
            jnp.einsum("hqk,khd->qhd", d_scores, keys_all, preferred_element_type=jnp.float32)
            * score_scale
        )
        d_keys = d_keys.at[:key_count].add(
            jnp.einsum("hqk,qhd->khd", d_scores, block_q, preferred_element_type=jnp.float32)
            * score_scale
        )
        d_values = d_values.at[:key_count].add(
            jnp.einsum("hqk,qhd->khd", probs_low, block_d, preferred_element_type=jnp.float32)
        )
    return (jnp.concatenate(query_parts, 0), d_keys, d_values)


def attention_forward(qkv_low, labels_all, key_spans):
    length, seq_count, width = (qkv_low.shape[0], qkv_low.shape[1], qkv_low.shape[3])
    per_seq = jnp.moveaxis(qkv_low, 1, 0).reshape(seq_count, length, 3, width // HEAD_DIM, HEAD_DIM)

    def one_seq(seq_items):
        seq_qkv, labels = seq_items
        return attend_forward(seq_qkv[:, 0], seq_qkv[:, 1], seq_qkv[:, 2], labels, key_spans)

    seq_outs, totals = lax.map(one_seq, (per_seq, labels_all))
    return (jnp.moveaxis(seq_outs.reshape(seq_count, length, width), 0, 1), totals)


def attention_backward(qkv_low, labels_all, totals, d_attended, key_spans):
    length, seq_count, width = (qkv_low.shape[0], qkv_low.shape[1], qkv_low.shape[3])
    per_seq = jnp.moveaxis(qkv_low, 1, 0).reshape(seq_count, length, 3, width // HEAD_DIM, HEAD_DIM)
    d_seq = jnp.moveaxis(d_attended, 1, 0).reshape(seq_count, length, width // HEAD_DIM, HEAD_DIM)

    def one_seq(seq_items):
        seq_qkv, labels, log_total, seq_d = seq_items
        d_query, d_keys, d_values = attend_backward(
            seq_qkv[:, 0], seq_qkv[:, 1], seq_qkv[:, 2], labels, log_total, seq_d, key_spans
        )
        return jnp.stack([d_query, d_keys, d_values], 1).astype(jnp.bfloat16)

    seq_grads = lax.map(one_seq, (per_seq, labels_all, totals, d_seq))
    return jnp.moveaxis(seq_grads, 0, 1).reshape(length, seq_count, 3, width)


def fetch_weights(w_qkv, w_out, w_gate_up, w_down):
    qkv_all, out_all, gate_up_all, down_weight_full = (
        lax.all_gather(w_qkv, "fsdp", axis=1, tiled=True),
        lax.all_gather(w_out, "fsdp", axis=1, tiled=True),
        lax.all_gather(w_gate_up, "fsdp", axis=1, tiled=True),
        lax.all_gather(w_down, "fsdp", axis=1, tiled=True),
    )
    return (qkv_all, out_all, gate_up_all, down_weight_full)


def local(tokens, piece_starts, gain_attn, w_qkv, w_out, gain_mlp, w_gate_up, w_down, out_grad):
    both_gains = lax.all_gather(
        jnp.stack([gain_attn, gain_mlp]), ("fsdp", "tensor"), axis=1, tiled=True
    )
    local_rows = tokens.shape[1]
    length = local_rows * lax.axis_size("tensor")
    key_spans = [(first_row, length) for first_row in range(0, length, QBLOCK)]

    def label_row(starts_row):
        return piece_index_labels(starts_row, length)

    labels_every = jax.vmap(jax.vmap(label_row))(piece_starts)
    ff_cols = w_gate_up.shape[2]
    acc_gain = jnp.zeros((2, D), jnp.float32)
    acc_qkv = jnp.zeros((3, D, w_qkv.shape[2]), jnp.float32)
    acc_out = jnp.zeros((w_out.shape[0], D), jnp.float32)
    acc_gate_up = jnp.zeros((2, D, ff_cols), jnp.float32)
    acc_down = jnp.zeros((ff_cols, D), jnp.float32)
    layer_outs = []
    input_grads = []
    for micro_idx in range(tokens.shape[0]):
        weights = fetch_weights(w_qkv, w_out, w_gate_up, w_down)
        qkv_all, out_all, gate_up_all, down_weight_full = weights
        rows_f32 = tokens[micro_idx].astype(jnp.float32)
        scale_attn = rms_scale(rows_f32)
        pre_attn = rows_f32 * scale_attn
        normed = (pre_attn * both_gains[0]).astype(jnp.bfloat16)
        piece_rows = lax.all_gather(normed, "tensor", axis=0, tiled=True)
        made = jnp.einsum("lsd,cde->lsce", piece_rows, qkv_all, preferred_element_type=jnp.float32)
        qkv_low = made.astype(jnp.bfloat16)
        attended, log_total = attention_forward(qkv_low, labels_every[micro_idx], key_spans)
        rows_now = lax.slice_in_dim(attended, 0, local_rows * lax.axis_size("tensor"), axis=0)
        attn_part = lax.psum_scatter(
            jnp.einsum("lsc,cd->lsd", rows_now, out_all, preferred_element_type=jnp.float32).astype(
                jnp.bfloat16
            ),
            "tensor",
            scatter_dimension=0,
            tiled=True,
        ).astype(jnp.float32)
        hidden = rows_f32 + attn_part
        scale_mlp = rms_scale(hidden)
        pre_mlp = hidden * scale_mlp
        normed_mlp = (pre_mlp * both_gains[1]).astype(jnp.bfloat16)
        expand_piece_rows = lax.all_gather(normed_mlp, "tensor", axis=0, tiled=True)
        gate_up = jnp.einsum(
            "lsd,cdf->lscf", expand_piece_rows, gate_up_all, preferred_element_type=jnp.float32
        )
        gate_part = gate_up[:, :, 0]
        up_part = gate_up[:, :, 1]
        sigmoid_gate = jax.nn.sigmoid(gate_part)
        activated = gate_part * sigmoid_gate
        mixed_lowp_rows = (activated * up_part).astype(jnp.bfloat16)
        down_rows_now = lax.slice_in_dim(
            mixed_lowp_rows, 0, local_rows * lax.axis_size("tensor"), axis=0
        )
        mlp_part = lax.psum_scatter(
            jnp.einsum(
                "meg,gp->mep", down_rows_now, down_weight_full, preferred_element_type=jnp.float32
            ).astype(jnp.bfloat16),
            "tensor",
            scatter_dimension=0,
            tiled=True,
        ).astype(jnp.float32)
        layer_outs.append((hidden + mlp_part).astype(jnp.bfloat16))
        qkv_all, out_all, gate_up_all, down_weight_full = fetch_weights(
            w_qkv, w_out, w_gate_up, w_down
        )
        grad_rows = out_grad[micro_idx]
        down_piece_rows = lax.all_gather(grad_rows, "tensor", axis=0, tiled=True)
        d_mixed = jnp.einsum(
            "xum,tm->xut", down_piece_rows, down_weight_full, preferred_element_type=jnp.float32
        )
        acc_down = acc_down + jnp.einsum(
            "zmp,zme->pe", mixed_lowp_rows, down_piece_rows, preferred_element_type=jnp.float32
        )
        d_gate = d_mixed * up_part * sigmoid_gate * (1.0 + gate_part * (1.0 - sigmoid_gate))
        d_up = d_mixed * activated
        d_gate_up = jnp.stack([d_gate, d_up], 2).astype(jnp.bfloat16)
        acc_gate_up = acc_gate_up + jnp.einsum(
            "lsd,lscf->cdf", expand_piece_rows, d_gate_up, preferred_element_type=jnp.float32
        )
        mlp_rows_now = lax.slice_in_dim(d_gate_up, 0, local_rows * lax.axis_size("tensor"), axis=0)
        d_normed_mlp = lax.psum_scatter(
            jnp.einsum(
                "lscf,cdf->lsd", mlp_rows_now, gate_up_all, preferred_element_type=jnp.float32
            ).astype(jnp.bfloat16),
            "tensor",
            scatter_dimension=0,
            tiled=True,
        ).astype(jnp.float32)
        gain_mlp_part = jnp.sum(d_normed_mlp * pre_mlp, axis=(0, 1))
        d_hidden = grad_rows.astype(jnp.float32) + norm_backward_pass(
            d_normed_mlp, pre_mlp, scale_mlp, both_gains[1]
        )
        attention_gradient_lowp = d_hidden.astype(jnp.bfloat16)
        out_piece_rows = lax.all_gather(attention_gradient_lowp, "tensor", axis=0, tiled=True)
        out_made = jnp.einsum(
            "lsd,cd->lsc", out_piece_rows, out_all, preferred_element_type=jnp.float32
        )
        d_attended = out_made.astype(jnp.bfloat16)
        acc_out = acc_out + jnp.einsum(
            "lsc,lsd->cd", attended, out_piece_rows, preferred_element_type=jnp.float32
        )
        d_qkv = attention_backward(
            qkv_low, labels_every[micro_idx], log_total, d_attended, key_spans
        )
        acc_qkv = acc_qkv + jnp.einsum(
            "lsd,lsce->cde", piece_rows, d_qkv, preferred_element_type=jnp.float32
        )
        d_normed = lax.psum_scatter(
            jnp.einsum("lsce,cde->lsd", d_qkv, qkv_all, preferred_element_type=jnp.float32).astype(
                jnp.bfloat16
            ),
            "tensor",
            scatter_dimension=0,
            tiled=True,
        ).astype(jnp.float32)
        gain_attn_part = jnp.sum(d_normed * pre_attn, axis=(0, 1))
        input_grads.append(
            d_hidden + norm_backward_pass(d_normed, pre_attn, scale_attn, both_gains[0])
        )
        acc_gain = acc_gain + jnp.stack([gain_attn_part, gain_mlp_part])
    gain_rows, qkv_rows, out_rows_sum, gate_up_rows, down_rows_sum = (
        lax.psum_scatter(
            acc_gain.astype(jnp.bfloat16), "fsdp", scatter_dimension=1, tiled=True
        ).astype(jnp.float32),
        lax.psum_scatter(
            acc_qkv.astype(jnp.bfloat16), "fsdp", scatter_dimension=1, tiled=True
        ).astype(jnp.float32),
        lax.psum_scatter(
            acc_out.astype(jnp.bfloat16), "fsdp", scatter_dimension=1, tiled=True
        ).astype(jnp.float32),
        lax.psum_scatter(
            acc_gate_up.astype(jnp.bfloat16), "fsdp", scatter_dimension=1, tiled=True
        ).astype(jnp.float32),
        lax.psum_scatter(
            acc_down.astype(jnp.bfloat16), "fsdp", scatter_dimension=1, tiled=True
        ).astype(jnp.float32),
    )
    gain_shares = lax.psum_scatter(gain_rows, "tensor", scatter_dimension=1, tiled=True)
    return (
        jnp.stack(layer_outs, 0),
        jnp.stack(input_grads, 0),
        gain_shares[0],
        qkv_rows,
        out_rows_sum,
        gain_shares[1],
        gate_up_rows,
        down_rows_sum,
    )


BF = jnp.bfloat16
F32 = jnp.float32
TILE = 256


def dot_f32(a, b, ca, cb):
    return lax.dot_general(a, b, (((ca,), (cb,)), ((), ())), preferred_element_type=F32)


def call(body, name, ids, ins, in_specs, outs, out_specs, grid, scratch=(), flops=0):
    moved = sum(a.size * a.dtype.itemsize for a in ins) + sum(
        o.size * o.dtype.itemsize for o in outs
    )
    return pl.pallas_call(
        body,
        name=name,
        out_shape=outs,
        grid_spec=pltpu.PrefetchScalarGridSpec(
            num_scalar_prefetch=1,
            grid=grid,
            in_specs=in_specs,
            out_specs=out_specs,
            scratch_shapes=list(scratch),
        ),
        compiler_params=pltpu.CompilerParams(
            dimension_semantics=("arbitrary",) * len(grid), vmem_limit_bytes=56 * 2**20
        ),
        cost_estimate=pl.CostEstimate(flops=flops, bytes_accessed=moved, transcendentals=0),
    )(ids, *ins)


def shape(dims, dtype):
    return jax.ShapeDtypeStruct(dims, dtype)


def whole(dims):
    zeros = (0,) * len(dims)
    return pl.BlockSpec(dims, lambda *_: zeros)


def store_transposed(ids, value, blocks_ref, out_ref):
    count, height = blocks_ref.shape[0], blocks_ref.shape[1]
    step = 128 // height
    for c in range(value.shape[1] // 128):
        part = value[:, c * 128 : (c + 1) * 128]
        blocks_ref[c * step : (c + 1) * step] = part.T.reshape(step, height, part.shape[0])
    for core in range(2):
        for pair in range(count // 2):
            source = 2 * (pair ^ ids[1]) + (core ^ ids[2])
            out_ref[core * (count // 2) + pair] = blocks_ref[source]


def rows_of(ref):
    block = ref[...]
    return block.reshape(block.shape[0] * block.shape[2], block.shape[3])


def make_qkv(ids, x, gain, packed, fsdp, half):
    length, width = x.shape
    height = width // fsdp

    def body(ids, x_ref, gain_ref, w_ref, qkv_ref, xt_ref, xn_ref, blocks_ref):
        @pl.when((pl.program_id(0) == 0) & (pl.program_id(1) == 0))
        def _():
            for r in range(0, length, TILE):
                rows = x_ref[r : r + TILE].astype(F32)
                xn_ref[r : r + TILE] = (rows * rms_scale(rows) * gain_ref[...]).astype(BF)
            store_transposed(ids, xn_ref[...], blocks_ref, xt_ref)

        factor = jnp.where(pl.program_id(0) == 0, HEAD_DIM ** (-0.5), 1.0)
        w = rows_of(w_ref)
        for r in range(0, length, TILE):
            made = dot_f32(xn_ref[r : r + TILE], w, 1, 0)
            qkv_ref[0, r : r + TILE] = (made * factor).astype(BF)

    return call(
        body,
        "qkv",
        ids,
        (x, gain, packed),
        [
            whole((length, width)),
            whole((1, width)),
            pl.BlockSpec((fsdp, 1, height, half), lambda c, t, ids: (0, t, c, 0)),
        ],
        (shape((3, length, width), BF), shape((fsdp, height, length), BF)),
        [
            pl.BlockSpec((1, length, half), lambda c, t, ids: (c, 0, t)),
            whole((fsdp, height, length)),
        ],
        (3, width // half),
        (pltpu.VMEM((length, width), BF), pltpu.VMEM((fsdp, height, length), BF)),
        flops=2 * length * width * 3 * width,
    )


def lane_mask(values, head):
    lanes = lax.broadcasted_iota(jnp.int32, values.shape, 1)
    return jnp.where(lanes // HEAD_DIM == head, values, jnp.zeros_like(values))


def attend(ids, qkv):
    length, width = qkv.shape[1:]
    tiles = length // TILE
    pair = 2 * HEAD_DIM

    def body(ids, q_ref, k_ref, v_ref, o_ref, ot_ref, e_ref, inv_ref, bias_ref, s_ref):
        @pl.when(pl.program_id(0) == 0)
        def _():
            for i in range(tiles):
                keys = i * TILE + lax.broadcasted_iota(jnp.int32, (2 * TILE, TILE), 0)
                rows = i * TILE + lax.broadcasted_iota(jnp.int32, (2 * TILE, TILE), 1)
                seen = keys <= rows
                for p in range(3):
                    start = ids[3 + p]
                    inside = (keys >= start) & (keys < start + PIECE)
                    inside &= (rows >= start) & (rows < start + PIECE)
                    seen |= inside
                bias_ref[i] = jnp.where(seen, 0.0, masked_score)

        k = k_ref[0]
        vt = v_ref[0].T
        for i in range(tiles):
            used = min(i + 2, tiles)
            q_rows = q_ref[0, i * TILE : (i + 1) * TILE]
            parts = []
            for head in range(2):
                slot = (2 * i + head) % 2
                q_head = lane_mask(q_rows, head)
                top = None
                for j in range(used):
                    s = dot_f32(k[j * TILE : (j + 1) * TILE], q_head, 1, 1)
                    if j >= i:
                        s = s + bias_ref[i, (j - i) * TILE : (j - i + 1) * TILE]
                    s_ref[slot, j] = s
                    now = jnp.max(s.reshape(TILE // 8, 8, TILE), axis=0)
                    top = now if top is None else jnp.maximum(top, now)
                top = jnp.max(top, axis=0, keepdims=True)
                total = None
                out = None
                for j in range(used):
                    e = jnp.exp(s_ref[slot, j] - top)
                    now = jnp.sum(e.reshape(TILE // 8, 8, TILE), axis=0)
                    total = now if total is None else total + now
                    low = e.astype(BF)
                    e_ref[head, j * TILE : (j + 1) * TILE, i * TILE : (i + 1) * TILE] = low
                    now = dot_f32(
                        vt[head * HEAD_DIM : (head + 1) * HEAD_DIM, j * TILE : (j + 1) * TILE],
                        low,
                        1,
                        0,
                    )
                    out = now if out is None else out + now
                inv = 1.0 / jnp.sum(total, axis=0, keepdims=True)
                inv_ref[0, head : head + 1, i * TILE : (i + 1) * TILE] = inv
                parts.append(out * inv)
            both = jnp.concatenate(parts, axis=0)
            ot_ref[:, i * TILE : (i + 1) * TILE] = both.astype(BF)
            o_ref[i * TILE : (i + 1) * TILE] = both.T.astype(BF)

    spec = [
        pl.BlockSpec((1, length, pair), lambda p, ids, c=c: (c, 0, p)) for c in range(3)
    ]
    heads = width // HEAD_DIM
    return call(
        body,
        "attend",
        ids,
        (qkv, qkv, qkv),
        spec,
        (
            shape((length, width), BF),
            shape((width, length), BF),
            shape((heads, length, length), BF),
            shape((heads // 2, 2, length), F32),
        ),
        [
            pl.BlockSpec((length, pair), lambda p, ids: (0, p)),
            pl.BlockSpec((pair, length), lambda p, ids: (p, 0)),
            pl.BlockSpec((2, length, length), lambda p, ids: (p, 0, 0)),
            pl.BlockSpec((1, 2, length), lambda p, ids: (p, 0, 0)),
        ],
        (heads // 2,),
        (
            pltpu.VMEM((tiles, 2 * TILE, TILE), F32),
            pltpu.VMEM((2, tiles, TILE, TILE), F32),
        ),
        flops=4 * length * length * width,
    )


def attend_back(ids, qkv, d_heads, ot, e, inv):
    length, width = qkv.shape[1:]
    tiles = length // TILE
    pair = 2 * HEAD_DIM

    def body(ids, q_ref, k_ref, v_ref, d_ref, ot_ref, e_ref, inv_ref, out_ref, ds_ref, dq_ref):
        k = k_ref[0]
        v = v_ref[0]
        kt = k.T
        dt = d_ref[...].astype(F32).T
        q_heads = []
        d_scaled = []
        deltas = []
        for head in range(2):
            span = slice(head * HEAD_DIM, (head + 1) * HEAD_DIM)
            inv_row = inv_ref[0, head : head + 1]
            mine = dt[span] * inv_row
            deltas.append(jnp.sum(mine * ot_ref[span].astype(F32), axis=0, keepdims=True))
            blank = jnp.zeros((HEAD_DIM, length), BF)
            mine = mine.astype(BF)
            d_scaled.append(
                jnp.concatenate([mine, blank] if head == 0 else [blank, mine], axis=0)
            )
            q_heads.append(lane_mask(q_ref[0], head))
        dq_ref[...] = jnp.zeros_like(dq_ref)
        for j in range(tiles):
            keys = slice(j * TILE, (j + 1) * TILE)
            first = max(j - 1, 0) * TILE
            d_key = None
            d_value = None
            for head in range(2):
                for r in range(first, length, TILE):
                    cols = slice(r, r + TILE)
                    dp = dot_f32(v[keys], d_scaled[head][:, cols], 1, 0)
                    weights = e_ref[head, keys, cols].astype(F32)
                    ds_ref[j % 2, head, :, cols] = (
                        weights * (dp - deltas[head][:, cols])
                    ).astype(BF)
                ds = ds_ref[j % 2, head, :, first:length]
                now = dot_f32(ds, q_heads[head][first:length], 1, 0)
                d_key = now if d_key is None else d_key + now
                now = dot_f32(e_ref[head, keys, first:length], d_scaled[head][:, first:length], 1, 1)
                d_value = now if d_value is None else d_value + now
                rows = slice(head * HEAD_DIM, (head + 1) * HEAD_DIM)
                dq_ref[rows, first:length] += dot_f32(kt[rows, keys], ds, 1, 0)
            out_ref[1, keys] = d_key.astype(BF)
            out_ref[2, keys] = d_value.astype(BF)
        out_ref[0] = (dq_ref[...] * HEAD_DIM ** (-0.5)).T.astype(BF)

    spec = [
        pl.BlockSpec((1, length, pair), lambda p, ids, c=c: (c, 0, p)) for c in range(3)
    ]
    heads = width // HEAD_DIM
    return call(
        body,
        "attend_back",
        ids,
        (qkv, qkv, qkv, d_heads, ot, e, inv),
        spec
        + [
            pl.BlockSpec((length, pair), lambda p, ids: (0, p)),
            pl.BlockSpec((pair, length), lambda p, ids: (p, 0)),
            pl.BlockSpec((2, length, length), lambda p, ids: (p, 0, 0)),
            pl.BlockSpec((1, 2, length), lambda p, ids: (p, 0, 0)),
        ],
        (shape((3, length, width), BF),),
        [pl.BlockSpec((3, length, pair), lambda p, ids: (0, 0, p))],
        (heads // 2,),
        (pltpu.VMEM((2, 2, TILE, length), BF), pltpu.VMEM((pair, length), F32)),
        flops=8 * length * length * width,
    )[0]


def out_project(ids, attended, packed, x, gain, fsdp, half):
    length, width = x.shape
    height = width // fsdp
    parts = width // half

    def body(ids, a_ref, w_ref, x_ref, gain_ref, hidden_ref, hn_ref, ht_ref, blocks_ref):
        for r in range(0, length, TILE):
            total = x_ref[r : r + TILE].astype(F32)
            for t in range(parts):
                w = w_ref[:, t].reshape(width, half)
                total += dot_f32(a_ref[r : r + TILE, t * half : (t + 1) * half], w, 1, 1)
            hidden_ref[r : r + TILE] = total
            hn_ref[r : r + TILE] = (total * rms_scale(total) * gain_ref[...]).astype(BF)
        store_transposed(ids, hn_ref[...], blocks_ref, ht_ref)

    return call(
        body,
        "out_project",
        ids,
        (attended, packed, x, gain),
        [
            whole((length, width)),
            pl.BlockSpec((fsdp, parts, height, half), lambda g, ids: (0, 0, 3, 0)),
            whole((length, width)),
            whole((1, width)),
        ],
        (
            shape((length, width), F32),
            shape((length, width), BF),
            shape((fsdp, height, length), BF),
        ),
        [whole((length, width)), whole((length, width)), whole((fsdp, height, length))],
        (1,),
        (pltpu.VMEM((fsdp, height, length), BF),),
        flops=2 * length * width * width,
    )


def feed_forward(ids, hn, grad, packed, fsdp):
    length, width = hn.shape
    height = width // fsdp
    half = packed.shape[3]
    parts = packed.shape[1]
    tile = 256
    per = half // tile

    def body(ids, hn_ref, g_ref, w_ref, mixed_ref, d_ref, gt_ref, blocks_ref):
        @pl.when((pl.program_id(0) == 0) & (pl.program_id(1) == 0))
        def _():
            store_transposed(ids, g_ref[...], blocks_ref, gt_ref)

        w = w_ref[:, 0]
        w_gate, w_up, w_down = [
            w[:, c * height : (c + 1) * height].reshape(width, tile) for c in range(3)
        ]
        for r in range(0, length, TILE):
            rows = hn_ref[r : r + TILE]
            gate = dot_f32(rows, w_gate, 1, 0)
            up = dot_f32(rows, w_up, 1, 0)
            d_mixed = dot_f32(g_ref[r : r + TILE], w_down, 1, 0)
            sig = jax.nn.sigmoid(gate)
            act = gate * sig
            mixed_ref[r : r + TILE] = (act * up).astype(BF)
            d_ref[0, r : r + TILE] = (d_mixed * up * sig * (1.0 + gate * (1.0 - sig))).astype(BF)
            d_ref[1, r : r + TILE] = (d_mixed * act).astype(BF)

    return call(
        body,
        "feed_forward",
        ids,
        (hn, grad, packed),
        [
            whole((length, width)),
            whole((length, width)),
            pl.BlockSpec((fsdp, 1, 3 * height, tile), lambda t, n, ids: (0, t, 0, n)),
        ],
        (
            shape((length, parts * half), BF),
            shape((2, length, parts * half), BF),
            shape((fsdp, height, length), BF),
        ),
        [
            pl.BlockSpec((length, tile), lambda t, n, ids: (0, t * per + n)),
            pl.BlockSpec((2, length, tile), lambda t, n, ids: (0, 0, t * per + n)),
            whole((fsdp, height, length)),
        ],
        (parts, per),
        (pltpu.VMEM((fsdp, height, length), BF),),
        flops=6 * length * width * parts * half,
    )


def feed_forward_out(ids, mixed, packed, hidden, fsdp):
    length, width = hidden.shape
    height = width // fsdp
    half = packed.shape[3]
    parts = packed.shape[1]
    tile = 512
    per = half // tile
    kept = length // parts

    def body(ids, m_ref, w_ref, hidden_ref, keep_ref, send_ref, acc_ref):
        first = (pl.program_id(0) == 0) & (pl.program_id(1) == 0)
        last = (pl.program_id(0) == parts - 1) & (pl.program_id(1) == per - 1)

        @pl.when(first)
        def _():
            acc_ref[...] = hidden_ref[...]

        w = rows_of(w_ref)
        for r in range(0, length, TILE):
            acc_ref[r : r + TILE] += dot_f32(m_ref[r : r + TILE], w, 1, 1)

        @pl.when(last)
        def _():
            keep_ref[...] = acc_ref[pl.ds(pl.multiple_of(ids[0] * kept, kept), kept)].astype(BF)
            send_ref[...] = acc_ref[
                pl.ds(pl.multiple_of((1 - ids[0]) * kept, kept), kept)
            ].astype(BF)

    return call(
        body,
        "feed_forward_out",
        ids,
        (mixed, packed, hidden),
        [
            pl.BlockSpec((length, tile), lambda t, n, ids: (0, t * per + n)),
            pl.BlockSpec((fsdp, 1, height, tile), lambda t, n, ids: (0, t, 2, n)),
            whole((length, width)),
        ],
        (shape((kept, width), BF), shape((kept, width), BF)),
        [whole((kept, width)), whole((kept, width))],
        (parts, per),
        (pltpu.VMEM((length, width), F32),),
        flops=2 * length * width * parts * half,
    )


def weight_grad(ids, name, left, right, index, parts, tile, extra=None):
    fsdp, height, length = left.shape
    half = right.shape[2] // parts
    tile = min(tile, half)
    per = half // tile
    rows = height if extra is None else height + 8
    hop = fsdp // 2

    def body(ids, l_ref, r_ref, *refs):
        right_tile = r_ref[0]
        outs = refs[-2:]
        for b in range(0, fsdp, 4):
            block = l_ref[b : b + 4].reshape(4 * height, length)
            made = dot_f32(block, right_tile, 1, 0).astype(BF).reshape(4, height, tile)
            out = outs[b // hop]
            out[0, b % hop : b % hop + 4, :height] = made
        if extra is not None:
            for core in range(2):
                for pair in range(hop):
                    source = 2 * (pair ^ ids[1]) + (core ^ ids[2])
                    outs[core][0, pair, height:] = refs[0][source, 0]

    ins = [left, right]
    specs = [
        whole((fsdp, height, length)),
        pl.BlockSpec((1, length, tile), lambda t, n, ids: (index, 0, t * per + n)),
    ]
    if extra is not None:
        ins.append(extra)
        specs.append(pl.BlockSpec((fsdp, 1, 8, tile), lambda t, n, ids: (0, t, 0, n)))
    out_spec = pl.BlockSpec((1, hop, rows, tile), lambda t, n, ids: (t ^ ids[0], 0, 0, n))
    return call(
        body,
        name,
        ids,
        tuple(ins),
        specs,
        (shape((parts, hop, rows, half), BF),) * 2,
        [out_spec, out_spec],
        (parts, per),
        flops=2 * length * fsdp * height * parts * half,
    )


def feed_forward_back(ids, d_gate_up, packed, hidden, grad, gain, fsdp):
    length, width = hidden.shape
    height = width // fsdp
    half = packed.shape[3]
    parts = packed.shape[1]
    tile = 512
    per = half // tile

    def body(
        ids, d_ref, w_ref, hidden_ref, g_ref, gain_ref, dh_ref, low_ref, lt_ref, gg_ref, acc_ref, blocks_ref
    ):
        first = (pl.program_id(0) == 0) & (pl.program_id(1) == 0)
        last = (pl.program_id(0) == parts - 1) & (pl.program_id(1) == per - 1)

        @pl.when(first)
        def _():
            acc_ref[...] = jnp.zeros_like(acc_ref)

        w = w_ref[:, 0]
        w_gate, w_up = [w[:, c * height : (c + 1) * height].reshape(width, tile) for c in range(2)]
        for r in range(0, length, TILE):
            acc_ref[r : r + TILE] += dot_f32(d_ref[0, r : r + TILE], w_gate, 1, 1) + dot_f32(
                d_ref[1, r : r + TILE], w_up, 1, 1
            )

        @pl.when(last)
        def _():
            total = jnp.zeros((1, width), F32)
            for r in range(0, length, TILE):
                rows = hidden_ref[r : r + TILE]
                scale = rms_scale(rows)
                normed = rows * scale
                d_normed = acc_ref[r : r + TILE]
                total += jnp.sum(d_normed * normed, axis=0, keepdims=True)
                dh = g_ref[r : r + TILE].astype(F32) + norm_backward_pass(
                    d_normed, normed, scale, gain_ref[...]
                )
                dh_ref[r : r + TILE] = dh
                low_ref[r : r + TILE] = dh.astype(BF)
            gg_ref[...] = total
            store_transposed(ids, low_ref[...], blocks_ref, lt_ref)

    return call(
        body,
        "feed_forward_back",
        ids,
        (d_gate_up, packed, hidden, grad, gain),
        [
            pl.BlockSpec((2, length, tile), lambda t, n, ids: (0, 0, t * per + n)),
            pl.BlockSpec((fsdp, 1, 2 * height, tile), lambda t, n, ids: (0, t, 0, n)),
            whole((length, width)),
            whole((length, width)),
            whole((1, width)),
        ],
        (
            shape((length, width), F32),
            shape((length, width), BF),
            shape((fsdp, height, length), BF),
            shape((1, width), F32),
        ),
        [
            whole((length, width)),
            whole((length, width)),
            whole((fsdp, height, length)),
            whole((1, width)),
        ],
        (parts, per),
        (pltpu.VMEM((length, width), F32), pltpu.VMEM((fsdp, height, length), BF)),
        flops=4 * length * width * parts * half,
    )


def out_project_back(ids, d_attn, packed, fsdp):
    length, width = d_attn.shape
    height = width // fsdp
    half = packed.shape[3]
    parts = packed.shape[1]

    def body(ids, d_ref, w_ref, out_ref):
        w = rows_of(w_ref)
        for r in range(0, length, TILE):
            out_ref[r : r + TILE] = dot_f32(d_ref[r : r + TILE], w, 1, 0).astype(BF)

    return call(
        body,
        "out_project_back",
        ids,
        (d_attn, packed),
        [
            whole((length, width)),
            pl.BlockSpec((fsdp, 1, height, half), lambda t, ids: (0, t, 3, 0)),
        ],
        (shape((length, width), BF),),
        [pl.BlockSpec((length, half), lambda t, ids: (0, t))],
        (parts,),
        flops=2 * length * width * width,
    )[0]


def qkv_back(ids, d_qkv, packed, x, dh, gain, fsdp):
    length, width = x.shape
    height = width // fsdp
    half = packed.shape[3]
    parts = packed.shape[1]
    kept = length // parts

    def body(ids, d_ref, w_ref, x_ref, dh_ref, gain_ref, keep_ref, send_ref, gg_ref, acc_ref):
        first = (pl.program_id(0) == 0) & (pl.program_id(1) == 0)
        last = (pl.program_id(0) == 2) & (pl.program_id(1) == parts - 1)

        @pl.when(first)
        def _():
            acc_ref[...] = jnp.zeros_like(acc_ref)

        w = rows_of(w_ref)
        for r in range(0, length, TILE):
            acc_ref[r : r + TILE] += dot_f32(d_ref[0, r : r + TILE], w, 1, 1)

        @pl.when(last)
        def _():
            total = jnp.zeros((1, width), F32)
            for r in range(0, length, TILE):
                rows = x_ref[r : r + TILE].astype(F32)
                scale = rms_scale(rows)
                normed = rows * scale
                d_normed = acc_ref[r : r + TILE]
                total += jnp.sum(d_normed * normed, axis=0, keepdims=True)
                acc_ref[r : r + TILE] = dh_ref[r : r + TILE] + norm_backward_pass(
                    d_normed, normed, scale, gain_ref[...]
                )
            gg_ref[...] = total
            keep_ref[...] = acc_ref[pl.ds(pl.multiple_of(ids[0] * kept, kept), kept)]
            send_ref[...] = acc_ref[
                pl.ds(pl.multiple_of((1 - ids[0]) * kept, kept), kept)
            ].astype(BF)

    return call(
        body,
        "qkv_back",
        ids,
        (d_qkv, packed, x, dh, gain),
        [
            pl.BlockSpec((1, length, half), lambda c, t, ids: (c, 0, t)),
            pl.BlockSpec((fsdp, 1, height, half), lambda c, t, ids: (0, t, c, 0)),
            whole((length, width)),
            whole((length, width)),
            whole((1, width)),
        ],
        (shape((kept, width), F32), shape((kept, width), BF), shape((1, width), F32)),
        [whole((kept, width)), whole((kept, width)), whole((1, width))],
        (3, parts),
        (pltpu.VMEM((length, width), F32),),
        flops=6 * length * width * width,
    )


def swap(value, bit):
    if bit == 0:
        return lax.ppermute(value, "tensor", [(0, 1), (1, 0)])
    return lax.ppermute(
        value, "fsdp", [(i, i ^ bit) for i in range(lax.axis_size("fsdp"))]
    )


def scatter_sum(keep, send, order):
    bits = keep.shape[1].bit_length() - 1
    dims = (2,) * (bits + 1)
    got = swap(send, 1)
    total = keep.reshape(dims + keep.shape[2:]).astype(F32) + got.reshape(
        dims + keep.shape[2:]
    ).astype(F32)
    axes = [0] + [2 << b for b in reversed(range(bits))]
    for bit in order:
        at = axes.index(bit)
        low = total.astype(BF)
        mine = lax.index_in_dim(low, 0, at, keepdims=False)
        other = lax.index_in_dim(low, 1, at, keepdims=False)
        axes.remove(bit)
        total = mine.astype(F32) + swap(other, bit).astype(F32)
    return total


def three_parts(values):
    high = values.astype(BF)
    rest = values - high.astype(F32)
    middle = rest.astype(BF)
    return jnp.stack([high, middle, (rest - middle.astype(F32)).astype(BF)], -1)


def local_sequence(
    tokens, piece_starts, gain_attn, w_qkv, w_out, gain_mlp, w_gate_up, w_down, out_grad
):
    fsdp = lax.axis_size("fsdp")
    parts = lax.axis_size("tensor")
    me_f = lax.axis_index("fsdp")
    me_t = lax.axis_index("tensor")
    local_rows = tokens.shape[1]
    height = w_qkv.shape[1]
    half = w_qkv.shape[2]
    share = gain_attn.shape[0]
    order_down, order_gate, order_up = (2, 0, 4, 8), (0, 4, 8, 2), (4, 8, 2, 0)

    starts = lax.dynamic_index_in_dim(piece_starts, me_t, 0, keepdims=False)[0]
    ids = jnp.concatenate([jnp.stack([me_t, me_f // 2, me_f % 2]).astype(jnp.int32), starts])

    def sequence_of(rows):
        rows = rows.reshape(parts, local_rows, D)
        mine = lax.dynamic_index_in_dim(rows, me_t, 0, keepdims=False)
        got = swap(lax.dynamic_index_in_dim(rows, 1 - me_t, 0, keepdims=False), 0)
        return jnp.where(
            me_t == 0, jnp.concatenate([mine, got]), jnp.concatenate([got, mine])
        )

    def micro_rows(keep, got):
        both = jnp.where(me_t == 0, jnp.stack([keep, got]), jnp.stack([got, keep]))
        return both.reshape(tokens.shape)

    gains = three_parts(jnp.stack([gain_attn, gain_mlp])).reshape(1, -1)
    gains = jnp.pad(gains, ((0, 7), (0, half - gains.shape[1])))
    mine = jnp.concatenate([w_qkv.reshape(3 * height, half), w_out.T, gains])
    attn_w = lax.all_gather(mine, ("fsdp", "tensor"), axis=0, tiled=False)
    attn_w = attn_w.reshape(fsdp, parts, 4 * height + 8, half)
    gains = attn_w[:, :, 4 * height, : 6 * share].reshape(fsdp * parts, 2, share, 3)
    gains = jnp.sum(gains.astype(F32), axis=3)
    gain_one, gain_two = [gains[:, i].reshape(1, D) for i in range(2)]

    mine = jnp.concatenate([w_gate_up.reshape(2 * height, -1), w_down.T])
    ff_w = lax.all_gather(mine, ("fsdp", "tensor"), axis=0, tiled=False)
    ff_w = ff_w.reshape(fsdp, parts, 3 * height, -1)

    x = sequence_of(tokens)
    grad = sequence_of(out_grad)

    qkv, xt = make_qkv(ids, x, gain_one, attn_w, fsdp, half)
    attended, ot, e, inv = attend(ids, qkv)
    hidden, hn, ht = out_project(ids, attended, attn_w, x, gain_two, fsdp, half)
    mixed, d_gate_up, gt = feed_forward(ids, hn, grad, ff_w, fsdp)

    down = weight_grad(ids, "grad_down", gt, mixed[None], 0, parts, 512)
    down = scatter_sum(*down, order_down)
    gate = weight_grad(ids, "grad_gate", ht, d_gate_up, 0, parts, 512)
    gate = scatter_sum(*gate, order_gate)
    up = weight_grad(ids, "grad_up", ht, d_gate_up, 1, parts, 512)
    up = scatter_sum(*up, order_up)

    dh, d_attn, dt, gain_two_grad = feed_forward_back(
        ids, d_gate_up, ff_w, hidden, grad, gain_two, fsdp
    )
    d_attended = out_project_back(ids, d_attn, attn_w, fsdp)
    out = weight_grad(ids, "grad_out", dt, attended[None], 0, parts, 512)
    out = scatter_sum(*out, order_down)
    keep, send = feed_forward_out(ids, mixed, ff_w, hidden, fsdp)
    layer_out = micro_rows(keep, swap(send, 0))

    d_qkv = attend_back(ids, qkv, d_attended, ot, e, inv)
    keep, send, gain_one_grad = qkv_back(ids, d_qkv, attn_w, x, dh, gain_one, fsdp)
    input_grad = micro_rows(keep, swap(send, 0).astype(F32))

    gain_grads = jnp.stack([gain_one_grad[0], gain_two_grad[0]]).reshape(2, fsdp, parts, share)
    gain_grads = gain_grads.transpose(1, 2, 0, 3).reshape(fsdp, parts, 1, 2 * share)
    gain_grads = jnp.pad(gain_grads, ((0, 0), (0, 0), (0, 7), (0, half - 2 * share))).astype(BF)
    three = []
    for c, order in enumerate((order_down, order_gate, order_up)):
        pieces = weight_grad(
            ids, "grad_qkv", xt, d_qkv, c, parts, 512, gain_grads if c == 2 else None
        )
        three.append(scatter_sum(*pieces, order))
    gain_shares = three[2][height, : 2 * share].reshape(2, share)
    three[2] = three[2][:height]
    return (
        layer_out,
        input_grad,
        gain_shares[0],
        jnp.stack(three),
        out.T,
        gain_shares[1],
        jnp.stack([gate, up]),
        down.T,
    )


def local_any(tokens, *rest):
    if lax.axis_size("tensor") == tokens.shape[0] == 2 and tokens.shape[2] == 1:
        return local_sequence(tokens, *rest)
    return local(tokens, *rest)


def solution(mesh):
    return jax.shard_map(
        local_any,
        mesh=mesh,
        in_specs=(
            P(None, "tensor", "fsdp", None),
            P(None, "fsdp", None),
            P(("fsdp", "tensor")),
            P(None, "fsdp", "tensor"),
            P("tensor", "fsdp"),
            P(("fsdp", "tensor")),
            P(None, "fsdp", "tensor"),
            P("tensor", "fsdp"),
            P(None, "tensor", "fsdp", None),
        ),
        out_specs=(
            P(None, "tensor", "fsdp", None),
            P(None, "tensor", "fsdp", None),
            P(("fsdp", "tensor")),
            P(None, "fsdp", "tensor"),
            P("tensor", "fsdp"),
            P(("fsdp", "tensor")),
            P(None, "fsdp", "tensor"),
            P("tensor", "fsdp"),
        ),
        check_vma=False,
    )
```

```python
import jax
import jax.numpy as jnp
from jax import lax
from jax.experimental import pallas as pl
from jax.experimental.pallas import tpu as pltpu
from jax.sharding import PartitionSpec as P

D = 1024
HEAD_DIM = 64
QBLOCK = 512
PIECE = 256


norm_eps = 1e-05
masked_score = -1e30


def rms_scale(values_float_rows):
    return lax.rsqrt(
        jnp.mean(values_float_rows * values_float_rows, axis=-1, keepdims=True) + norm_eps
    )


def norm_backward_pass(d_normed, normed_pre, scale_rows, gain_vector_row):
    d_scaled = d_normed * gain_vector_row
    return scale_rows * (
        d_scaled - normed_pre * jnp.mean(d_scaled * normed_pre, axis=-1, keepdims=True)
    )


def piece_index_labels(starts_row, length):
    positions = jnp.arange(length, dtype=jnp.int32)[:, None]
    inside = (positions >= starts_row[None, :]) & (positions < starts_row[None, :] + PIECE)
    numbers = jnp.arange(1, starts_row.shape[0] + 1, dtype=jnp.int32)
    return jnp.sum(jnp.where(inside, numbers[None, :], 0), axis=1)


def allowed_block(labels, first_row, key_count):
    row_ids = first_row + jnp.arange(QBLOCK, dtype=jnp.int32)
    col_ids = jnp.arange(key_count, dtype=jnp.int32)
    row_labels = labels[first_row : first_row + QBLOCK]
    causal = col_ids[None, :] <= row_ids[:, None]
    same_piece = (row_labels[:, None] == labels[None, :]) & (row_labels[:, None] > 0)
    return causal | same_piece


def attend_forward(queries, keys_all, values_all, labels, key_spans):
    score_scale = HEAD_DIM ** (-0.5)
    outputs = []
    totals = []
    for first_row, key_count in key_spans:
        block_q = queries[first_row : first_row + QBLOCK]
        scores = (
            jnp.einsum("qhd,khd->hqk", block_q, keys_all, preferred_element_type=jnp.float32)
            * score_scale
        )
        scores = jnp.where(allowed_block(labels, first_row, key_count)[None], scores, masked_score)
        row_max = jnp.max(scores, axis=-1, keepdims=True)
        exp_scores = jnp.exp(scores - row_max)
        row_total = jnp.sum(exp_scores, axis=-1, keepdims=True)
        attn_probs = (exp_scores / row_total).astype(jnp.bfloat16)
        block_out = jnp.einsum(
            "hqk,khd->qhd", attn_probs, values_all, preferred_element_type=jnp.float32
        )
        outputs.append(block_out.astype(jnp.bfloat16))
        totals.append((row_max + jnp.log(row_total))[..., 0])
    return (jnp.concatenate(outputs, 0), jnp.concatenate(totals, 1))


def attend_backward(queries, keys_all, values_all, labels, log_total, d_heads, key_spans):
    score_scale = HEAD_DIM ** (-0.5)
    query_parts = []
    d_keys = jnp.zeros(keys_all.shape, jnp.float32)
    d_values = jnp.zeros(values_all.shape, jnp.float32)
    for first_row, key_count in key_spans:
        block_q = queries[first_row : first_row + QBLOCK]
        block_d = d_heads[first_row : first_row + QBLOCK]
        scores = (
            jnp.einsum("qhd,khd->hqk", block_q, keys_all, preferred_element_type=jnp.float32)
            * score_scale
        )
        mask_now = allowed_block(labels, first_row, key_count)[None]
        attn_probs = jnp.where(
            mask_now, jnp.exp(scores - log_total[:, first_row : first_row + QBLOCK, None]), 0.0
        )
        probs_low = attn_probs.astype(jnp.bfloat16)
        d_probs = jnp.einsum(
            "qhd,khd->hqk", block_d, values_all, preferred_element_type=jnp.float32
        )
        row_dot = jnp.sum(attn_probs * d_probs, axis=-1, keepdims=True)
        d_scores = (attn_probs * (d_probs - row_dot)).astype(jnp.bfloat16)
        query_parts.append(
            jnp.einsum("hqk,khd->qhd", d_scores, keys_all, preferred_element_type=jnp.float32)
            * score_scale
        )
        d_keys = d_keys.at[:key_count].add(
            jnp.einsum("hqk,qhd->khd", d_scores, block_q, preferred_element_type=jnp.float32)
            * score_scale
        )
        d_values = d_values.at[:key_count].add(
            jnp.einsum("hqk,qhd->khd", probs_low, block_d, preferred_element_type=jnp.float32)
        )
    return (jnp.concatenate(query_parts, 0), d_keys, d_values)


def attention_forward(qkv_low, labels_all, key_spans):
    length, seq_count, width = (qkv_low.shape[0], qkv_low.shape[1], qkv_low.shape[3])
    per_seq = jnp.moveaxis(qkv_low, 1, 0).reshape(seq_count, length, 3, width // HEAD_DIM, HEAD_DIM)

    def one_seq(seq_items):
        seq_qkv, labels = seq_items
        return attend_forward(seq_qkv[:, 0], seq_qkv[:, 1], seq_qkv[:, 2], labels, key_spans)

    seq_outs, totals = lax.map(one_seq, (per_seq, labels_all))
    return (jnp.moveaxis(seq_outs.reshape(seq_count, length, width), 0, 1), totals)


def attention_backward(qkv_low, labels_all, totals, d_attended, key_spans):
    length, seq_count, width = (qkv_low.shape[0], qkv_low.shape[1], qkv_low.shape[3])
    per_seq = jnp.moveaxis(qkv_low, 1, 0).reshape(seq_count, length, 3, width // HEAD_DIM, HEAD_DIM)
    d_seq = jnp.moveaxis(d_attended, 1, 0).reshape(seq_count, length, width // HEAD_DIM, HEAD_DIM)

    def one_seq(seq_items):
        seq_qkv, labels, log_total, seq_d = seq_items
        d_query, d_keys, d_values = attend_backward(
            seq_qkv[:, 0], seq_qkv[:, 1], seq_qkv[:, 2], labels, log_total, seq_d, key_spans
        )
        return jnp.stack([d_query, d_keys, d_values], 1).astype(jnp.bfloat16)

    seq_grads = lax.map(one_seq, (per_seq, labels_all, totals, d_seq))
    return jnp.moveaxis(seq_grads, 0, 1).reshape(length, seq_count, 3, width)


def fetch_weights(w_qkv, w_out, w_gate_up, w_down):
    qkv_all, out_all, gate_up_all, down_weight_full = (
        lax.all_gather(w_qkv, "fsdp", axis=1, tiled=True),
        lax.all_gather(w_out, "fsdp", axis=1, tiled=True),
        lax.all_gather(w_gate_up, "fsdp", axis=1, tiled=True),
        lax.all_gather(w_down, "fsdp", axis=1, tiled=True),
    )
    return (qkv_all, out_all, gate_up_all, down_weight_full)


def local(tokens, piece_starts, gain_attn, w_qkv, w_out, gain_mlp, w_gate_up, w_down, out_grad):
    both_gains = lax.all_gather(
        jnp.stack([gain_attn, gain_mlp]), ("fsdp", "tensor"), axis=1, tiled=True
    )
    local_rows = tokens.shape[1]
    length = local_rows * lax.axis_size("tensor")
    key_spans = [(first_row, length) for first_row in range(0, length, QBLOCK)]

    def label_row(starts_row):
        return piece_index_labels(starts_row, length)

    labels_every = jax.vmap(jax.vmap(label_row))(piece_starts)
    ff_cols = w_gate_up.shape[2]
    acc_gain = jnp.zeros((2, D), jnp.float32)
    acc_qkv = jnp.zeros((3, D, w_qkv.shape[2]), jnp.float32)
    acc_out = jnp.zeros((w_out.shape[0], D), jnp.float32)
    acc_gate_up = jnp.zeros((2, D, ff_cols), jnp.float32)
    acc_down = jnp.zeros((ff_cols, D), jnp.float32)
    layer_outs = []
    input_grads = []
    for micro_idx in range(tokens.shape[0]):
        weights = fetch_weights(w_qkv, w_out, w_gate_up, w_down)
        qkv_all, out_all, gate_up_all, down_weight_full = weights
        rows_f32 = tokens[micro_idx].astype(jnp.float32)
        scale_attn = rms_scale(rows_f32)
        pre_attn = rows_f32 * scale_attn
        normed = (pre_attn * both_gains[0]).astype(jnp.bfloat16)
        piece_rows = lax.all_gather(normed, "tensor", axis=0, tiled=True)
        made = jnp.einsum("lsd,cde->lsce", piece_rows, qkv_all, preferred_element_type=jnp.float32)
        qkv_low = made.astype(jnp.bfloat16)
        attended, log_total = attention_forward(qkv_low, labels_every[micro_idx], key_spans)
        rows_now = lax.slice_in_dim(attended, 0, local_rows * lax.axis_size("tensor"), axis=0)
        attn_part = lax.psum_scatter(
            jnp.einsum("lsc,cd->lsd", rows_now, out_all, preferred_element_type=jnp.float32).astype(
                jnp.bfloat16
            ),
            "tensor",
            scatter_dimension=0,
            tiled=True,
        ).astype(jnp.float32)
        hidden = rows_f32 + attn_part
        scale_mlp = rms_scale(hidden)
        pre_mlp = hidden * scale_mlp
        normed_mlp = (pre_mlp * both_gains[1]).astype(jnp.bfloat16)
        expand_piece_rows = lax.all_gather(normed_mlp, "tensor", axis=0, tiled=True)
        gate_up = jnp.einsum(
            "lsd,cdf->lscf", expand_piece_rows, gate_up_all, preferred_element_type=jnp.float32
        )
        gate_part = gate_up[:, :, 0]
        up_part = gate_up[:, :, 1]
        sigmoid_gate = jax.nn.sigmoid(gate_part)
        activated = gate_part * sigmoid_gate
        mixed_lowp_rows = (activated * up_part).astype(jnp.bfloat16)
        down_rows_now = lax.slice_in_dim(
            mixed_lowp_rows, 0, local_rows * lax.axis_size("tensor"), axis=0
        )
        mlp_part = lax.psum_scatter(
            jnp.einsum(
                "meg,gp->mep", down_rows_now, down_weight_full, preferred_element_type=jnp.float32
            ).astype(jnp.bfloat16),
            "tensor",
            scatter_dimension=0,
            tiled=True,
        ).astype(jnp.float32)
        layer_outs.append((hidden + mlp_part).astype(jnp.bfloat16))
        qkv_all, out_all, gate_up_all, down_weight_full = fetch_weights(
            w_qkv, w_out, w_gate_up, w_down
        )
        grad_rows = out_grad[micro_idx]
        down_piece_rows = lax.all_gather(grad_rows, "tensor", axis=0, tiled=True)
        d_mixed = jnp.einsum(
            "xum,tm->xut", down_piece_rows, down_weight_full, preferred_element_type=jnp.float32
        )
        acc_down = acc_down + jnp.einsum(
            "zmp,zme->pe", mixed_lowp_rows, down_piece_rows, preferred_element_type=jnp.float32
        )
        d_gate = d_mixed * up_part * sigmoid_gate * (1.0 + gate_part * (1.0 - sigmoid_gate))
        d_up = d_mixed * activated
        d_gate_up = jnp.stack([d_gate, d_up], 2).astype(jnp.bfloat16)
        acc_gate_up = acc_gate_up + jnp.einsum(
            "lsd,lscf->cdf", expand_piece_rows, d_gate_up, preferred_element_type=jnp.float32
        )
        mlp_rows_now = lax.slice_in_dim(d_gate_up, 0, local_rows * lax.axis_size("tensor"), axis=0)
        d_normed_mlp = lax.psum_scatter(
            jnp.einsum(
                "lscf,cdf->lsd", mlp_rows_now, gate_up_all, preferred_element_type=jnp.float32
            ).astype(jnp.bfloat16),
            "tensor",
            scatter_dimension=0,
            tiled=True,
        ).astype(jnp.float32)
        gain_mlp_part = jnp.sum(d_normed_mlp * pre_mlp, axis=(0, 1))
        d_hidden = grad_rows.astype(jnp.float32) + norm_backward_pass(
            d_normed_mlp, pre_mlp, scale_mlp, both_gains[1]
        )
        attention_gradient_lowp = d_hidden.astype(jnp.bfloat16)
        out_piece_rows = lax.all_gather(attention_gradient_lowp, "tensor", axis=0, tiled=True)
        out_made = jnp.einsum(
            "lsd,cd->lsc", out_piece_rows, out_all, preferred_element_type=jnp.float32
        )
        d_attended = out_made.astype(jnp.bfloat16)
        acc_out = acc_out + jnp.einsum(
            "lsc,lsd->cd", attended, out_piece_rows, preferred_element_type=jnp.float32
        )
        d_qkv = attention_backward(
            qkv_low, labels_every[micro_idx], log_total, d_attended, key_spans
        )
        acc_qkv = acc_qkv + jnp.einsum(
            "lsd,lsce->cde", piece_rows, d_qkv, preferred_element_type=jnp.float32
        )
        d_normed = lax.psum_scatter(
            jnp.einsum("lsce,cde->lsd", d_qkv, qkv_all, preferred_element_type=jnp.float32).astype(
                jnp.bfloat16
            ),
            "tensor",
            scatter_dimension=0,
            tiled=True,
        ).astype(jnp.float32)
        gain_attn_part = jnp.sum(d_normed * pre_attn, axis=(0, 1))
        input_grads.append(
            d_hidden + norm_backward_pass(d_normed, pre_attn, scale_attn, both_gains[0])
        )
        acc_gain = acc_gain + jnp.stack([gain_attn_part, gain_mlp_part])
    gain_rows, qkv_rows, out_rows_sum, gate_up_rows, down_rows_sum = (
        lax.psum_scatter(
            acc_gain.astype(jnp.bfloat16), "fsdp", scatter_dimension=1, tiled=True
        ).astype(jnp.float32),
        lax.psum_scatter(
            acc_qkv.astype(jnp.bfloat16), "fsdp", scatter_dimension=1, tiled=True
        ).astype(jnp.float32),
        lax.psum_scatter(
            acc_out.astype(jnp.bfloat16), "fsdp", scatter_dimension=1, tiled=True
        ).astype(jnp.float32),
        lax.psum_scatter(
            acc_gate_up.astype(jnp.bfloat16), "fsdp", scatter_dimension=1, tiled=True
        ).astype(jnp.float32),
        lax.psum_scatter(
            acc_down.astype(jnp.bfloat16), "fsdp", scatter_dimension=1, tiled=True
        ).astype(jnp.float32),
    )
    gain_shares = lax.psum_scatter(gain_rows, "tensor", scatter_dimension=1, tiled=True)
    return (
        jnp.stack(layer_outs, 0),
        jnp.stack(input_grads, 0),
        gain_shares[0],
        qkv_rows,
        out_rows_sum,
        gain_shares[1],
        gate_up_rows,
        down_rows_sum,
    )


BF = jnp.bfloat16
F32 = jnp.float32
TILE = 256
UNITS = 512
CORE, TENSOR, X, Z_NEAR, Z_FAR = 1, 0, 2, 4, 8


def dot_f32(a, b, ca, cb):
    return lax.dot_general(a, b, (((ca,), (cb,)), ((), ())), preferred_element_type=F32)


def call(body, name, ids, ins, in_specs, outs, out_specs, grid, scratch=(), aliases=None):
    return pl.pallas_call(
        body,
        name=name,
        out_shape=outs,
        grid_spec=pltpu.PrefetchScalarGridSpec(
            num_scalar_prefetch=1,
            grid=grid,
            in_specs=in_specs,
            out_specs=out_specs,
            scratch_shapes=list(scratch),
        ),
        input_output_aliases=aliases or {},
        compiler_params=pltpu.CompilerParams(
            dimension_semantics=("arbitrary",) * len(grid), vmem_limit_bytes=56 * 2**20
        ),
        cost_estimate=pl.CostEstimate(flops=1024, bytes_accessed=1024, transcendentals=0),
    )(ids, *ins)


def shape(dims, dtype):
    return jax.ShapeDtypeStruct(dims, dtype)


def whole(dims):
    zeros = (0,) * len(dims)
    return pl.BlockSpec(dims, lambda *_: zeros)


IN_PLACE = pl.BlockSpec(memory_space=pl.ANY)


def store_transposed(ids, value, blocks_ref, out_ref):
    count, height = blocks_ref.shape[0], blocks_ref.shape[1]
    step = 128 // height
    for c in range(value.shape[1] // 128):
        part = value[:, c * 128 : (c + 1) * 128]
        blocks_ref[c * step : (c + 1) * step] = part.T.reshape(step, height, part.shape[0])
    for core in range(2):
        for pair in range(count // 2):
            source = 2 * (pair ^ ids[1]) + (core ^ ids[2])
            out_ref[core * (count // 2) + pair] = blocks_ref[source]


def position(order, f, t):
    at = 0
    for k, bit in enumerate(order):
        value = t if bit == TENSOR else (f // bit) % 2
        at = at + value * 2**k
    return at


def swap(value, bit):
    if bit == TENSOR:
        return lax.ppermute(value, "tensor", [(0, 1), (1, 0)])
    return lax.ppermute(value, "fsdp", [(i, i ^ bit) for i in range(lax.axis_size("fsdp"))])


class Gathered:
    def __init__(self, mine, order):
        self.order = order
        self.left = [*order, CORE]
        self.held = mine
        self.rows = mine.shape
        self.ready = False
        self.begin()

    def begin(self):
        self.got = swap(self.held, self.left[0])

    def advance(self):
        if self.left.pop(0) == CORE:
            self.pair = [a.reshape((-1,) + self.rows) for a in (self.held, self.got)]
            self.ready = True
        else:
            self.held = jnp.stack([self.held, self.got])
            self.begin()


class Summed:
    def __init__(self, keep, send, order):
        dims = (2,) * 4 + keep.shape[2:]
        axes = (TENSOR, Z_FAR, Z_NEAR, X)
        self.arrays = [(keep.reshape(dims), axes)]
        self.axes = axes
        self.left = list(order)
        self.got = swap(send.reshape(dims), CORE)
        self.bit = None

    def received(self):
        self.arrays.append((self.got, self.axes))
        self.bit = self.left.pop(0) if self.left else None
        self.axes = tuple(a for a in self.axes if a != self.bit)


def halve(ids, sums):
    for s in sums:
        s.received()
    last = sums[0].bit is None
    depth = 0 if last else max(len(s.axes) for s in sums)
    blocks = 2**depth
    ins, in_specs, outs, out_specs, counts = [], [], [], [], []
    for s in sums:
        rows, columns = s.arrays[0][0].shape[-2:]

        def index(axes, g, now=s.axes, bit=s.bit):
            at = []
            for a in axes:
                if last or a not in now:
                    at.append(int(a == bit))
                else:
                    at.append(g // 2 ** (depth - 1 - now.index(a)) % 2)
            return (*at, 0, 0)

        for array, axes in s.arrays:
            ins.append(array)
            in_specs.append(
                pl.BlockSpec(
                    (None,) * len(axes) + (rows, columns),
                    lambda g, ids, axes=axes, index=index: index(axes, g),
                )
            )
        counts.append(len(s.arrays))
        lead = () if last else (2,) * len(s.axes)
        outs.append(shape(lead + (rows, columns), F32 if last else BF))
        out_specs.append(
            pl.BlockSpec(
                (None,) * len(lead) + (rows, columns),
                lambda g, ids, axes=() if last else s.axes, index=index: index(axes, g),
            )
        )

    def body(ids, *refs):
        out_refs = refs[len(ins) :]
        at = 0
        for out_ref, count in zip(out_refs, counts):
            rows = out_ref.shape[0]
            for r in range(0, rows, 64):
                total = refs[at][r : r + 64].astype(F32)
                for k in range(1, count):
                    total += refs[at + k][r : r + 64].astype(F32)
                out_ref[r : r + 64] = total.astype(out_ref.dtype)
            at += count

    made = call(body, "halve", ids, tuple(ins), in_specs, tuple(outs), out_specs, (blocks,))
    for s, value in zip(sums, made):
        if last:
            s.result = value
        else:
            s.got = swap(value, s.bit)
    return made


def after(values, running):
    running = [r for r in running if not r.ready]
    values, got = lax.optimization_barrier((values, [r.got for r in running]))
    for r, g in zip(running, got):
        r.got = g
        r.advance()
    return values


def gathered_rows(ids, refs, order, part, height):
    mine = position(order, ids[3], ids[0])
    flipped = ids[2] == 1
    blocks = []
    for pair in range(refs[0].shape[0] // 2):
        at = position(order, 2 * pair, part) ^ mine
        a, b = [ref[at, :height] for ref in refs]
        blocks += [jnp.where(flipped, b, a), jnp.where(flipped, a, b)]
    return jnp.concatenate(blocks, axis=0)


def make_qkv(ids, rows, gots, gain, gathered):
    parts, local_rows, width = rows.shape
    length = parts * local_rows
    fsdp = gathered[0].pair[0].shape[0]
    height = width // fsdp
    half = width // parts

    piece = local_rows // len(gots)

    def body(ids, rows_ref, gain_ref, *refs):
        qkv_ref, xt_ref, x_ref, xn_ref, blocks_ref = refs[-5:]
        x_ref[pl.ds(pl.multiple_of(ids[0] * local_rows, local_rows), local_rows)] = rows_ref[0]
        for k in range(len(gots)):
            first = pl.multiple_of((1 - ids[0]) * local_rows + k * piece, piece)
            x_ref[pl.ds(first, piece)] = refs[6 + k][...]
        for r in range(0, length, TILE):
            rows = x_ref[r : r + TILE].astype(F32)
            xn_ref[r : r + TILE] = (rows * rms_scale(rows) * gain_ref[...]).astype(BF)
        for c in range(3):
            for t in range(parts):
                w = gathered_rows(ids, refs[2 * c : 2 * c + 2], gathered[c].order, t, height)
                for r in range(0, length, TILE):
                    made = dot_f32(xn_ref[r : r + TILE], w, 1, 0)
                    if c == 0:
                        made = made * HEAD_DIM ** (-0.5)
                    qkv_ref[c, r : r + TILE, t * half : (t + 1) * half] = made.astype(BF)
        store_transposed(ids, xn_ref[...], blocks_ref, xt_ref)

    weights = [a for g in gathered for a in g.pair]
    return call(
        body,
        "qkv",
        ids,
        (rows, gain, *weights, *gots),
        [pl.BlockSpec((1, local_rows, width), lambda g, ids: (ids[0], 0, 0)), whole((1, width))]
        + [whole(a.shape) for a in (*weights, *gots)],
        (
            shape((3, length, width), BF),
            shape((fsdp, height, length), BF),
            shape((length, width), BF),
        ),
        [whole((3, length, width)), whole((fsdp, height, length)), whole((length, width))],
        (1,),
        (pltpu.VMEM((length, width), BF), pltpu.VMEM((fsdp, height, length), BF)),
    )


def store_natural(value, out_ref):
    height = out_ref.shape[-2]
    step = 128 // height
    for c in range(value.shape[1] // 128):
        part = value[:, c * 128 : (c + 1) * 128]
        out_ref[c * step : (c + 1) * step] = part.T.reshape(step, height, part.shape[0])


def join_rows(ids, rows, got, fsdp):
    parts, local_rows, width = rows.shape
    length = parts * local_rows
    height = width // fsdp

    def body(ids, rows_ref, got_ref, out_ref, t_ref):
        out_ref[0, pl.ds(pl.multiple_of(ids[0] * local_rows, local_rows), local_rows)] = rows_ref[
            0
        ]
        out_ref[
            0, pl.ds(pl.multiple_of((1 - ids[0]) * local_rows, local_rows), local_rows)
        ] = got_ref[0]
        store_natural(out_ref[0], t_ref.at[0])

    spec = pl.BlockSpec((1, local_rows, width), lambda s, ids: (s ^ ids[0], 0, 0))
    return call(
        body,
        "join_rows",
        ids,
        (rows, got),
        [spec, spec],
        (shape((parts, length, width), BF), shape((parts, fsdp, height, length), BF)),
        [
            pl.BlockSpec((1, length, width), lambda s, ids: (s, 0, 0)),
            pl.BlockSpec((1, fsdp, height, length), lambda s, ids: (s, 0, 0, 0)),
        ],
        (parts,),
    )


def transposed(ids, rows, fsdp):
    length, width = rows.shape
    height = width // fsdp

    def body(ids, rows_ref, t_ref):
        store_natural(rows_ref[...], t_ref)

    return call(
        body,
        "transposed",
        ids,
        (rows,),
        [whole((length, width))],
        (shape((fsdp, height, length), BF),),
        [whole((fsdp, height, length))],
        (1,),
    )[0]


def lane_mask(values, head):
    lanes = lax.broadcasted_iota(jnp.int32, values.shape, 1)
    return jnp.where(lanes // HEAD_DIM == head, values, jnp.zeros_like(values))


def attend(ids, qkv):
    length, width = qkv.shape[1:]
    tiles = length // TILE
    pair = 2 * HEAD_DIM
    heads = width // HEAD_DIM

    def body(ids, q_ref, k_ref, v_ref, *refs):
        o_ref, ot_ref, e_ref, inv_ref, bias_ref, s_ref = refs[-6:]

        @pl.when(pl.program_id(0) == 0)
        def _():
            for i in range(tiles):
                keys = i * TILE + lax.broadcasted_iota(jnp.int32, (2 * TILE, TILE), 0)
                rows = i * TILE + lax.broadcasted_iota(jnp.int32, (2 * TILE, TILE), 1)
                seen = keys <= rows
                for p in range(3):
                    start = ids[4 + p]
                    inside = (keys >= start) & (keys < start + PIECE)
                    inside &= (rows >= start) & (rows < start + PIECE)
                    seen |= inside
                bias_ref[i] = jnp.where(seen, 0.0, masked_score)

        k = k_ref[0]
        vt = v_ref[0].T
        for i in range(tiles):
            used = min(i + 2, tiles)
            q_rows = q_ref[0, i * TILE : (i + 1) * TILE]
            parts = []
            for head in range(2):
                slot = (2 * i + head) % 2
                q_head = lane_mask(q_rows, head)
                top = None
                for j in range(used):
                    s = dot_f32(k[j * TILE : (j + 1) * TILE], q_head, 1, 1)
                    if j >= i:
                        s = s + bias_ref[i, (j - i) * TILE : (j - i + 1) * TILE]
                    s_ref[slot, j] = s
                    now = jnp.max(s.reshape(TILE // 8, 8, TILE), axis=0)
                    top = now if top is None else jnp.maximum(top, now)
                top = jnp.max(top, axis=0, keepdims=True)
                total = None
                out = None
                for j in range(used):
                    e = jnp.exp(s_ref[slot, j] - top)
                    now = jnp.sum(e.reshape(TILE // 8, 8, TILE), axis=0)
                    total = now if total is None else total + now
                    low = e.astype(BF)
                    e_ref[head, j * TILE : (j + 1) * TILE, i * TILE : (i + 1) * TILE] = low
                    now = dot_f32(
                        vt[head * HEAD_DIM : (head + 1) * HEAD_DIM, j * TILE : (j + 1) * TILE],
                        low,
                        1,
                        0,
                    )
                    out = now if out is None else out + now
                inv = 1.0 / jnp.sum(total, axis=0, keepdims=True)
                inv_ref[0, head : head + 1, i * TILE : (i + 1) * TILE] = inv
                parts.append(out * inv)
            both = jnp.concatenate(parts, axis=0)
            ot_ref[:, i * TILE : (i + 1) * TILE] = both.astype(BF)
            o_ref[i * TILE : (i + 1) * TILE] = both.T.astype(BF)

    spec = [
        pl.BlockSpec((1, length, pair), lambda p, ids, c=c: (c, 0, p)) for c in range(3)
    ]
    return call(
        body,
        "attend",
        ids,
        (qkv, qkv, qkv),
        spec,
        (
            shape((length, width), BF),
            shape((width, length), BF),
            shape((heads, length, length), BF),
            shape((heads // 2, 2, length), F32),
        ),
        [
            pl.BlockSpec((length, pair), lambda p, ids: (0, p)),
            pl.BlockSpec((pair, length), lambda p, ids: (p, 0)),
            pl.BlockSpec((2, length, length), lambda p, ids: (p, 0, 0)),
            pl.BlockSpec((1, 2, length), lambda p, ids: (p, 0, 0)),
        ],
        (heads // 2,),
        (
            pltpu.VMEM((tiles, 2 * TILE, TILE), F32),
            pltpu.VMEM((2, tiles, TILE, TILE), F32),
        ),
    )


def attend_back(ids, qkv, d_heads, saved):
    length, width = qkv.shape[1:]
    tiles = length // TILE
    pair = 2 * HEAD_DIM
    heads = width // HEAD_DIM

    def body(ids, q_ref, k_ref, v_ref, d_ref, ot_ref, e_ref, inv_ref, *refs):
        out_ref, ds_ref, dq_ref = refs[-3:]
        k = k_ref[0]
        v = v_ref[0]
        kt = k.T
        dt = d_ref[...].astype(F32).T
        q_heads = []
        d_scaled = []
        deltas = []
        for head in range(2):
            span = slice(head * HEAD_DIM, (head + 1) * HEAD_DIM)
            inv_row = inv_ref[0, head : head + 1]
            mine = dt[span] * inv_row
            deltas.append(jnp.sum(mine * ot_ref[span].astype(F32), axis=0, keepdims=True))
            blank = jnp.zeros((HEAD_DIM, length), BF)
            mine = mine.astype(BF)
            d_scaled.append(
                jnp.concatenate([mine, blank] if head == 0 else [blank, mine], axis=0)
            )
            q_heads.append(lane_mask(q_ref[0], head))
        dq_ref[...] = jnp.zeros_like(dq_ref)
        for j in range(tiles):
            keys = slice(j * TILE, (j + 1) * TILE)
            first = max(j - 1, 0) * TILE
            d_key = None
            d_value = None
            for head in range(2):
                for r in range(first, length, TILE):
                    cols = slice(r, r + TILE)
                    dp = dot_f32(v[keys], d_scaled[head][:, cols], 1, 0)
                    weights = e_ref[head, keys, cols].astype(F32)
                    ds_ref[j % 2, head, :, cols] = (
                        weights * (dp - deltas[head][:, cols])
                    ).astype(BF)
                ds = ds_ref[j % 2, head, :, first:length]
                now = dot_f32(ds, q_heads[head][first:length], 1, 0)
                d_key = now if d_key is None else d_key + now
                now = dot_f32(
                    e_ref[head, keys, first:length], d_scaled[head][:, first:length], 1, 1
                )
                d_value = now if d_value is None else d_value + now
                rows = slice(head * HEAD_DIM, (head + 1) * HEAD_DIM)
                dq_ref[rows, first:length] += dot_f32(kt[rows, keys], ds, 1, 0)
            out_ref[1, keys] = d_key.astype(BF)
            out_ref[2, keys] = d_value.astype(BF)
        out_ref[0] = (dq_ref[...] * HEAD_DIM ** (-0.5)).T.astype(BF)

    spec = [
        pl.BlockSpec((1, length, pair), lambda p, ids, c=c: (c, 0, p)) for c in range(3)
    ]
    return call(
        body,
        "attend_back",
        ids,
        (qkv, qkv, qkv, d_heads, *saved),
        spec
        + [
            pl.BlockSpec((length, pair), lambda p, ids: (0, p)),
            pl.BlockSpec((pair, length), lambda p, ids: (p, 0)),
            pl.BlockSpec((2, length, length), lambda p, ids: (p, 0, 0)),
            pl.BlockSpec((1, 2, length), lambda p, ids: (p, 0, 0)),
        ],
        (shape((3, length, width), BF),),
        [pl.BlockSpec((3, length, pair), lambda p, ids: (0, 0, p))],
        (heads // 2,),
        (pltpu.VMEM((2, 2, TILE, length), BF), pltpu.VMEM((pair, length), F32)),
    )[0]


def out_project(ids, attended, gathered, x, gain):
    length, width = x.shape
    fsdp = gathered.pair[0].shape[0]
    height = width // fsdp
    parts = 2
    half = width // parts

    def body(ids, a_ref, wa_ref, wb_ref, x_ref, gain_ref, hidden_ref, hn_ref, ht_ref):
        w = [
            gathered_rows(ids, (wa_ref, wb_ref), gathered.order, t, height) for t in range(parts)
        ]
        for r in range(0, length, TILE):
            total = x_ref[r : r + TILE].astype(F32)
            for t in range(parts):
                total += dot_f32(a_ref[r : r + TILE, t * half : (t + 1) * half], w[t], 1, 1)
            hidden_ref[r : r + TILE] = total
            hn_ref[r : r + TILE] = (total * rms_scale(total) * gain_ref[...]).astype(BF)
        store_natural(hn_ref[...], ht_ref)

    return call(
        body,
        "out_project",
        ids,
        (attended, *gathered.pair, x, gain),
        [whole((length, width))]
        + [whole(a.shape) for a in gathered.pair]
        + [whole((length, width)), whole((1, width))],
        (
            shape((length, width), F32),
            shape((length, width), BF),
            shape((fsdp, height, length), BF),
        ),
        [whole((length, width)), whole((length, width)), whole((fsdp, height, length))],
        (1,),
    )


def feed_forward(ids, hn, grads, which, packed):
    length, width = hn.shape
    fsdp, rows, units = packed.shape
    height = rows // 3
    tile = 256

    def body(ids, hn_ref, g_ref, w_ref, out_ref):
        w_gate, w_up, w_down = [
            w_ref[:, c * height : (c + 1) * height].reshape(width, tile) for c in range(3)
        ]
        for r in range(0, length, TILE):
            rows = hn_ref[r : r + TILE]
            gate = dot_f32(rows, w_gate, 1, 0)
            up = dot_f32(rows, w_up, 1, 0)
            d_mixed = dot_f32(g_ref[0, r : r + TILE], w_down, 1, 0)
            sig = jax.nn.sigmoid(gate)
            act = gate * sig
            out_ref[0, r : r + TILE] = (
                d_mixed * up * sig * (1.0 + gate * (1.0 - sig))
            ).astype(BF)
            out_ref[1, r : r + TILE] = (d_mixed * act).astype(BF)
            out_ref[2, r : r + TILE] = (act * up).astype(BF)

    return call(
        body,
        "feed_forward",
        ids,
        (hn, grads, packed),
        [
            whole((length, width)),
            pl.BlockSpec((1, length, width), lambda n, ids: (which, 0, 0)),
            pl.BlockSpec((fsdp, rows, tile), lambda n, ids: (0, 0, n)),
        ],
        (shape((3, length, units), BF),),
        [pl.BlockSpec((3, length, tile), lambda n, ids: (0, 0, n))],
        (units // tile,),
    )[0]


def feed_forward_out(ids, own, theirs, packed, hidden):
    length, width = hidden.shape
    fsdp, rows, units = packed.shape
    height = rows // 3
    per = units // UNITS
    kept = length // 2

    def body(ids, own_ref, theirs_ref, w_ref, hidden_ref, keep_ref, send_ref, acc_ref):
        first = pl.program_id(1) == 0

        @pl.when(first & (pl.program_id(0) == 0))
        def _():
            acc_ref[...] = hidden_ref[...]

        @pl.when(first & (pl.program_id(0) == 1))
        def _():
            acc_ref[...] = jnp.zeros_like(acc_ref)

        w = w_ref[...].reshape(width, UNITS)

        def add(m_ref):
            for r in range(0, length, TILE):
                acc_ref[r : r + TILE] += dot_f32(m_ref[0, r : r + TILE], w, 1, 1)

        pl.when(pl.program_id(0) == 0)(lambda: add(own_ref))
        pl.when(pl.program_id(0) == 1)(lambda: add(theirs_ref))

        @pl.when(pl.program_id(1) == per - 1)
        def _():
            keep_ref[0] = acc_ref[pl.ds(pl.multiple_of(ids[0] * kept, kept), kept)]
            send_ref[0] = acc_ref[
                pl.ds(pl.multiple_of((1 - ids[0]) * kept, kept), kept)
            ].astype(BF)

    out_spec = pl.BlockSpec((1, kept, width), lambda s, n, ids: (s ^ ids[0], 0, 0))
    return call(
        body,
        "feed_forward_out",
        ids,
        (own, theirs, packed, hidden),
        [
            pl.BlockSpec((1, length, UNITS), lambda s, n, ids: (2, 0, jnp.where(s == 0, n, per - 1))),
            pl.BlockSpec((1, length, UNITS), lambda s, n, ids: (2, 0, jnp.where(s == 1, n, 0))),
            pl.BlockSpec((fsdp, height, UNITS), lambda s, n, ids: (0, 2, n)),
            whole((length, width)),
        ],
        (shape((2, kept, width), F32), shape((2, kept, width), BF)),
        [out_spec, out_spec],
        (2, per),
        (pltpu.VMEM((length, width), F32),),
    )


def feed_forward_grads(ids, hn_t, hn_t_theirs, grads_t, own, theirs):
    fsdp, height, length = hn_t.shape
    units = own.shape[2]
    per = units // UNITS

    def body(ids, h_ref, h2_ref, g_ref, own_ref, theirs_ref, out_ref):
        def make(a_ref, b_ref):
            for f in range(0, fsdp, 4):
                a = a_ref[f : f + 4].reshape(4 * height, length)
                b = b_ref[f : f + 4].reshape(4 * height, length)
                made = dot_f32(a, own_ref[0], 1, 0) + dot_f32(b, theirs_ref[0], 1, 0)
                out_ref[f : f + 4] = made.astype(BF).reshape(4, height, UNITS)

        pl.when(pl.program_id(0) < 2)(lambda: make(h_ref, h2_ref))
        pl.when(pl.program_id(0) == 2)(lambda: make(g_ref.at[0], g_ref.at[1]))

    side = pl.BlockSpec((1, length, UNITS), lambda c, n, ids: (c, 0, n))
    return call(
        body,
        "feed_forward_grads",
        ids,
        (hn_t, hn_t_theirs, grads_t, own, theirs),
        [whole(hn_t.shape), whole(hn_t.shape), whole(grads_t.shape), side, side],
        (shape((fsdp, 3 * height, units), BF),),
        [pl.BlockSpec((fsdp, height, UNITS), lambda c, n, ids: (0, c, n))],
        (3, per),
    )[0]


def weight_grad(ids, name, sources):
    fsdp, height, length = sources[0][0].shape
    parts = 2
    half = sources[0][1].shape[2] // parts
    tile = min(UNITS, half)
    per = half // tile
    hop = fsdp // 2

    def body(ids, *refs):
        outs = refs[-2:]
        for k in range(len(sources)):
            l_ref, r_ref = refs[2 * k : 2 * k + 2]

            @pl.when(pl.program_id(0) == k)
            def _(l_ref=l_ref, r_ref=r_ref):
                right_tile = r_ref[0]
                for b in range(0, fsdp, 4):
                    block = l_ref[b : b + 4].reshape(4 * height, length)
                    made = dot_f32(block, right_tile, 1, 0).astype(BF)
                    outs[b // hop][0, b % hop : b % hop + 4] = made.reshape(4, height, tile)

    ins, specs = [], []
    for k, (left, right, index) in enumerate(sources):
        ins += [left, right]

        def columns(c, t, n, ids, k=k, index=index):
            at = n * parts + t
            at = jnp.where(c == k, at, 0 if k else half * parts // tile - 1)
            return (index, 0, at)

        specs += [whole(left.shape), pl.BlockSpec((1, length, tile), columns)]
    spec = pl.BlockSpec((1, hop, height, tile), lambda c, t, n, ids: (t ^ ids[0], 0, c, n))
    return call(
        body,
        name,
        ids,
        tuple(ins),
        specs,
        (shape((parts, hop, len(sources) * height, half), BF),) * 2,
        [spec, spec],
        (len(sources), parts, per),
    )


def feed_forward_back(ids, stacked, packed, cut=None):
    length = stacked.shape[1]
    fsdp, rows, units = packed.shape
    height = rows // 3
    width = fsdp * height
    per = units // UNITS

    def body(ids, d_ref, w_ref, *refs):
        acc_ref = refs[-1]

        @pl.when(pl.program_id(0) == 0)
        def _():
            acc_ref[...] = jnp.zeros_like(acc_ref)

        w_gate, w_up = [
            w_ref[:, c * height : (c + 1) * height].reshape(width, UNITS) for c in range(2)
        ]
        for r in range(0, length, TILE):
            acc_ref[r : r + TILE] += dot_f32(d_ref[0, r : r + TILE], w_gate, 1, 1) + dot_f32(
                d_ref[1, r : r + TILE], w_up, 1, 1
            )

        @pl.when(pl.program_id(0) == per - 1)
        def _():
            if cut is None:
                refs[0][...] = acc_ref[...]
            else:
                refs[0][...] = acc_ref[:cut].astype(BF)
                refs[1][...] = acc_ref[cut:].astype(BF)

    outs = [shape((length, width), F32)]
    if cut is not None:
        outs = [shape((cut, width), BF), shape((length - cut, width), BF)]
    return call(
        body,
        "feed_forward_back",
        ids,
        (stacked, packed),
        [
            pl.BlockSpec((2, length, UNITS), lambda n, ids: (0, 0, n)),
            pl.BlockSpec((fsdp, 2 * height, UNITS), lambda n, ids: (0, 0, n)),
        ],
        tuple(outs),
        [whole(o.shape) for o in outs],
        (per,),
        (pltpu.VMEM((length, width), F32),),
    )


def norm_and_project_back(ids, share, gots, hidden, grads, gain, gathered):
    length, width = hidden.shape
    fsdp = gathered.pair[0].shape[0]
    height = width // fsdp
    parts = 2
    half = width // parts

    cut = gots[0].shape[0]

    def body(ids, share_ref, got_ref, tail_ref, hidden_ref, g_ref, gain_ref, wa_ref, wb_ref, *refs):
        dh_ref, lt_ref, out_ref, low_ref = refs
        for r in range(0, length, TILE):
            rows = hidden_ref[r : r + TILE]
            scale = rms_scale(rows)
            normed = rows * scale
            theirs = got_ref[r : r + TILE] if r < cut else tail_ref[r - cut : r - cut + TILE]
            d_normed = share_ref[r : r + TILE] + theirs.astype(F32)
            dh = g_ref[0, r : r + TILE].astype(F32) + norm_backward_pass(
                d_normed, normed, scale, gain_ref[...]
            )
            dh_ref[r : r + TILE] = dh
            low_ref[r : r + TILE] = dh.astype(BF)
        for t in range(parts):
            w = gathered_rows(ids, (wa_ref, wb_ref), gathered.order, t, height)
            for r in range(0, length, TILE):
                out_ref[r : r + TILE, t * half : (t + 1) * half] = dot_f32(
                    low_ref[r : r + TILE], w, 1, 0
                ).astype(BF)
        store_natural(low_ref[...], lt_ref)

    square = whole((length, width))
    return call(
        body,
        "norm_and_project_back",
        ids,
        (share, *gots, hidden, grads, gain, *gathered.pair),
        [
            square,
            *[whole(g.shape) for g in gots],
            square,
            pl.BlockSpec((1, length, width), lambda g, ids: (0, 0, 0)),
            whole((1, width)),
        ]
        + [whole(a.shape) for a in gathered.pair],
        (
            shape((length, width), F32),
            shape((fsdp, height, length), BF),
            shape((length, width), BF),
        ),
        [square, whole((fsdp, height, length)), square],
        (1,),
        (pltpu.VMEM((length, width), BF),),
    )


def out_grad_halves(ids, left, right):
    fsdp, height, length = left.shape
    half = right.shape[1] // 2

    def body(ids, l_ref, r_ref, keep_ref, send_ref):
        def make(out_ref):
            for f in range(0, fsdp, 4):
                a = l_ref[f : f + 4].reshape(4 * height, length)
                out_ref[f : f + 4] = (
                    dot_f32(a, r_ref[...], 1, 0).astype(BF).reshape(4, height, half)
                )

        pl.when(pl.program_id(0) == 0)(lambda: make(send_ref))
        pl.when(pl.program_id(0) == 1)(lambda: make(keep_ref))

    blocks = whole((fsdp, height, half))
    return call(
        body,
        "grad_out",
        ids,
        (left, right),
        [whole(left.shape), pl.BlockSpec((length, half), lambda s, ids: (0, (1 - s) ^ ids[0]))],
        (shape((fsdp, height, half), BF),) * 2,
        [blocks, blocks],
        (2,),
    )


def store_lines(out_ref, values):
    lines = values.shape[1] // 128
    for n in range(lines):
        out_ref[0, pl.ds(n, values.shape[0], stride=lines)] = values[:, n * 128 : (n + 1) * 128]


def qkv_back(ids, d_qkv, gathered, x, dh, gain, sent):
    length, width = x.shape
    fsdp = gathered[1].pair[0].shape[0]
    height = width // fsdp
    parts = 2
    half = width // parts
    kept = length // parts

    def body(ids, d_ref, *refs):
        x_ref, dh_ref, gain_ref, out_ref, acc_ref = refs[-5:]
        for c in range(3):
            for t in range(parts):
                w = gathered_rows(ids, refs[2 * c : 2 * c + 2], gathered[c].order, t, height)
                for r in range(0, kept, TILE):
                    part = dot_f32(d_ref[c, r : r + TILE, t * half : (t + 1) * half], w, 1, 1)
                    if c == 0 and t == 0:
                        acc_ref[r : r + TILE] = part
                    else:
                        acc_ref[r : r + TILE] += part
        for r in range(0, kept, TILE):
            rows = x_ref[r : r + TILE].astype(F32)
            scale = rms_scale(rows)
            normed = rows * scale
            d_normed = acc_ref[r : r + TILE]
            acc_ref[r : r + TILE] = dh_ref[r : r + TILE] + norm_backward_pass(
                d_normed, normed, scale, gain_ref[...]
            )
        if sent:
            out_ref[...] = acc_ref[...].astype(BF)
        else:
            store_lines(out_ref, acc_ref)

    def rows(ids):
        return 1 - ids[0] if sent else ids[0]

    weights = [a for g in gathered for a in g.pair]
    lines = kept * width // 128
    return call(
        body,
        "qkv_back",
        ids,
        (d_qkv, *weights, x, dh, gain),
        [pl.BlockSpec((3, kept, width), lambda g, ids: (0, rows(ids), 0))]
        + [whole(a.shape) for a in weights]
        + [pl.BlockSpec((kept, width), lambda g, ids: (rows(ids), 0))] * 2
        + [whole((1, width))],
        (shape((kept, width), BF) if sent else shape((parts, lines, 128), F32),),
        [
            whole((kept, width))
            if sent
            else pl.BlockSpec((1, lines, 128), lambda g, ids: (ids[0], 0, 0)),
        ],
        (1,),
        (pltpu.VMEM((kept, width), F32),),
    )[0]


def place_rows(ids, got, lines):
    kept, width = got.shape

    def body(ids, got_ref, _, out_ref, wide_ref):
        wide_ref[...] = got_ref[...].astype(F32)
        store_lines(out_ref, wide_ref)

    return call(
        body,
        "place_rows",
        ids,
        (got, lines),
        [whole((kept, width)), IN_PLACE],
        (shape(lines.shape, F32),),
        [pl.BlockSpec((1,) + lines.shape[1:], lambda g, ids: (1 - ids[0], 0, 0))],
        (1,),
        (pltpu.VMEM((kept, width), F32),),
        aliases={2: 0},
    )[0]


def three_parts(values):
    high = values.astype(BF)
    rest = values - high.astype(F32)
    middle = rest.astype(BF)
    return jnp.stack([high, middle, (rest - middle.astype(F32)).astype(BF)], -1)


def local_sequence(
    tokens, piece_starts, gain_attn, w_qkv, w_out, gain_mlp, w_gate_up, w_down, out_grad
):
    fsdp = lax.axis_size("fsdp")
    parts = lax.axis_size("tensor")
    me_f = lax.axis_index("fsdp")
    me_t = lax.axis_index("tensor")
    local_rows = tokens.shape[1]
    height = w_qkv.shape[1]
    half = w_qkv.shape[2]
    share = gain_attn.shape[0]

    starts = lax.dynamic_index_in_dim(piece_starts, me_t, 0, keepdims=False)[0]
    ids = jnp.stack([me_t, me_f // 2, me_f % 2, me_f]).astype(jnp.int32)
    ids = jnp.concatenate([ids, starts])
    rows_in = tokens.reshape(parts, local_rows, D)
    grads_in = out_grad.reshape(parts, local_rows, D)

    def other(rows):
        return lax.dynamic_index_in_dim(rows, 1 - me_t, 0, keepdims=False)

    wk = Gathered(w_qkv[1], (TENSOR, Z_FAR, X, Z_NEAR))
    wv = Gathered(w_qkv[2], (TENSOR, Z_NEAR, Z_FAR, X))
    gains = three_parts(jnp.stack([gain_attn, gain_mlp])).reshape(1, -1)
    gains = jnp.pad(gains, ((0, 7), (0, half - gains.shape[1])))
    wq = Gathered(jnp.concatenate([w_qkv[0], gains]), (Z_FAR, X, Z_NEAR, TENSOR))
    o_mine = w_out.T
    ff_mine = jnp.concatenate([w_gate_up.reshape(2 * height, -1), w_down.T])
    aways = jnp.split(other(rows_in), 2)
    three = [wq, wk, wv]
    o_mine = after(o_mine, three)
    wo = Gathered(o_mine, (Z_FAR, TENSOR, Z_NEAR, X))
    got_one = swap(aways[0], TENSOR)
    got_one, aways[1] = after((got_one, aways[1]), [*three, wo])
    got_two = swap(aways[1], TENSOR)
    got_two = after(got_two, [*three, wo])
    ff_mine = after(ff_mine, [*three, wo])
    packed = lax.all_gather(ff_mine, "fsdp", axis=0, tiled=False)
    got_rows = after((got_one, got_two), three)

    each = jnp.arange(fsdp * parts)
    each_f, each_t = each // parts, each % parts
    at = position(wq.order, each_f, each_t) ^ position(wq.order, me_f, me_t)
    at = at + fsdp * ((each_f ^ me_f) % 2)
    gains = jnp.concatenate([a[:, height, : 6 * share] for a in wq.pair])[at]
    gains = jnp.sum(gains.reshape(fsdp * parts, 2, share, 3).astype(F32), axis=3)
    gain_one, gain_two = [gains[:, i].reshape(1, D) for i in range(2)]

    qkv, xt, x = make_qkv(ids, rows_in, got_rows, gain_one, (wq, wk, wv))
    _, away = lax.optimization_barrier((got_rows, grads_in))
    got_grads = swap(away, TENSOR)
    qkv = after(qkv, [wo])
    attended, *saved = after(attend(ids, qkv), [wo])
    hidden, hn, ht = out_project(ids, attended, wo, x, gain_two)
    hn_theirs = swap(hn, TENSOR)
    grads, gt = join_rows(ids, grads_in, got_grads, fsdp)
    hn, grads, packed = lax.optimization_barrier((hn, grads, packed))

    own = feed_forward(ids, hn, grads, 0, packed)
    own, hn_theirs = lax.optimization_barrier((own, hn_theirs))
    theirs = feed_forward(ids, hn_theirs, grads, 1, packed)
    ht_theirs = transposed(ids, hn_theirs, fsdp)
    *d_theirs, = feed_forward_back(ids, theirs, packed, local_rows * parts * 3 // 4)
    d_theirs, ht_theirs, own = lax.optimization_barrier((d_theirs, ht_theirs, own))
    got_one = swap(d_theirs[0], TENSOR)
    made = feed_forward_grads(ids, ht, ht_theirs, gt, own, theirs)
    made, own, got_one, d_tail = lax.optimization_barrier((made, own, got_one, d_theirs[1]))
    summed = lax.psum_scatter(made, "fsdp", scatter_dimension=0, tiled=False)
    got_two = swap(d_tail, TENSOR)
    share_own = feed_forward_back(ids, own, packed)[0]
    share_own, got_two = lax.optimization_barrier((share_own, got_two))
    dh, dt, d_attended = norm_and_project_back(
        ids, share_own, (got_one, got_two), hidden, grads, gain_two, wo
    )

    def join(values, sums):
        values, gots = lax.optimization_barrier((values, [s.got for s in sums]))
        for s, g in zip(sums, gots):
            s.got = g
        made = halve(ids, sums)
        return lax.optimization_barrier((values, made))[0]

    o_keep, o_send = out_grad_halves(ids, dt, attended)
    o_send, d_attended, own, theirs = lax.optimization_barrier((o_send, d_attended, own, theirs))
    o_got = swap(o_send, TENSOR)
    keep_out, send_out = feed_forward_out(ids, own, theirs, packed, hidden)
    d_attended, send_out, o_got = lax.optimization_barrier((d_attended, send_out, o_got))
    o_sum = (o_keep.astype(F32) + o_got.astype(F32)).astype(BF)
    got_out = swap(send_out, TENSOR)
    d_qkv = attend_back(ids, qkv, d_attended, saved)

    orders = (
        (X, Z_NEAR, Z_FAR, TENSOR),
        (Z_NEAR, X, TENSOR, Z_FAR),
        (TENSOR, Z_FAR, X, Z_NEAR),
    )
    sums = []
    for c, order in enumerate(orders):
        made = weight_grad(ids, "grad_qkv", [(xt, d_qkv, c)])
        made, d_qkv = lax.optimization_barrier((made, d_qkv))
        sums.append(Summed(*made, order))
    d_qkv = join(d_qkv, sums)
    sent = qkv_back(ids, d_qkv, (wq, wk, wv), x, dh, gain_one, True)
    sent, d_qkv, got_out, summed, o_sum = join((sent, d_qkv, got_out, summed, o_sum), sums)
    o_sum = lax.psum_scatter(o_sum, "fsdp", scatter_dimension=0, tiled=False)
    layer_out = (keep_out + got_out.astype(F32)).astype(BF).reshape(tokens.shape)
    got_grad = swap(sent, TENSOR)
    lines = qkv_back(ids, d_qkv, (wq, wk, wv), x, dh, gain_one, False)
    lines = join(lines, sums)
    halve(ids, sums)
    halve(ids, sums)

    input_grad = place_rows(ids, got_grad, lines).reshape(tokens.shape)
    qkv_grad = jnp.stack([s.result for s in sums])
    summed = summed.astype(F32)
    gate_up_grad = summed[: 2 * height].reshape(w_gate_up.shape)
    from_qkv = jnp.sum(w_qkv.astype(F32) * qkv_grad, axis=(0, 2))
    from_gate_up = jnp.sum(w_gate_up.astype(F32) * gate_up_grad, axis=(0, 2))
    both = jnp.stack([from_qkv, from_gate_up]).reshape(2, parts, share)
    mine = lax.dynamic_index_in_dim(both, me_t, 1, keepdims=False)
    theirs = lax.dynamic_index_in_dim(both, 1 - me_t, 1, keepdims=False)
    mine = mine + swap(theirs, TENSOR)
    return (
        layer_out,
        input_grad,
        mine[0] / gain_attn,
        qkv_grad,
        o_sum.astype(F32).T,
        mine[1] / gain_mlp,
        gate_up_grad,
        summed[2 * height :].T,
    )


def local_any(tokens, *rest):
    sizes = (lax.axis_size("tensor"), tokens.shape[0], tokens.shape[2], lax.axis_size("fsdp"))
    if sizes == (2, 2, 1, 16):
        return local_sequence(tokens, *rest)
    return local(tokens, *rest)


def solution(mesh):
    return jax.shard_map(
        local_any,
        mesh=mesh,
        in_specs=(
            P(None, "tensor", "fsdp", None),
            P(None, "fsdp", None),
            P(("fsdp", "tensor")),
            P(None, "fsdp", "tensor"),
            P("tensor", "fsdp"),
            P(("fsdp", "tensor")),
            P(None, "fsdp", "tensor"),
            P("tensor", "fsdp"),
            P(None, "tensor", "fsdp", None),
        ),
        out_specs=(
            P(None, "tensor", "fsdp", None),
            P(None, "tensor", "fsdp", None),
            P(("fsdp", "tensor")),
            P(None, "fsdp", "tensor"),
            P("tensor", "fsdp"),
            P(("fsdp", "tensor")),
            P(None, "fsdp", "tensor"),
            P("tensor", "fsdp"),
        ),
        check_vma=False,
    )
```

```python
import itertools

import jax
import jax.numpy as jnp
from jax import lax
from jax.experimental import pallas as pl
from jax.experimental.pallas import tpu as pltpu
from jax.sharding import PartitionSpec as P

D = 1024
HEAD_DIM = 64
QBLOCK = 512
PIECE = 256


norm_eps = 1e-05
masked_score = -1e30


def rms_scale(values_float_rows):
    return lax.rsqrt(
        jnp.mean(values_float_rows * values_float_rows, axis=-1, keepdims=True) + norm_eps
    )


def norm_backward_pass(d_normed, normed_pre, scale_rows, gain_vector_row):
    d_scaled = d_normed * gain_vector_row
    return scale_rows * (
        d_scaled - normed_pre * jnp.mean(d_scaled * normed_pre, axis=-1, keepdims=True)
    )


def piece_index_labels(starts_row, length):
    positions = jnp.arange(length, dtype=jnp.int32)[:, None]
    inside = (positions >= starts_row[None, :]) & (positions < starts_row[None, :] + PIECE)
    numbers = jnp.arange(1, starts_row.shape[0] + 1, dtype=jnp.int32)
    return jnp.sum(jnp.where(inside, numbers[None, :], 0), axis=1)


def allowed_block(labels, first_row, key_count):
    row_ids = first_row + jnp.arange(QBLOCK, dtype=jnp.int32)
    col_ids = jnp.arange(key_count, dtype=jnp.int32)
    row_labels = labels[first_row : first_row + QBLOCK]
    causal = col_ids[None, :] <= row_ids[:, None]
    same_piece = (row_labels[:, None] == labels[None, :]) & (row_labels[:, None] > 0)
    return causal | same_piece


def attend_forward(queries, keys_all, values_all, labels, key_spans):
    score_scale = HEAD_DIM ** (-0.5)
    outputs = []
    totals = []
    for first_row, key_count in key_spans:
        block_q = queries[first_row : first_row + QBLOCK]
        scores = (
            jnp.einsum("qhd,khd->hqk", block_q, keys_all, preferred_element_type=jnp.float32)
            * score_scale
        )
        scores = jnp.where(allowed_block(labels, first_row, key_count)[None], scores, masked_score)
        row_max = jnp.max(scores, axis=-1, keepdims=True)
        exp_scores = jnp.exp(scores - row_max)
        row_total = jnp.sum(exp_scores, axis=-1, keepdims=True)
        attn_probs = (exp_scores / row_total).astype(jnp.bfloat16)
        block_out = jnp.einsum(
            "hqk,khd->qhd", attn_probs, values_all, preferred_element_type=jnp.float32
        )
        outputs.append(block_out.astype(jnp.bfloat16))
        totals.append((row_max + jnp.log(row_total))[..., 0])
    return (jnp.concatenate(outputs, 0), jnp.concatenate(totals, 1))


def attend_backward(queries, keys_all, values_all, labels, log_total, d_heads, key_spans):
    score_scale = HEAD_DIM ** (-0.5)
    query_parts = []
    d_keys = jnp.zeros(keys_all.shape, jnp.float32)
    d_values = jnp.zeros(values_all.shape, jnp.float32)
    for first_row, key_count in key_spans:
        block_q = queries[first_row : first_row + QBLOCK]
        block_d = d_heads[first_row : first_row + QBLOCK]
        scores = (
            jnp.einsum("qhd,khd->hqk", block_q, keys_all, preferred_element_type=jnp.float32)
            * score_scale
        )
        mask_now = allowed_block(labels, first_row, key_count)[None]
        attn_probs = jnp.where(
            mask_now, jnp.exp(scores - log_total[:, first_row : first_row + QBLOCK, None]), 0.0
        )
        probs_low = attn_probs.astype(jnp.bfloat16)
        d_probs = jnp.einsum(
            "qhd,khd->hqk", block_d, values_all, preferred_element_type=jnp.float32
        )
        row_dot = jnp.sum(attn_probs * d_probs, axis=-1, keepdims=True)
        d_scores = (attn_probs * (d_probs - row_dot)).astype(jnp.bfloat16)
        query_parts.append(
            jnp.einsum("hqk,khd->qhd", d_scores, keys_all, preferred_element_type=jnp.float32)
            * score_scale
        )
        d_keys = d_keys.at[:key_count].add(
            jnp.einsum("hqk,qhd->khd", d_scores, block_q, preferred_element_type=jnp.float32)
            * score_scale
        )
        d_values = d_values.at[:key_count].add(
            jnp.einsum("hqk,qhd->khd", probs_low, block_d, preferred_element_type=jnp.float32)
        )
    return (jnp.concatenate(query_parts, 0), d_keys, d_values)


def attention_forward(qkv_low, labels_all, key_spans):
    length, seq_count, width = (qkv_low.shape[0], qkv_low.shape[1], qkv_low.shape[3])
    per_seq = jnp.moveaxis(qkv_low, 1, 0).reshape(seq_count, length, 3, width // HEAD_DIM, HEAD_DIM)

    def one_seq(seq_items):
        seq_qkv, labels = seq_items
        return attend_forward(seq_qkv[:, 0], seq_qkv[:, 1], seq_qkv[:, 2], labels, key_spans)

    seq_outs, totals = lax.map(one_seq, (per_seq, labels_all))
    return (jnp.moveaxis(seq_outs.reshape(seq_count, length, width), 0, 1), totals)


def attention_backward(qkv_low, labels_all, totals, d_attended, key_spans):
    length, seq_count, width = (qkv_low.shape[0], qkv_low.shape[1], qkv_low.shape[3])
    per_seq = jnp.moveaxis(qkv_low, 1, 0).reshape(seq_count, length, 3, width // HEAD_DIM, HEAD_DIM)
    d_seq = jnp.moveaxis(d_attended, 1, 0).reshape(seq_count, length, width // HEAD_DIM, HEAD_DIM)

    def one_seq(seq_items):
        seq_qkv, labels, log_total, seq_d = seq_items
        d_query, d_keys, d_values = attend_backward(
            seq_qkv[:, 0], seq_qkv[:, 1], seq_qkv[:, 2], labels, log_total, seq_d, key_spans
        )
        return jnp.stack([d_query, d_keys, d_values], 1).astype(jnp.bfloat16)

    seq_grads = lax.map(one_seq, (per_seq, labels_all, totals, d_seq))
    return jnp.moveaxis(seq_grads, 0, 1).reshape(length, seq_count, 3, width)


def fetch_weights(w_qkv, w_out, w_gate_up, w_down):
    qkv_all, out_all, gate_up_all, down_weight_full = (
        lax.all_gather(w_qkv, "fsdp", axis=1, tiled=True),
        lax.all_gather(w_out, "fsdp", axis=1, tiled=True),
        lax.all_gather(w_gate_up, "fsdp", axis=1, tiled=True),
        lax.all_gather(w_down, "fsdp", axis=1, tiled=True),
    )
    return (qkv_all, out_all, gate_up_all, down_weight_full)


def local(tokens, piece_starts, gain_attn, w_qkv, w_out, gain_mlp, w_gate_up, w_down, out_grad):
    both_gains = lax.all_gather(
        jnp.stack([gain_attn, gain_mlp]), ("fsdp", "tensor"), axis=1, tiled=True
    )
    local_rows = tokens.shape[1]
    length = local_rows * lax.axis_size("tensor")
    key_spans = [(first_row, length) for first_row in range(0, length, QBLOCK)]

    def label_row(starts_row):
        return piece_index_labels(starts_row, length)

    labels_every = jax.vmap(jax.vmap(label_row))(piece_starts)
    ff_cols = w_gate_up.shape[2]
    acc_gain = jnp.zeros((2, D), jnp.float32)
    acc_qkv = jnp.zeros((3, D, w_qkv.shape[2]), jnp.float32)
    acc_out = jnp.zeros((w_out.shape[0], D), jnp.float32)
    acc_gate_up = jnp.zeros((2, D, ff_cols), jnp.float32)
    acc_down = jnp.zeros((ff_cols, D), jnp.float32)
    layer_outs = []
    input_grads = []
    for micro_idx in range(tokens.shape[0]):
        weights = fetch_weights(w_qkv, w_out, w_gate_up, w_down)
        qkv_all, out_all, gate_up_all, down_weight_full = weights
        rows_f32 = tokens[micro_idx].astype(jnp.float32)
        scale_attn = rms_scale(rows_f32)
        pre_attn = rows_f32 * scale_attn
        normed = (pre_attn * both_gains[0]).astype(jnp.bfloat16)
        piece_rows = lax.all_gather(normed, "tensor", axis=0, tiled=True)
        made = jnp.einsum("lsd,cde->lsce", piece_rows, qkv_all, preferred_element_type=jnp.float32)
        qkv_low = made.astype(jnp.bfloat16)
        attended, log_total = attention_forward(qkv_low, labels_every[micro_idx], key_spans)
        rows_now = lax.slice_in_dim(attended, 0, local_rows * lax.axis_size("tensor"), axis=0)
        attn_part = lax.psum_scatter(
            jnp.einsum("lsc,cd->lsd", rows_now, out_all, preferred_element_type=jnp.float32).astype(
                jnp.bfloat16
            ),
            "tensor",
            scatter_dimension=0,
            tiled=True,
        ).astype(jnp.float32)
        hidden = rows_f32 + attn_part
        scale_mlp = rms_scale(hidden)
        pre_mlp = hidden * scale_mlp
        normed_mlp = (pre_mlp * both_gains[1]).astype(jnp.bfloat16)
        expand_piece_rows = lax.all_gather(normed_mlp, "tensor", axis=0, tiled=True)
        gate_up = jnp.einsum(
            "lsd,cdf->lscf", expand_piece_rows, gate_up_all, preferred_element_type=jnp.float32
        )
        gate_part = gate_up[:, :, 0]
        up_part = gate_up[:, :, 1]
        sigmoid_gate = jax.nn.sigmoid(gate_part)
        activated = gate_part * sigmoid_gate
        mixed_lowp_rows = (activated * up_part).astype(jnp.bfloat16)
        down_rows_now = lax.slice_in_dim(
            mixed_lowp_rows, 0, local_rows * lax.axis_size("tensor"), axis=0
        )
        mlp_part = lax.psum_scatter(
            jnp.einsum(
                "meg,gp->mep", down_rows_now, down_weight_full, preferred_element_type=jnp.float32
            ).astype(jnp.bfloat16),
            "tensor",
            scatter_dimension=0,
            tiled=True,
        ).astype(jnp.float32)
        layer_outs.append((hidden + mlp_part).astype(jnp.bfloat16))
        qkv_all, out_all, gate_up_all, down_weight_full = fetch_weights(
            w_qkv, w_out, w_gate_up, w_down
        )
        grad_rows = out_grad[micro_idx]
        down_piece_rows = lax.all_gather(grad_rows, "tensor", axis=0, tiled=True)
        d_mixed = jnp.einsum(
            "xum,tm->xut", down_piece_rows, down_weight_full, preferred_element_type=jnp.float32
        )
        acc_down = acc_down + jnp.einsum(
            "zmp,zme->pe", mixed_lowp_rows, down_piece_rows, preferred_element_type=jnp.float32
        )
        d_gate = d_mixed * up_part * sigmoid_gate * (1.0 + gate_part * (1.0 - sigmoid_gate))
        d_up = d_mixed * activated
        d_gate_up = jnp.stack([d_gate, d_up], 2).astype(jnp.bfloat16)
        acc_gate_up = acc_gate_up + jnp.einsum(
            "lsd,lscf->cdf", expand_piece_rows, d_gate_up, preferred_element_type=jnp.float32
        )
        mlp_rows_now = lax.slice_in_dim(d_gate_up, 0, local_rows * lax.axis_size("tensor"), axis=0)
        d_normed_mlp = lax.psum_scatter(
            jnp.einsum(
                "lscf,cdf->lsd", mlp_rows_now, gate_up_all, preferred_element_type=jnp.float32
            ).astype(jnp.bfloat16),
            "tensor",
            scatter_dimension=0,
            tiled=True,
        ).astype(jnp.float32)
        gain_mlp_part = jnp.sum(d_normed_mlp * pre_mlp, axis=(0, 1))
        d_hidden = grad_rows.astype(jnp.float32) + norm_backward_pass(
            d_normed_mlp, pre_mlp, scale_mlp, both_gains[1]
        )
        attention_gradient_lowp = d_hidden.astype(jnp.bfloat16)
        out_piece_rows = lax.all_gather(attention_gradient_lowp, "tensor", axis=0, tiled=True)
        out_made = jnp.einsum(
            "lsd,cd->lsc", out_piece_rows, out_all, preferred_element_type=jnp.float32
        )
        d_attended = out_made.astype(jnp.bfloat16)
        acc_out = acc_out + jnp.einsum(
            "lsc,lsd->cd", attended, out_piece_rows, preferred_element_type=jnp.float32
        )
        d_qkv = attention_backward(
            qkv_low, labels_every[micro_idx], log_total, d_attended, key_spans
        )
        acc_qkv = acc_qkv + jnp.einsum(
            "lsd,lsce->cde", piece_rows, d_qkv, preferred_element_type=jnp.float32
        )
        d_normed = lax.psum_scatter(
            jnp.einsum("lsce,cde->lsd", d_qkv, qkv_all, preferred_element_type=jnp.float32).astype(
                jnp.bfloat16
            ),
            "tensor",
            scatter_dimension=0,
            tiled=True,
        ).astype(jnp.float32)
        gain_attn_part = jnp.sum(d_normed * pre_attn, axis=(0, 1))
        input_grads.append(
            d_hidden + norm_backward_pass(d_normed, pre_attn, scale_attn, both_gains[0])
        )
        acc_gain = acc_gain + jnp.stack([gain_attn_part, gain_mlp_part])
    gain_rows, qkv_rows, out_rows_sum, gate_up_rows, down_rows_sum = (
        lax.psum_scatter(
            acc_gain.astype(jnp.bfloat16), "fsdp", scatter_dimension=1, tiled=True
        ).astype(jnp.float32),
        lax.psum_scatter(
            acc_qkv.astype(jnp.bfloat16), "fsdp", scatter_dimension=1, tiled=True
        ).astype(jnp.float32),
        lax.psum_scatter(
            acc_out.astype(jnp.bfloat16), "fsdp", scatter_dimension=1, tiled=True
        ).astype(jnp.float32),
        lax.psum_scatter(
            acc_gate_up.astype(jnp.bfloat16), "fsdp", scatter_dimension=1, tiled=True
        ).astype(jnp.float32),
        lax.psum_scatter(
            acc_down.astype(jnp.bfloat16), "fsdp", scatter_dimension=1, tiled=True
        ).astype(jnp.float32),
    )
    gain_shares = lax.psum_scatter(gain_rows, "tensor", scatter_dimension=1, tiled=True)
    return (
        jnp.stack(layer_outs, 0),
        jnp.stack(input_grads, 0),
        gain_shares[0],
        qkv_rows,
        out_rows_sum,
        gain_shares[1],
        gate_up_rows,
        down_rows_sum,
    )


BF = jnp.bfloat16
F32 = jnp.float32
TILE = 256
UNITS = 512
O_ROWS = (16, 16, 32)
CORE, TENSOR, X, Z_NEAR, Z_FAR = 1, 0, 2, 4, 8


def dot_f32(a, b, ca, cb):
    return lax.dot_general(a, b, (((ca,), (cb,)), ((), ())), preferred_element_type=F32)


def call(body, name, ids, ins, in_specs, outs, out_specs, grid, scratch=(), aliases=None):
    return pl.pallas_call(
        body,
        name=name,
        out_shape=outs,
        grid_spec=pltpu.PrefetchScalarGridSpec(
            num_scalar_prefetch=1,
            grid=grid,
            in_specs=in_specs,
            out_specs=out_specs,
            scratch_shapes=list(scratch),
        ),
        input_output_aliases=aliases or {},
        compiler_params=pltpu.CompilerParams(
            dimension_semantics=("arbitrary",) * len(grid), vmem_limit_bytes=56 * 2**20
        ),
        cost_estimate=pl.CostEstimate(flops=1024, bytes_accessed=1024, transcendentals=0),
    )(ids, *ins)


def shape(dims, dtype):
    return jax.ShapeDtypeStruct(dims, dtype)


def whole(dims):
    zeros = (0,) * len(dims)
    return pl.BlockSpec(dims, lambda *_: zeros)


IN_PLACE = pl.BlockSpec(memory_space=pl.ANY)


def store_transposed(ids, value, blocks_ref, out_ref):
    count, height = blocks_ref.shape[0], blocks_ref.shape[1]
    step = 128 // height
    for c in range(value.shape[1] // 128):
        part = value[:, c * 128 : (c + 1) * 128]
        blocks_ref[c * step : (c + 1) * step] = part.T.reshape(step, height, part.shape[0])
    for core in range(2):
        for pair in range(count // 2):
            source = 2 * (pair ^ ids[1]) + (core ^ ids[2])
            out_ref[core * (count // 2) + pair] = blocks_ref[source]


def position(order, f, t):
    at = 0
    for k, bit in enumerate(order):
        value = t if bit == TENSOR else (f // bit) % 2
        at = at + value * 2**k
    return at


def swap(value, bit):
    if bit == TENSOR:
        return lax.ppermute(value, "tensor", [(0, 1), (1, 0)])
    return lax.ppermute(value, "fsdp", [(i, i ^ bit) for i in range(lax.axis_size("fsdp"))])


class Gathered:
    def __init__(self, mine, order):
        self.order = order
        self.left = [*order, CORE]
        self.held = mine
        self.rows = mine.shape
        self.ready = False
        self.begin()

    def begin(self):
        self.got = swap(self.held, self.left[0])
        if len(self.left) == 2:
            self.early = swap(self.held, CORE)

    def advance(self):
        if self.left.pop(0) == CORE:
            arrays = (self.held, self.last, self.early, self.got)
            self.arrays = [a.reshape((-1,) + self.rows) for a in arrays]
            self.ready = True
        elif self.left == [CORE]:
            self.last = self.got
            self.got = swap(self.last, CORE)
        else:
            self.held = jnp.stack([self.held, self.got])
            self.begin()


class Summed:
    def __init__(self, keep, send, order):
        dims = (2,) * 4 + keep.shape[2:]
        axes = (TENSOR, Z_FAR, Z_NEAR, X)
        self.arrays = [(keep.reshape(dims), axes)]
        self.axes = axes
        self.left = list(order)
        self.got = swap(send.reshape(dims), CORE)
        self.bit = None

    def received(self):
        self.arrays.append((self.got, self.axes))
        self.bit = self.left.pop(0) if self.left else None
        self.axes = tuple(a for a in self.axes if a != self.bit)


def halve(ids, sums):
    for s in sums:
        s.received()
    steps = 2 if any(s.axes for s in sums) else 1
    ins, in_specs, outs, out_specs, counts = [], [], [], [], []
    for s in sums:
        rows, columns = s.arrays[0][0].shape[-2:]
        split = s.axes[0] if steps == 2 and s.axes else None

        def spec(axes, now=s.axes, bit=s.bit, split=split, tail=(rows, columns)):
            block = tuple(2 if a in now and a != split else None for a in axes)

            def index(g, ids):
                at = tuple(g if a == split else int(a == bit and a not in now) for a in axes)
                return (*at, 0, 0)

            return pl.BlockSpec(block + tail, index)

        for array, axes in s.arrays:
            ins.append(array)
            in_specs.append(spec(axes))
        counts.append(len(s.arrays))
        kind = F32 if s.bit is None else BF
        outs.append(shape((2,) * len(s.axes) + (rows, columns), kind))
        out_specs.append(spec(s.axes))

    def body(ids, *refs):
        out_refs = refs[len(ins) :]
        at = 0
        for out_ref, count in zip(out_refs, counts):
            for where in itertools.product(range(2), repeat=len(out_ref.shape) - 2):
                total = refs[at][where].astype(F32)
                for k in range(1, count):
                    total += refs[at + k][where].astype(F32)
                out_ref[where] = total.astype(out_ref.dtype)
            at += count

    made = call(body, "halve", ids, tuple(ins), in_specs, tuple(outs), out_specs, (steps,))
    for s, value in zip(sums, made):
        if s.bit is None:
            s.result = value
        else:
            s.got = swap(value, s.bit)
    return made


def after(values, running):
    running = [r for r in running if not r.ready]
    values, got = lax.optimization_barrier((values, [r.got for r in running]))
    for r, g in zip(running, got):
        r.got = g
        r.advance()
    return values


def gathered_rows(ids, refs, order, part, low, high):
    mine = position(order, ids[3], ids[0])
    count = refs[0].shape[0]
    flipped = ids[2] == 1
    blocks = []
    for pair in range(count):
        at = position(order, 2 * pair, part) ^ mine
        late = at >= count
        at = at % count
        held, last, early, other = [ref[at, low:high] for ref in refs]
        a, b = jnp.where(late, last, held), jnp.where(late, other, early)
        blocks += [jnp.where(flipped, b, a), jnp.where(flipped, a, b)]
    return blocks


def make_qkv(ids, rows, gots, gain, gathered, height):
    parts, local_rows, width = rows.shape
    length = parts * local_rows
    fsdp = width // height
    half = width // parts
    per = local_rows // TILE

    def body(ids, rows_ref, gain_ref, *refs):
        qkv_ref, xt_ref, x_ref, w_ref, wo_ref, blocks_ref = refs[-6:]
        step = pl.program_id(0)

        @pl.when(step == 0)
        def _():
            for t in range(parts):
                pieces = []
                for c in range(3):
                    args = (ids, refs[4 * c : 4 * c + 4], gathered[c].order, t)
                    w_ref[c, t] = jnp.concatenate(gathered_rows(*args, 0, height), axis=0)
                    pieces.append(gathered_rows(*args, height, height + O_ROWS[c]))
                blocks = [block for of_one in zip(*pieces) for block in of_one]
                wo_ref[t] = jnp.concatenate(blocks, axis=0)

        @pl.when(step // per == ids[0])
        def _():
            x_ref[...] = rows_ref[0]

        for k in range(per):

            @pl.when((step // per != ids[0]) & (step % per == k))
            def _(k=k):
                x_ref[...] = refs[12 + k][...]

        values = x_ref[...].astype(F32)
        xn = (values * rms_scale(values) * gain_ref[...]).astype(BF)
        for c in range(3):
            for t in range(parts):
                made = dot_f32(xn, w_ref[c, t], 1, 0)
                if c == 0:
                    made = made * HEAD_DIM ** (-0.5)
                qkv_ref[c, :, t * half : (t + 1) * half] = made.astype(BF)
        store_transposed(ids, xn, blocks_ref, xt_ref)

    weights = [a for g in gathered for a in g.arrays]
    return call(
        body,
        "qkv",
        ids,
        (rows, gain, *weights, *gots),
        [
            pl.BlockSpec((1, TILE, width), lambda r, ids: (ids[0], r % per, 0)),
            whole((1, width)),
        ]
        + [whole(a.shape) for a in (*weights, *gots)],
        (
            shape((3, length, width), BF),
            shape((fsdp, height, length), BF),
            shape((length, width), BF),
            shape((3, parts, width, half), BF),
            shape((parts, width, half), BF),
        ),
        [
            pl.BlockSpec((3, TILE, width), lambda r, ids: (0, r, 0)),
            pl.BlockSpec((fsdp, height, TILE), lambda r, ids: (0, 0, r)),
            pl.BlockSpec((TILE, width), lambda r, ids: (r, 0)),
            whole((3, parts, width, half)),
            whole((parts, width, half)),
        ],
        (length // TILE,),
        (pltpu.VMEM((fsdp, height, TILE), BF),),
    )


def store_natural(value, out_ref):
    height = out_ref.shape[-2]
    step = 128 // height
    for c in range(value.shape[1] // 128):
        part = value[:, c * 128 : (c + 1) * 128]
        out_ref[c * step : (c + 1) * step] = part.T.reshape(step, height, part.shape[0])


def join_rows(ids, rows, got):
    parts, local_rows, width = rows.shape
    length = parts * local_rows

    def body(ids, rows_ref, got_ref, out_ref):
        mine = pl.multiple_of(ids[0] * local_rows, local_rows)
        out_ref[0, pl.ds(mine, local_rows)] = rows_ref[0]
        rest = pl.multiple_of((1 - ids[0]) * local_rows, local_rows)
        out_ref[0, pl.ds(rest, local_rows)] = got_ref[0]

    spec = pl.BlockSpec((1, local_rows, width), lambda s, ids: (s ^ ids[0], 0, 0))
    return call(
        body,
        "join_rows",
        ids,
        (rows, got),
        [spec, spec],
        (shape((parts, length, width), BF),),
        [pl.BlockSpec((1, length, width), lambda s, ids: (s, 0, 0))],
        (parts,),
    )[0]


def lane_mask(values, head):
    lanes = lax.broadcasted_iota(jnp.int32, values.shape, 1)
    return jnp.where(lanes // HEAD_DIM == head, values, jnp.zeros_like(values))


def attend(ids, qkv):
    length, width = qkv.shape[1:]
    tiles = length // TILE
    pair = 2 * HEAD_DIM
    heads = width // HEAD_DIM

    def body(ids, q_ref, k_ref, v_ref, *refs):
        o_ref, ot_ref, e_ref, inv_ref, bias_ref, s_ref = refs[-6:]

        @pl.when(pl.program_id(0) == 0)
        def _():
            for i in range(tiles):
                keys = i * TILE + lax.broadcasted_iota(jnp.int32, (2 * TILE, TILE), 0)
                rows = i * TILE + lax.broadcasted_iota(jnp.int32, (2 * TILE, TILE), 1)
                seen = keys <= rows
                for p in range(3):
                    start = ids[4 + p]
                    inside = (keys >= start) & (keys < start + PIECE)
                    inside &= (rows >= start) & (rows < start + PIECE)
                    seen |= inside
                bias_ref[i] = jnp.where(seen, 0.0, masked_score)

        k = k_ref[0]
        vt = v_ref[0].T
        slots = s_ref.shape[0]
        todo = [(i, head) for i in range(tiles) for head in range(2)]
        state = {}

        def score(n):
            i, head = todo[n]
            q_head = lane_mask(q_ref[0, i * TILE : (i + 1) * TILE], head)
            top = None
            for j in range(min(i + 2, tiles)):
                s = dot_f32(k[j * TILE : (j + 1) * TILE], q_head, 1, 1)
                if j >= i:
                    s = s + bias_ref[i, (j - i) * TILE : (j - i + 1) * TILE]
                s_ref[n % slots, j] = s
                now = jnp.max(s.reshape(TILE // 8, 8, TILE), axis=0)
                top = now if top is None else jnp.maximum(top, now)
            state[n] = jnp.max(top, axis=0, keepdims=True)

        def soften(n):
            i, head = todo[n]
            total = None
            for j in range(min(i + 2, tiles)):
                e = jnp.exp(s_ref[n % slots, j] - state[n])
                now = jnp.sum(e.reshape(TILE // 8, 8, TILE), axis=0)
                total = now if total is None else total + now
                e_ref[head, j * TILE : (j + 1) * TILE, i * TILE : (i + 1) * TILE] = e.astype(BF)
            state[n] = 1.0 / jnp.sum(total, axis=0, keepdims=True)
            inv_ref[0, head : head + 1, i * TILE : (i + 1) * TILE] = state[n]

        def gather_values(n):
            i, head = todo[n]
            used = min(i + 2, tiles) * TILE
            out = dot_f32(
                vt[head * HEAD_DIM : (head + 1) * HEAD_DIM, :used],
                e_ref[head, :used, i * TILE : (i + 1) * TILE],
                1,
                0,
            )
            state[n] = out * state[n]
            if head == 1:
                both = jnp.concatenate([state[n - 1], state[n]], axis=0)
                ot_ref[:, i * TILE : (i + 1) * TILE] = both.astype(BF)
                o_ref[i * TILE : (i + 1) * TILE] = both.T.astype(BF)

        for n in range(len(todo) + 2):
            if n < len(todo):
                score(n)
            if 1 <= n <= len(todo):
                soften(n - 1)
            if n >= 2:
                gather_values(n - 2)

    spec = [
        pl.BlockSpec((1, length, pair), lambda p, ids, c=c: (c, 0, p)) for c in range(3)
    ]
    return call(
        body,
        "attend",
        ids,
        (qkv, qkv, qkv),
        spec,
        (
            shape((length, width), BF),
            shape((width, length), BF),
            shape((heads, length, length), BF),
            shape((heads // 2, 2, length), F32),
        ),
        [
            pl.BlockSpec((length, pair), lambda p, ids: (0, p)),
            pl.BlockSpec((pair, length), lambda p, ids: (p, 0)),
            pl.BlockSpec((2, length, length), lambda p, ids: (p, 0, 0)),
            pl.BlockSpec((1, 2, length), lambda p, ids: (p, 0, 0)),
        ],
        (heads // 2,),
        (
            pltpu.VMEM((tiles, 2 * TILE, TILE), F32),
            pltpu.VMEM((4, tiles, TILE, TILE), F32),
        ),
    )


def attend_back(ids, qkv, d_heads, saved):
    length, width = qkv.shape[1:]
    tiles = length // TILE
    pair = 2 * HEAD_DIM
    heads = width // HEAD_DIM

    def body(ids, q_ref, k_ref, v_ref, d_ref, ot_ref, e_ref, inv_ref, *refs):
        out_ref, ds_ref, dq_ref = refs[-3:]
        k = k_ref[0]
        v = v_ref[0]
        kt = k.T
        dt = d_ref[...].astype(F32).T
        q_heads = []
        d_scaled = []
        deltas = []
        for head in range(2):
            span = slice(head * HEAD_DIM, (head + 1) * HEAD_DIM)
            inv_row = inv_ref[0, head : head + 1]
            mine = dt[span] * inv_row
            deltas.append(jnp.sum(mine * ot_ref[span].astype(F32), axis=0, keepdims=True))
            blank = jnp.zeros((HEAD_DIM, length), BF)
            mine = mine.astype(BF)
            d_scaled.append(
                jnp.concatenate([mine, blank] if head == 0 else [blank, mine], axis=0)
            )
            q_heads.append(lane_mask(q_ref[0], head))
        dq_ref[...] = jnp.zeros_like(dq_ref)
        sums = {}

        def scores_back(j, head):
            keys = slice(j * TILE, (j + 1) * TILE)
            for r in range(max(j - 1, 0) * TILE, length, TILE):
                cols = slice(r, r + TILE)
                dp = dot_f32(v[keys], d_scaled[head][:, cols], 1, 0)
                weights = e_ref[head, keys, cols].astype(F32)
                ds_ref[j % 2, head, :, cols] = (weights * (dp - deltas[head][:, cols])).astype(BF)

        def operands_back(j, head):
            keys = slice(j * TILE, (j + 1) * TILE)
            rows = slice(head * HEAD_DIM, (head + 1) * HEAD_DIM)
            first = max(j - 1, 0) * TILE
            ds = ds_ref[j % 2, head, :, first:length]
            d_key = dot_f32(ds, q_heads[head][first:length], 1, 0)
            d_value = dot_f32(
                e_ref[head, keys, first:length], d_scaled[head][:, first:length], 1, 1
            )
            dq_ref[rows, first:length] += dot_f32(kt[rows, keys], ds, 1, 0)
            if head == 0:
                sums[j] = (d_key, d_value)
            else:
                out_ref[1, keys] = (sums[j][0] + d_key).astype(BF)
                out_ref[2, keys] = (sums[j][1] + d_value).astype(BF)

        todo = [(j, head) for j in range(tiles) for head in range(2)]
        for n in range(len(todo) + 1):
            if n < len(todo):
                scores_back(*todo[n])
            if n >= 1:
                operands_back(*todo[n - 1])
        out_ref[0] = (dq_ref[...] * HEAD_DIM ** (-0.5)).T.astype(BF)

    spec = [
        pl.BlockSpec((1, length, pair), lambda p, ids, c=c: (c, 0, p)) for c in range(3)
    ]
    return call(
        body,
        "attend_back",
        ids,
        (qkv, qkv, qkv, d_heads, *saved),
        spec
        + [
            pl.BlockSpec((length, pair), lambda p, ids: (0, p)),
            pl.BlockSpec((pair, length), lambda p, ids: (p, 0)),
            pl.BlockSpec((2, length, length), lambda p, ids: (p, 0, 0)),
            pl.BlockSpec((1, 2, length), lambda p, ids: (p, 0, 0)),
        ],
        (shape((3, length, width), BF),),
        [pl.BlockSpec((3, length, pair), lambda p, ids: (0, 0, p))],
        (heads // 2,),
        (pltpu.VMEM((2, 2, TILE, length), BF), pltpu.VMEM((pair, length), F32)),
    )[0]


def out_project(ids, attended, w_out, x, gain):
    length, width = x.shape
    parts, _, half = w_out.shape

    def body(ids, a_ref, w_ref, x_ref, gain_ref, hidden_ref, hn_ref):
        total = x_ref[...].astype(F32)
        for t in range(parts):
            total += dot_f32(a_ref[:, t * half : (t + 1) * half], w_ref[t], 1, 1)
        hidden_ref[...] = total
        hn_ref[...] = (total * rms_scale(total) * gain_ref[...]).astype(BF)

    tile = pl.BlockSpec((TILE, width), lambda r, ids: (r, 0))
    return call(
        body,
        "out_project",
        ids,
        (attended, w_out, x, gain),
        [tile, whole(w_out.shape), tile, whole((1, width))],
        (shape((length, width), F32), shape((length, width), BF)),
        [tile, tile],
        (length // TILE,),
    )


def feed_forward(ids, hn, grads, which, packed):
    length, width = hn.shape
    fsdp, rows, units = packed.shape
    height = rows // 3
    tile = 256
    steps = units // tile
    columns = width // steps

    def body(ids, hn_ref, g_ref, w_ref, out_ref, ht_ref, gt_ref):
        first = pl.multiple_of(pl.program_id(0) * columns, columns)
        store_natural(hn_ref[:, pl.ds(first, columns)], ht_ref)
        store_natural(g_ref[0, :, pl.ds(first, columns)], gt_ref)
        w_gate, w_up, w_down = [
            w_ref[:, c * height : (c + 1) * height].reshape(width, tile) for c in range(3)
        ]
        for r in range(0, length, TILE):
            rows = hn_ref[r : r + TILE]
            gate = dot_f32(rows, w_gate, 1, 0)
            up = dot_f32(rows, w_up, 1, 0)
            d_mixed = dot_f32(g_ref[0, r : r + TILE], w_down, 1, 0)
            sig = jax.nn.sigmoid(gate)
            act = gate * sig
            out_ref[0, r : r + TILE] = (
                d_mixed * up * sig * (1.0 + gate * (1.0 - sig))
            ).astype(BF)
            out_ref[1, r : r + TILE] = (d_mixed * act).astype(BF)
            out_ref[2, r : r + TILE] = (act * up).astype(BF)

    return call(
        body,
        "feed_forward",
        ids,
        (hn, grads, packed),
        [
            whole((length, width)),
            pl.BlockSpec((1, length, width), lambda n, ids: (which, 0, 0)),
            pl.BlockSpec((fsdp, rows, tile), lambda n, ids: (0, 0, n)),
        ],
        (
            shape((3, length, units), BF),
            shape((fsdp, height, length), BF),
            shape((fsdp, height, length), BF),
        ),
        [
            pl.BlockSpec((3, length, tile), lambda n, ids: (0, 0, n)),
            pl.BlockSpec((columns // height, height, length), lambda n, ids: (n, 0, 0)),
            pl.BlockSpec((columns // height, height, length), lambda n, ids: (n, 0, 0)),
        ],
        (steps,),
    )


def feed_forward_out(ids, own, theirs, packed, hidden):
    length, width = hidden.shape
    fsdp, rows, units = packed.shape
    height = rows // 3
    kept = length // 2
    per = kept // TILE

    def body(ids, own_ref, theirs_ref, w_ref, hidden_ref, keep_ref, send_ref):
        w = w_ref[...].reshape(width, units)
        mine = pl.program_id(0) == 0
        keeps = pl.program_id(1) >= per

        @pl.when(mine & keeps)
        def _():
            keep_ref[0] = hidden_ref[...] + dot_f32(own_ref[0], w, 1, 1)

        @pl.when(mine & ~keeps)
        def _():
            send_ref[0] = (hidden_ref[...] + dot_f32(own_ref[0], w, 1, 1)).astype(BF)

        @pl.when(~mine & keeps)
        def _():
            keep_ref[0] = dot_f32(theirs_ref[0], w, 1, 1)

        @pl.when(~mine & ~keeps)
        def _():
            send_ref[0] = dot_f32(theirs_ref[0], w, 1, 1).astype(BF)

    def row(j, ids):
        return jnp.where(j < per, (1 - ids[0]) * per + j, ids[0] * per + j - per)

    return call(
        body,
        "feed_forward_out",
        ids,
        (own, theirs, packed, hidden),
        [
            pl.BlockSpec(
                (1, TILE, units),
                lambda s, j, ids: (2, row(jnp.where(s == 0, j, 2 * per - 1), ids), 0),
            ),
            pl.BlockSpec(
                (1, TILE, units), lambda s, j, ids: (2, row(jnp.where(s == 1, j, 0), ids), 0)
            ),
            pl.BlockSpec((fsdp, height, units), lambda s, j, ids: (0, 2, 0)),
            pl.BlockSpec(
                (TILE, width), lambda s, j, ids: (row(jnp.where(s == 0, j, 2 * per - 1), ids), 0)
            ),
        ],
        (shape((2, kept, width), F32), shape((2, kept, width), BF)),
        [
            pl.BlockSpec(
                (1, TILE, width), lambda s, j, ids: (s ^ ids[0], jnp.maximum(j - per, 0), 0)
            ),
            pl.BlockSpec(
                (1, TILE, width), lambda s, j, ids: (s ^ ids[0], jnp.minimum(j, per - 1), 0)
            ),
        ],
        (2, 2 * per),
    )


def feed_forward_grads(ids, hn_t, hn_t_theirs, grads_t, grads_t_theirs, own, theirs):
    fsdp, height, length = hn_t.shape
    units = own.shape[2]
    per = units // UNITS

    def body(ids, h_ref, h2_ref, g_ref, g2_ref, own_ref, theirs_ref, out_ref):
        def make(a_ref, b_ref):
            for f in range(0, fsdp, 4):
                a = a_ref[f : f + 4].reshape(4 * height, length)
                b = b_ref[f : f + 4].reshape(4 * height, length)
                made = dot_f32(a, own_ref[0], 1, 0) + dot_f32(b, theirs_ref[0], 1, 0)
                out_ref[f : f + 4] = made.astype(BF).reshape(4, height, UNITS)

        pl.when(pl.program_id(0) < 2)(lambda: make(h_ref, h2_ref))
        pl.when(pl.program_id(0) == 2)(lambda: make(g_ref, g2_ref))

    side = pl.BlockSpec((1, length, UNITS), lambda c, n, ids: (c, 0, n))
    return call(
        body,
        "feed_forward_grads",
        ids,
        (hn_t, hn_t_theirs, grads_t, grads_t_theirs, own, theirs),
        [whole(hn_t.shape)] * 4 + [side, side],
        (shape((fsdp, 3 * height, units), BF),),
        [pl.BlockSpec((fsdp, height, UNITS), lambda c, n, ids: (0, c, n))],
        (3, per),
    )[0]


def weight_grad(ids, name, sources):
    fsdp, height, length = sources[0][0].shape
    parts = 2
    half = sources[0][1].shape[2] // parts
    tile = min(UNITS, half)
    per = half // tile
    hop = fsdp // 2

    def body(ids, *refs):
        outs = refs[-2:]
        for k in range(len(sources)):
            l_ref, r_ref = refs[2 * k : 2 * k + 2]

            @pl.when(pl.program_id(0) == k)
            def _(l_ref=l_ref, r_ref=r_ref):
                right_tile = r_ref[0]
                for b in range(0, fsdp, 4):
                    block = l_ref[b : b + 4].reshape(4 * height, length)
                    made = dot_f32(block, right_tile, 1, 0).astype(BF)
                    outs[b // hop][0, b % hop : b % hop + 4] = made.reshape(4, height, tile)

    ins, specs = [], []
    for k, (left, right, index) in enumerate(sources):
        ins += [left, right]

        def columns(c, t, n, ids, k=k, index=index):
            at = n * parts + t
            at = jnp.where(c == k, at, 0 if k else half * parts // tile - 1)
            return (index, 0, at)

        specs += [whole(left.shape), pl.BlockSpec((1, length, tile), columns)]
    spec = pl.BlockSpec((1, hop, height, tile), lambda c, t, n, ids: (t ^ ids[0], 0, c, n))
    return call(
        body,
        name,
        ids,
        tuple(ins),
        specs,
        (shape((parts, hop, len(sources) * height, half), BF),) * 2,
        [spec, spec],
        (len(sources), parts, per),
    )


def feed_forward_back(ids, stacked, packed, half=None):
    length = stacked.shape[1] if half is None else stacked.shape[1] // 2
    at = half or 0
    fsdp, rows, units = packed.shape
    height = rows // 3
    width = fsdp * height
    per = units // UNITS

    def body(ids, d_ref, w_ref, *refs):
        acc_ref = refs[-1]

        @pl.when(pl.program_id(0) == 0)
        def _():
            acc_ref[...] = jnp.zeros_like(acc_ref)

        w_gate, w_up = [
            w_ref[:, c * height : (c + 1) * height].reshape(width, UNITS) for c in range(2)
        ]
        for r in range(0, length, TILE):
            acc_ref[r : r + TILE] += dot_f32(d_ref[0, r : r + TILE], w_gate, 1, 1) + dot_f32(
                d_ref[1, r : r + TILE], w_up, 1, 1
            )

        @pl.when(pl.program_id(0) == per - 1)
        def _():
            refs[0][...] = acc_ref[...].astype(refs[0].dtype)

    return call(
        body,
        "feed_forward_back",
        ids,
        (stacked, packed),
        [
            pl.BlockSpec((2, length, UNITS), lambda n, ids: (0, at, n)),
            pl.BlockSpec((fsdp, 2 * height, UNITS), lambda n, ids: (0, 0, n)),
        ],
        (shape((length, width), F32 if half is None else BF),),
        [whole((length, width))],
        (per,),
        (pltpu.VMEM((length, width), F32),),
    )[0]


def norm_and_project_back(ids, share, gots, hidden, grads, gain, w_out):
    length, width = hidden.shape
    parts, _, half = w_out.shape
    fsdp = lax.axis_size("fsdp")
    height = width // fsdp
    cut = gots[0].shape[0] // TILE

    def body(ids, share_ref, got_ref, tail_ref, hidden_ref, g_ref, gain_ref, w_ref, *refs):
        dh_ref, lt_ref, out_ref, blocks_ref, got_scr = refs

        @pl.when(pl.program_id(0) < cut)
        def _():
            got_scr[...] = got_ref[...]

        @pl.when(pl.program_id(0) >= cut)
        def _():
            got_scr[...] = tail_ref[...]

        rows = hidden_ref[...]
        scale = rms_scale(rows)
        normed = rows * scale
        d_normed = share_ref[...] + got_scr[...].astype(F32)
        dh = g_ref[0].astype(F32) + norm_backward_pass(d_normed, normed, scale, gain_ref[...])
        dh_ref[...] = dh
        low = dh.astype(BF)
        for t in range(parts):
            out_ref[:, t * half : (t + 1) * half] = dot_f32(low, w_ref[t], 1, 0).astype(BF)
        store_transposed(ids, low, blocks_ref, lt_ref)

    tile = pl.BlockSpec((TILE, width), lambda r, ids: (r, 0))
    return call(
        body,
        "norm_and_project_back",
        ids,
        (share, *gots, hidden, grads, gain, w_out),
        [
            tile,
            pl.BlockSpec((TILE, width), lambda r, ids: (jnp.minimum(r, cut - 1), 0)),
            pl.BlockSpec((TILE, width), lambda r, ids: (jnp.maximum(r - cut, 0), 0)),
            tile,
            pl.BlockSpec((1, TILE, width), lambda r, ids: (0, r, 0)),
            whole((1, width)),
            whole(w_out.shape),
        ],
        (
            shape((length, width), F32),
            shape((fsdp, height, length), BF),
            shape((length, width), BF),
        ),
        [tile, pl.BlockSpec((fsdp, height, TILE), lambda r, ids: (0, 0, r)), tile],
        (length // TILE,),
        (pltpu.VMEM((fsdp, height, TILE), BF), pltpu.VMEM((TILE, width), BF)),
    )


def store_lines(out_ref, values):
    lines = values.shape[1] // 128
    for n in range(lines):
        out_ref[0, pl.ds(n, values.shape[0], stride=lines)] = values[:, n * 128 : (n + 1) * 128]


def qkv_back(ids, d_qkv, weights, x, dh, gain, sent):
    length, width = x.shape
    parts, _, half = weights.shape[1:]
    kept = length // parts
    per = kept // TILE

    def body(ids, d_ref, w_ref, x_ref, dh_ref, gain_ref, out_ref, acc_ref):
        d_normed = None
        for c in range(3):
            for t in range(parts):
                part = dot_f32(d_ref[c, :, t * half : (t + 1) * half], w_ref[c, t], 1, 1)
                d_normed = part if d_normed is None else d_normed + part
        rows = x_ref[...].astype(F32)
        scale = rms_scale(rows)
        made = dh_ref[...] + norm_backward_pass(d_normed, rows * scale, scale, gain_ref[...])
        if sent:
            out_ref[...] = made.astype(BF)
        else:
            acc_ref[...] = made
            store_lines(out_ref, acc_ref)

    def rows(r, ids):
        return per * (1 - ids[0] if sent else ids[0]) + r

    lines = kept * width // 128
    return call(
        body,
        "qkv_back",
        ids,
        (d_qkv, weights, x, dh, gain),
        [
            pl.BlockSpec((3, TILE, width), lambda r, ids: (0, rows(r, ids), 0)),
            whole(weights.shape),
            pl.BlockSpec((TILE, width), lambda r, ids: (rows(r, ids), 0)),
            pl.BlockSpec((TILE, width), lambda r, ids: (rows(r, ids), 0)),
            whole((1, width)),
        ],
        (shape((kept, width), BF) if sent else shape((parts, lines, 128), F32),),
        [
            pl.BlockSpec((TILE, width), lambda r, ids: (r, 0))
            if sent
            else pl.BlockSpec((1, lines // per, 128), lambda r, ids: (ids[0], r, 0)),
        ],
        (per,),
        (pltpu.VMEM((TILE, width), F32),),
    )[0]


def place_rows(ids, got, lines):
    kept, width = got.shape

    def body(ids, got_ref, _, out_ref, wide_ref):
        wide_ref[...] = got_ref[...].astype(F32)
        store_lines(out_ref, wide_ref)

    return call(
        body,
        "place_rows",
        ids,
        (got, lines),
        [whole((kept, width)), IN_PLACE],
        (shape(lines.shape, F32),),
        [pl.BlockSpec((1,) + lines.shape[1:], lambda g, ids: (1 - ids[0], 0, 0))],
        (1,),
        (pltpu.VMEM((kept, width), F32),),
        aliases={2: 0},
    )[0]


def three_parts(values):
    high = values.astype(BF)
    rest = values - high.astype(F32)
    middle = rest.astype(BF)
    return jnp.stack([high, middle, (rest - middle.astype(F32)).astype(BF)], -1)


def local_sequence(
    tokens, piece_starts, gain_attn, w_qkv, w_out, gain_mlp, w_gate_up, w_down, out_grad
):
    fsdp = lax.axis_size("fsdp")
    parts = lax.axis_size("tensor")
    me_f = lax.axis_index("fsdp")
    me_t = lax.axis_index("tensor")
    local_rows = tokens.shape[1]
    height = w_qkv.shape[1]
    half = w_qkv.shape[2]
    share = gain_attn.shape[0]

    starts = lax.dynamic_index_in_dim(piece_starts, me_t, 0, keepdims=False)[0]
    ids = jnp.stack([me_t, me_f // 2, me_f % 2, me_f]).astype(jnp.int32)
    ids = jnp.concatenate([ids, starts])
    rows_in = tokens.reshape(parts, local_rows, D)
    grads_in = out_grad.reshape(parts, local_rows, D)

    def other(rows):
        return lax.dynamic_index_in_dim(rows, 1 - me_t, 0, keepdims=False)

    o_mine = jnp.split(w_out.T, (O_ROWS[0], O_ROWS[0] + O_ROWS[1]))
    wk = Gathered(jnp.concatenate([w_qkv[1], o_mine[1]]), (TENSOR, Z_FAR, X, Z_NEAR))
    wv = Gathered(jnp.concatenate([w_qkv[2], o_mine[2]]), (TENSOR, Z_NEAR, Z_FAR, X))
    gains = three_parts(jnp.stack([gain_attn, gain_mlp])).reshape(1, -1)
    gains = jnp.pad(gains, ((0, 7), (0, half - gains.shape[1])))
    wq = Gathered(
        jnp.concatenate([w_qkv[0], o_mine[0], gains]), (Z_FAR, X, Z_NEAR, TENSOR)
    )
    ff_mine = jnp.concatenate([w_gate_up.reshape(2 * height, -1), w_down.T])
    aways = jnp.split(other(rows_in), 2)
    three = [wq, wk, wv]
    aways[0] = after(aways[0], three)
    got_one = swap(aways[0], TENSOR)
    got_one, aways[1] = after((got_one, aways[1]), three)
    got_two = swap(aways[1], TENSOR)
    got_two = after(got_two, three)
    ff_mine = after(ff_mine, three)
    packed = lax.all_gather(ff_mine, "fsdp", axis=0, tiled=False)
    got_rows = after((got_one, got_two), three)

    each = jnp.arange(fsdp * parts)
    each_f, each_t = each // parts, each % parts
    at = position(wq.order, each_f, each_t) ^ position(wq.order, me_f, me_t)
    at = at + fsdp * ((each_f ^ me_f) % 2)
    row = height + O_ROWS[0]
    gains = jnp.concatenate([a[:, row, : 6 * share] for a in wq.arrays])[at]
    gains = jnp.sum(gains.reshape(fsdp * parts, 2, share, 3).astype(F32), axis=3)
    gain_one, gain_two = [gains[:, i].reshape(1, D) for i in range(2)]

    qkv, xt, x, w_all, wo_all = make_qkv(ids, rows_in, got_rows, gain_one, three, height)
    _, away = lax.optimization_barrier((got_rows, grads_in))
    got_grads = swap(away, TENSOR)
    attended, *saved = attend(ids, qkv)
    hidden, hn = out_project(ids, attended, wo_all, x, gain_two)
    hn_theirs = swap(hn, TENSOR)
    grads = join_rows(ids, grads_in, got_grads)
    hn, grads, packed = lax.optimization_barrier((hn, grads, packed))

    own, ht, gt = feed_forward(ids, hn, grads, 0, packed)
    own, hn_theirs = lax.optimization_barrier((own, hn_theirs))
    theirs, ht_theirs, gt_theirs = feed_forward(ids, hn_theirs, grads, 1, packed)
    d_one = feed_forward_back(ids, theirs, packed, 0)
    d_one, theirs, own = lax.optimization_barrier((d_one, theirs, own))
    got_one = swap(d_one, TENSOR)
    made = feed_forward_grads(ids, ht, ht_theirs, gt, gt_theirs, own, theirs)
    made, own, theirs, got_one = lax.optimization_barrier((made, own, theirs, got_one))
    summed = lax.psum_scatter(made, "fsdp", scatter_dimension=0, tiled=False)
    d_two = feed_forward_back(ids, theirs, packed, 1)
    d_two, own, theirs = lax.optimization_barrier((d_two, own, theirs))
    got_two = swap(d_two, TENSOR)
    share_own = feed_forward_back(ids, own, packed)
    share_own, own, theirs = lax.optimization_barrier((share_own, own, theirs))
    keep_out, send_out = feed_forward_out(ids, own, theirs, packed, hidden)
    share_own, got_two, send_out = lax.optimization_barrier((share_own, got_two, send_out))
    dh, dt, d_attended = norm_and_project_back(
        ids, share_own, (got_one, got_two), hidden, grads, gain_two, wo_all
    )

    def join(values, sums):
        values, gots = lax.optimization_barrier((values, [s.got for s in sums]))
        for s, g in zip(sums, gots):
            s.got = g
        made = halve(ids, sums)
        return lax.optimization_barrier((values, made))[0]

    o_sum = weight_grad(ids, "grad_out", [(dt, attended[None], 0)])
    o_sum, d_attended, send_out = lax.optimization_barrier((o_sum, d_attended, send_out))
    o_sum = Summed(*o_sum, (X, Z_NEAR, TENSOR, Z_FAR))
    got_out = swap(send_out, TENSOR)
    d_qkv = attend_back(ids, qkv, d_attended, saved)

    d_qkv = join(d_qkv, [o_sum])

    orders = (
        (X, Z_NEAR, TENSOR, Z_FAR),
        (Z_NEAR, X, Z_FAR, TENSOR),
        (TENSOR, Z_FAR, X, Z_NEAR),
    )
    sums = []
    for c, order in enumerate(orders):
        made = weight_grad(ids, "grad_qkv", [(xt, d_qkv, c)])
        made, d_qkv = lax.optimization_barrier((made, d_qkv))
        sums.append(Summed(*made, order))
    d_qkv = join(d_qkv, sums)
    sums.append(o_sum)
    sent = qkv_back(ids, d_qkv, w_all, x, dh, gain_one, True)
    sent, d_qkv, got_out = join((sent, d_qkv, got_out), sums)
    layer_out = (keep_out + got_out.astype(F32)).astype(BF).reshape(tokens.shape)
    got_grad = swap(sent, TENSOR)
    lines = qkv_back(ids, d_qkv, w_all, x, dh, gain_one, False)
    lines, summed = join((lines, summed), sums)
    halve(ids, sums)
    lines, got_grad = lax.optimization_barrier((lines, got_grad))
    input_grad = join(place_rows(ids, got_grad, lines), sums).reshape(tokens.shape)
    qkv_grad = jnp.stack([s.result for s in sums[:3]])
    summed = summed.astype(F32)
    gate_up_grad = summed[: 2 * height].reshape(w_gate_up.shape)
    from_qkv = jnp.sum(w_qkv.astype(F32) * qkv_grad, axis=(0, 2))
    from_gate_up = jnp.sum(w_gate_up.astype(F32) * gate_up_grad, axis=(0, 2))
    both = jnp.stack([from_qkv, from_gate_up]).reshape(2, parts, share)
    mine = lax.dynamic_index_in_dim(both, me_t, 1, keepdims=False)
    theirs = lax.dynamic_index_in_dim(both, 1 - me_t, 1, keepdims=False)
    mine = mine + swap(theirs, TENSOR)
    return (
        layer_out,
        input_grad,
        mine[0] / gain_attn,
        qkv_grad,
        o_sum.result.T,
        mine[1] / gain_mlp,
        gate_up_grad,
        summed[2 * height :].T,
    )


def local_any(tokens, *rest):
    sizes = (lax.axis_size("tensor"), tokens.shape[0], tokens.shape[2], lax.axis_size("fsdp"))
    if sizes == (2, 2, 1, 16):
        return local_sequence(tokens, *rest)
    return local(tokens, *rest)


def solution(mesh):
    return jax.shard_map(
        local_any,
        mesh=mesh,
        in_specs=(
            P(None, "tensor", "fsdp", None),
            P(None, "fsdp", None),
            P(("fsdp", "tensor")),
            P(None, "fsdp", "tensor"),
            P("tensor", "fsdp"),
            P(("fsdp", "tensor")),
            P(None, "fsdp", "tensor"),
            P("tensor", "fsdp"),
            P(None, "tensor", "fsdp", None),
        ),
        out_specs=(
            P(None, "tensor", "fsdp", None),
            P(None, "tensor", "fsdp", None),
            P(("fsdp", "tensor")),
            P(None, "fsdp", "tensor"),
            P("tensor", "fsdp"),
            P(("fsdp", "tensor")),
            P(None, "fsdp", "tensor"),
            P("tensor", "fsdp"),
        ),
        check_vma=False,
    )
```

```python
import itertools

import jax
import jax.numpy as jnp
from jax import lax
from jax.experimental import pallas as pl
from jax.experimental.pallas import tpu as pltpu
from jax.sharding import PartitionSpec as P

D = 1024
HEAD_DIM = 64
QBLOCK = 512
PIECE = 256


norm_eps = 1e-05
masked_score = -1e30


def rms_scale(values_float_rows):
    return lax.rsqrt(
        jnp.mean(values_float_rows * values_float_rows, axis=-1, keepdims=True) + norm_eps
    )


def norm_backward_pass(d_normed, normed_pre, scale_rows, gain_vector_row):
    d_scaled = d_normed * gain_vector_row
    return scale_rows * (
        d_scaled - normed_pre * jnp.mean(d_scaled * normed_pre, axis=-1, keepdims=True)
    )


def piece_index_labels(starts_row, length):
    positions = jnp.arange(length, dtype=jnp.int32)[:, None]
    inside = (positions >= starts_row[None, :]) & (positions < starts_row[None, :] + PIECE)
    numbers = jnp.arange(1, starts_row.shape[0] + 1, dtype=jnp.int32)
    return jnp.sum(jnp.where(inside, numbers[None, :], 0), axis=1)


def allowed_block(labels, first_row, key_count):
    row_ids = first_row + jnp.arange(QBLOCK, dtype=jnp.int32)
    col_ids = jnp.arange(key_count, dtype=jnp.int32)
    row_labels = labels[first_row : first_row + QBLOCK]
    causal = col_ids[None, :] <= row_ids[:, None]
    same_piece = (row_labels[:, None] == labels[None, :]) & (row_labels[:, None] > 0)
    return causal | same_piece


def attend_forward(queries, keys_all, values_all, labels, key_spans):
    score_scale = HEAD_DIM ** (-0.5)
    outputs = []
    totals = []
    for first_row, key_count in key_spans:
        block_q = queries[first_row : first_row + QBLOCK]
        scores = (
            jnp.einsum("qhd,khd->hqk", block_q, keys_all, preferred_element_type=jnp.float32)
            * score_scale
        )
        scores = jnp.where(allowed_block(labels, first_row, key_count)[None], scores, masked_score)
        row_max = jnp.max(scores, axis=-1, keepdims=True)
        exp_scores = jnp.exp(scores - row_max)
        row_total = jnp.sum(exp_scores, axis=-1, keepdims=True)
        attn_probs = (exp_scores / row_total).astype(jnp.bfloat16)
        block_out = jnp.einsum(
            "hqk,khd->qhd", attn_probs, values_all, preferred_element_type=jnp.float32
        )
        outputs.append(block_out.astype(jnp.bfloat16))
        totals.append((row_max + jnp.log(row_total))[..., 0])
    return (jnp.concatenate(outputs, 0), jnp.concatenate(totals, 1))


def attend_backward(queries, keys_all, values_all, labels, log_total, d_heads, key_spans):
    score_scale = HEAD_DIM ** (-0.5)
    query_parts = []
    d_keys = jnp.zeros(keys_all.shape, jnp.float32)
    d_values = jnp.zeros(values_all.shape, jnp.float32)
    for first_row, key_count in key_spans:
        block_q = queries[first_row : first_row + QBLOCK]
        block_d = d_heads[first_row : first_row + QBLOCK]
        scores = (
            jnp.einsum("qhd,khd->hqk", block_q, keys_all, preferred_element_type=jnp.float32)
            * score_scale
        )
        mask_now = allowed_block(labels, first_row, key_count)[None]
        attn_probs = jnp.where(
            mask_now, jnp.exp(scores - log_total[:, first_row : first_row + QBLOCK, None]), 0.0
        )
        probs_low = attn_probs.astype(jnp.bfloat16)
        d_probs = jnp.einsum(
            "qhd,khd->hqk", block_d, values_all, preferred_element_type=jnp.float32
        )
        row_dot = jnp.sum(attn_probs * d_probs, axis=-1, keepdims=True)
        d_scores = (attn_probs * (d_probs - row_dot)).astype(jnp.bfloat16)
        query_parts.append(
            jnp.einsum("hqk,khd->qhd", d_scores, keys_all, preferred_element_type=jnp.float32)
            * score_scale
        )
        d_keys = d_keys.at[:key_count].add(
            jnp.einsum("hqk,qhd->khd", d_scores, block_q, preferred_element_type=jnp.float32)
            * score_scale
        )
        d_values = d_values.at[:key_count].add(
            jnp.einsum("hqk,qhd->khd", probs_low, block_d, preferred_element_type=jnp.float32)
        )
    return (jnp.concatenate(query_parts, 0), d_keys, d_values)


def attention_forward(qkv_low, labels_all, key_spans):
    length, seq_count, width = (qkv_low.shape[0], qkv_low.shape[1], qkv_low.shape[3])
    per_seq = jnp.moveaxis(qkv_low, 1, 0).reshape(seq_count, length, 3, width // HEAD_DIM, HEAD_DIM)

    def one_seq(seq_items):
        seq_qkv, labels = seq_items
        return attend_forward(seq_qkv[:, 0], seq_qkv[:, 1], seq_qkv[:, 2], labels, key_spans)

    seq_outs, totals = lax.map(one_seq, (per_seq, labels_all))
    return (jnp.moveaxis(seq_outs.reshape(seq_count, length, width), 0, 1), totals)


def attention_backward(qkv_low, labels_all, totals, d_attended, key_spans):
    length, seq_count, width = (qkv_low.shape[0], qkv_low.shape[1], qkv_low.shape[3])
    per_seq = jnp.moveaxis(qkv_low, 1, 0).reshape(seq_count, length, 3, width // HEAD_DIM, HEAD_DIM)
    d_seq = jnp.moveaxis(d_attended, 1, 0).reshape(seq_count, length, width // HEAD_DIM, HEAD_DIM)

    def one_seq(seq_items):
        seq_qkv, labels, log_total, seq_d = seq_items
        d_query, d_keys, d_values = attend_backward(
            seq_qkv[:, 0], seq_qkv[:, 1], seq_qkv[:, 2], labels, log_total, seq_d, key_spans
        )
        return jnp.stack([d_query, d_keys, d_values], 1).astype(jnp.bfloat16)

    seq_grads = lax.map(one_seq, (per_seq, labels_all, totals, d_seq))
    return jnp.moveaxis(seq_grads, 0, 1).reshape(length, seq_count, 3, width)


def fetch_weights(w_qkv, w_out, w_gate_up, w_down):
    qkv_all, out_all, gate_up_all, down_weight_full = (
        lax.all_gather(w_qkv, "fsdp", axis=1, tiled=True),
        lax.all_gather(w_out, "fsdp", axis=1, tiled=True),
        lax.all_gather(w_gate_up, "fsdp", axis=1, tiled=True),
        lax.all_gather(w_down, "fsdp", axis=1, tiled=True),
    )
    return (qkv_all, out_all, gate_up_all, down_weight_full)


def local(tokens, piece_starts, gain_attn, w_qkv, w_out, gain_mlp, w_gate_up, w_down, out_grad):
    both_gains = lax.all_gather(
        jnp.stack([gain_attn, gain_mlp]), ("fsdp", "tensor"), axis=1, tiled=True
    )
    local_rows = tokens.shape[1]
    length = local_rows * lax.axis_size("tensor")
    key_spans = [(first_row, length) for first_row in range(0, length, QBLOCK)]

    def label_row(starts_row):
        return piece_index_labels(starts_row, length)

    labels_every = jax.vmap(jax.vmap(label_row))(piece_starts)
    ff_cols = w_gate_up.shape[2]
    acc_gain = jnp.zeros((2, D), jnp.float32)
    acc_qkv = jnp.zeros((3, D, w_qkv.shape[2]), jnp.float32)
    acc_out = jnp.zeros((w_out.shape[0], D), jnp.float32)
    acc_gate_up = jnp.zeros((2, D, ff_cols), jnp.float32)
    acc_down = jnp.zeros((ff_cols, D), jnp.float32)
    layer_outs = []
    input_grads = []
    for micro_idx in range(tokens.shape[0]):
        weights = fetch_weights(w_qkv, w_out, w_gate_up, w_down)
        qkv_all, out_all, gate_up_all, down_weight_full = weights
        rows_f32 = tokens[micro_idx].astype(jnp.float32)
        scale_attn = rms_scale(rows_f32)
        pre_attn = rows_f32 * scale_attn
        normed = (pre_attn * both_gains[0]).astype(jnp.bfloat16)
        piece_rows = lax.all_gather(normed, "tensor", axis=0, tiled=True)
        made = jnp.einsum("lsd,cde->lsce", piece_rows, qkv_all, preferred_element_type=jnp.float32)
        qkv_low = made.astype(jnp.bfloat16)
        attended, log_total = attention_forward(qkv_low, labels_every[micro_idx], key_spans)
        rows_now = lax.slice_in_dim(attended, 0, local_rows * lax.axis_size("tensor"), axis=0)
        attn_part = lax.psum_scatter(
            jnp.einsum("lsc,cd->lsd", rows_now, out_all, preferred_element_type=jnp.float32).astype(
                jnp.bfloat16
            ),
            "tensor",
            scatter_dimension=0,
            tiled=True,
        ).astype(jnp.float32)
        hidden = rows_f32 + attn_part
        scale_mlp = rms_scale(hidden)
        pre_mlp = hidden * scale_mlp
        normed_mlp = (pre_mlp * both_gains[1]).astype(jnp.bfloat16)
        expand_piece_rows = lax.all_gather(normed_mlp, "tensor", axis=0, tiled=True)
        gate_up = jnp.einsum(
            "lsd,cdf->lscf", expand_piece_rows, gate_up_all, preferred_element_type=jnp.float32
        )
        gate_part = gate_up[:, :, 0]
        up_part = gate_up[:, :, 1]
        sigmoid_gate = jax.nn.sigmoid(gate_part)
        activated = gate_part * sigmoid_gate
        mixed_lowp_rows = (activated * up_part).astype(jnp.bfloat16)
        down_rows_now = lax.slice_in_dim(
            mixed_lowp_rows, 0, local_rows * lax.axis_size("tensor"), axis=0
        )
        mlp_part = lax.psum_scatter(
            jnp.einsum(
                "meg,gp->mep", down_rows_now, down_weight_full, preferred_element_type=jnp.float32
            ).astype(jnp.bfloat16),
            "tensor",
            scatter_dimension=0,
            tiled=True,
        ).astype(jnp.float32)
        layer_outs.append((hidden + mlp_part).astype(jnp.bfloat16))
        qkv_all, out_all, gate_up_all, down_weight_full = fetch_weights(
            w_qkv, w_out, w_gate_up, w_down
        )
        grad_rows = out_grad[micro_idx]
        down_piece_rows = lax.all_gather(grad_rows, "tensor", axis=0, tiled=True)
        d_mixed = jnp.einsum(
            "xum,tm->xut", down_piece_rows, down_weight_full, preferred_element_type=jnp.float32
        )
        acc_down = acc_down + jnp.einsum(
            "zmp,zme->pe", mixed_lowp_rows, down_piece_rows, preferred_element_type=jnp.float32
        )
        d_gate = d_mixed * up_part * sigmoid_gate * (1.0 + gate_part * (1.0 - sigmoid_gate))
        d_up = d_mixed * activated
        d_gate_up = jnp.stack([d_gate, d_up], 2).astype(jnp.bfloat16)
        acc_gate_up = acc_gate_up + jnp.einsum(
            "lsd,lscf->cdf", expand_piece_rows, d_gate_up, preferred_element_type=jnp.float32
        )
        mlp_rows_now = lax.slice_in_dim(d_gate_up, 0, local_rows * lax.axis_size("tensor"), axis=0)
        d_normed_mlp = lax.psum_scatter(
            jnp.einsum(
                "lscf,cdf->lsd", mlp_rows_now, gate_up_all, preferred_element_type=jnp.float32
            ).astype(jnp.bfloat16),
            "tensor",
            scatter_dimension=0,
            tiled=True,
        ).astype(jnp.float32)
        gain_mlp_part = jnp.sum(d_normed_mlp * pre_mlp, axis=(0, 1))
        d_hidden = grad_rows.astype(jnp.float32) + norm_backward_pass(
            d_normed_mlp, pre_mlp, scale_mlp, both_gains[1]
        )
        attention_gradient_lowp = d_hidden.astype(jnp.bfloat16)
        out_piece_rows = lax.all_gather(attention_gradient_lowp, "tensor", axis=0, tiled=True)
        out_made = jnp.einsum(
            "lsd,cd->lsc", out_piece_rows, out_all, preferred_element_type=jnp.float32
        )
        d_attended = out_made.astype(jnp.bfloat16)
        acc_out = acc_out + jnp.einsum(
            "lsc,lsd->cd", attended, out_piece_rows, preferred_element_type=jnp.float32
        )
        d_qkv = attention_backward(
            qkv_low, labels_every[micro_idx], log_total, d_attended, key_spans
        )
        acc_qkv = acc_qkv + jnp.einsum(
            "lsd,lsce->cde", piece_rows, d_qkv, preferred_element_type=jnp.float32
        )
        d_normed = lax.psum_scatter(
            jnp.einsum("lsce,cde->lsd", d_qkv, qkv_all, preferred_element_type=jnp.float32).astype(
                jnp.bfloat16
            ),
            "tensor",
            scatter_dimension=0,
            tiled=True,
        ).astype(jnp.float32)
        gain_attn_part = jnp.sum(d_normed * pre_attn, axis=(0, 1))
        input_grads.append(
            d_hidden + norm_backward_pass(d_normed, pre_attn, scale_attn, both_gains[0])
        )
        acc_gain = acc_gain + jnp.stack([gain_attn_part, gain_mlp_part])
    gain_rows, qkv_rows, out_rows_sum, gate_up_rows, down_rows_sum = (
        lax.psum_scatter(
            acc_gain.astype(jnp.bfloat16), "fsdp", scatter_dimension=1, tiled=True
        ).astype(jnp.float32),
        lax.psum_scatter(
            acc_qkv.astype(jnp.bfloat16), "fsdp", scatter_dimension=1, tiled=True
        ).astype(jnp.float32),
        lax.psum_scatter(
            acc_out.astype(jnp.bfloat16), "fsdp", scatter_dimension=1, tiled=True
        ).astype(jnp.float32),
        lax.psum_scatter(
            acc_gate_up.astype(jnp.bfloat16), "fsdp", scatter_dimension=1, tiled=True
        ).astype(jnp.float32),
        lax.psum_scatter(
            acc_down.astype(jnp.bfloat16), "fsdp", scatter_dimension=1, tiled=True
        ).astype(jnp.float32),
    )
    gain_shares = lax.psum_scatter(gain_rows, "tensor", scatter_dimension=1, tiled=True)
    return (
        jnp.stack(layer_outs, 0),
        jnp.stack(input_grads, 0),
        gain_shares[0],
        qkv_rows,
        out_rows_sum,
        gain_shares[1],
        gate_up_rows,
        down_rows_sum,
    )


BF = jnp.bfloat16
F32 = jnp.float32
TILE = 256
UNITS = 512
O_ROWS = (16, 32, 16)
CORE, TENSOR, X, Z_NEAR, Z_FAR = 1, 0, 2, 4, 8


def dot_f32(a, b, ca, cb):
    return lax.dot_general(a, b, (((ca,), (cb,)), ((), ())), preferred_element_type=F32)


def call(body, name, ids, ins, in_specs, outs, out_specs, grid, scratch=(), aliases=None):
    return pl.pallas_call(
        body,
        name=name,
        out_shape=outs,
        grid_spec=pltpu.PrefetchScalarGridSpec(
            num_scalar_prefetch=1,
            grid=grid,
            in_specs=in_specs,
            out_specs=out_specs,
            scratch_shapes=list(scratch),
        ),
        input_output_aliases=aliases or {},
        compiler_params=pltpu.CompilerParams(
            dimension_semantics=("arbitrary",) * len(grid), vmem_limit_bytes=56 * 2**20
        ),
        cost_estimate=pl.CostEstimate(flops=1024, bytes_accessed=1024, transcendentals=0),
    )(ids, *ins)


def shape(dims, dtype):
    return jax.ShapeDtypeStruct(dims, dtype)


def whole(dims):
    zeros = (0,) * len(dims)
    return pl.BlockSpec(dims, lambda *_: zeros)


IN_PLACE = pl.BlockSpec(memory_space=pl.ANY)


def store_transposed(ids, value, blocks_ref, out_ref):
    count, height = blocks_ref.shape[0], blocks_ref.shape[1]
    step = 128 // height
    for c in range(value.shape[1] // 128):
        part = value[:, c * 128 : (c + 1) * 128]
        blocks_ref[c * step : (c + 1) * step] = part.T.reshape(step, height, part.shape[0])
    for core in range(2):
        for pair in range(count // 2):
            source = 2 * (pair ^ ids[1]) + (core ^ ids[2])
            out_ref[core * (count // 2) + pair] = blocks_ref[source]


def position(order, f, t):
    at = 0
    for k, bit in enumerate(order):
        value = t if bit == TENSOR else (f // bit) % 2
        at = at + value * 2**k
    return at


def swap(value, bit):
    if bit == TENSOR:
        return lax.ppermute(value, "tensor", [(0, 1), (1, 0)])
    return lax.ppermute(value, "fsdp", [(i, i ^ bit) for i in range(lax.axis_size("fsdp"))])


class Gathered:
    def __init__(self, mine, order):
        self.order = order
        self.left = [*order, CORE]
        self.held = mine
        self.rows = mine.shape
        self.ready = False
        self.begin()

    def begin(self):
        self.got = swap(self.held, self.left[0])
        if len(self.left) == 2:
            self.early = swap(self.held, CORE)

    def advance(self):
        if self.left.pop(0) == CORE:
            arrays = (self.held, self.last, self.early, self.got)
            self.arrays = [a.reshape((-1,) + self.rows) for a in arrays]
            self.ready = True
        elif self.left == [CORE]:
            self.last = self.got
            self.got = swap(self.last, CORE)
        else:
            self.held = jnp.stack([self.held, self.got])
            self.begin()


class Summed:
    def __init__(self, keep, send, order):
        dims = (2,) * 4 + keep.shape[2:]
        axes = (TENSOR, Z_FAR, Z_NEAR, X)
        self.arrays = [(keep.reshape(dims), axes)]
        self.axes = axes
        self.left = list(order)
        self.got = swap(send.reshape(dims), CORE)
        self.bit = None

    def received(self):
        self.arrays.append((self.got, self.axes))
        self.bit = self.left.pop(0) if self.left else None
        self.axes = tuple(a for a in self.axes if a != self.bit)


def halve(ids, sums):
    for s in sums:
        s.received()
    steps = 2 if any(s.axes for s in sums) else 1
    ins, in_specs, outs, out_specs, counts = [], [], [], [], []
    for s in sums:
        rows, columns = s.arrays[0][0].shape[-2:]
        split = s.axes[0] if steps == 2 and s.axes else None

        def spec(axes, now=s.axes, bit=s.bit, split=split, tail=(rows, columns)):
            block = tuple(2 if a in now and a != split else None for a in axes)

            def index(g, ids):
                at = tuple(g if a == split else int(a == bit and a not in now) for a in axes)
                return (*at, 0, 0)

            return pl.BlockSpec(block + tail, index)

        for array, axes in s.arrays:
            ins.append(array)
            in_specs.append(spec(axes))
        counts.append(len(s.arrays))
        kind = F32 if s.bit is None else BF
        outs.append(shape((2,) * len(s.axes) + (rows, columns), kind))
        out_specs.append(spec(s.axes))

    def body(ids, *refs):
        out_refs = refs[len(ins) :]
        at = 0
        for out_ref, count in zip(out_refs, counts):
            for where in itertools.product(range(2), repeat=len(out_ref.shape) - 2):
                total = refs[at][where].astype(F32)
                for k in range(1, count):
                    total += refs[at + k][where].astype(F32)
                out_ref[where] = total.astype(out_ref.dtype)
            at += count

    made = call(body, "halve", ids, tuple(ins), in_specs, tuple(outs), out_specs, (steps,))
    for s, value in zip(sums, made):
        if s.bit is None:
            s.result = value
        else:
            s.got = swap(value, s.bit)
    return made


def after(values, running):
    running = [r for r in running if not r.ready]
    values, got = lax.optimization_barrier((values, [r.got for r in running]))
    for r, g in zip(running, got):
        r.got = g
        r.advance()
    return values


def gathered_pair(ids, refs, order, pair, part, low, high):
    count = refs[0].shape[0]
    at = position(order, 2 * pair, part) ^ position(order, ids[3], ids[0])
    late = at >= count
    at = at % count
    held, last, early, other = [ref[at, low:high] for ref in refs]
    a, b = jnp.where(late, last, held), jnp.where(late, other, early)
    flipped = ids[2] == 1
    return jnp.where(flipped, b, a), jnp.where(flipped, a, b)


def make_qkv(ids, rows, gots, gain, gathered, height):
    parts, local_rows, width = rows.shape
    length = parts * local_rows
    fsdp = width // height
    half = width // parts
    per = local_rows // TILE

    def body(ids, rows_ref, gain_ref, *refs):
        qkv_ref, xt_ref, x_ref, w_ref, wo_ref, blocks_ref = refs[-6:]
        step = pl.program_id(0)

        @pl.when(step == 0)
        def _():
            @pl.loop(0, fsdp // 2)
            def _(pair):
                for t in range(parts):
                    first = 0
                    for c in range(3):
                        args = (ids, refs[4 * c : 4 * c + 4], gathered[c].order, pair, t)
                        for core, rows in enumerate(gathered_pair(*args, 0, height)):
                            start = pl.multiple_of((2 * pair + core) * height, height)
                            w_ref[c, t, pl.ds(start, height)] = rows
                        count = O_ROWS[c]
                        if not count:
                            continue
                        for core, rows in enumerate(
                            gathered_pair(*args, height, height + count)
                        ):
                            start = (2 * pair + core) * height + first
                            wo_ref[t, pl.ds(pl.multiple_of(start, 16), count)] = rows
                        first += count

        @pl.when(step // per == ids[0])
        def _():
            x_ref[...] = rows_ref[0]

        for k in range(per):

            @pl.when((step // per != ids[0]) & (step % per == k))
            def _(k=k):
                x_ref[...] = refs[12 + k][...]

        values = x_ref[...].astype(F32)
        xn = (values * rms_scale(values) * gain_ref[...]).astype(BF)
        for c in range(3):
            for t in range(parts):
                made = dot_f32(xn, w_ref[c, t], 1, 0)
                if c == 0:
                    made = made * HEAD_DIM ** (-0.5)
                qkv_ref[c, :, t * half : (t + 1) * half] = made.astype(BF)
        store_transposed(ids, xn, blocks_ref, xt_ref)

    weights = [a for g in gathered for a in g.arrays]
    return call(
        body,
        "qkv",
        ids,
        (rows, gain, *weights, *gots),
        [
            pl.BlockSpec((1, TILE, width), lambda r, ids: (ids[0], r % per, 0)),
            whole((1, width)),
        ]
        + [whole(a.shape) for a in (*weights, *gots)],
        (
            shape((3, length, width), BF),
            shape((fsdp, height, length), BF),
            shape((length, width), BF),
            shape((3, parts, width, half), BF),
            shape((parts, width, half), BF),
        ),
        [
            pl.BlockSpec((3, TILE, width), lambda r, ids: (0, r, 0)),
            pl.BlockSpec((fsdp, height, TILE), lambda r, ids: (0, 0, r)),
            pl.BlockSpec((TILE, width), lambda r, ids: (r, 0)),
            whole((3, parts, width, half)),
            whole((parts, width, half)),
        ],
        (length // TILE,),
        (pltpu.VMEM((fsdp, height, TILE), BF),),
    )


def store_natural(value, out_ref):
    height = out_ref.shape[-2]
    step = 128 // height
    for c in range(value.shape[1] // 128):
        part = value[:, c * 128 : (c + 1) * 128]
        out_ref[c * step : (c + 1) * step] = part.T.reshape(step, height, part.shape[0])


def join_rows(ids, rows, got):
    parts, local_rows, width = rows.shape
    length = parts * local_rows

    def body(ids, rows_ref, got_ref, out_ref):
        mine = pl.multiple_of(ids[0] * local_rows, local_rows)
        out_ref[0, pl.ds(mine, local_rows)] = rows_ref[0]
        rest = pl.multiple_of((1 - ids[0]) * local_rows, local_rows)
        out_ref[0, pl.ds(rest, local_rows)] = got_ref[0]

    spec = pl.BlockSpec((1, local_rows, width), lambda s, ids: (s ^ ids[0], 0, 0))
    return call(
        body,
        "join_rows",
        ids,
        (rows, got),
        [spec, spec],
        (shape((parts, length, width), BF),),
        [pl.BlockSpec((1, length, width), lambda s, ids: (s, 0, 0))],
        (parts,),
    )[0]


def lane_mask(values, head):
    lanes = lax.broadcasted_iota(jnp.int32, values.shape, 1)
    return jnp.where(lanes // HEAD_DIM == head, values, jnp.zeros_like(values))


def attend(ids, qkv):
    length, width = qkv.shape[1:]
    tiles = length // TILE
    pair = 2 * HEAD_DIM
    heads = width // HEAD_DIM

    def body(ids, q_ref, k_ref, v_ref, *refs):
        o_ref, ot_ref, e_ref, inv_ref, bias_ref, s_ref = refs[-6:]

        @pl.when(pl.program_id(0) == 0)
        def _():
            for i in range(tiles):
                keys = i * TILE + lax.broadcasted_iota(jnp.int32, (2 * TILE, TILE), 0)
                rows = i * TILE + lax.broadcasted_iota(jnp.int32, (2 * TILE, TILE), 1)
                seen = keys <= rows
                for p in range(3):
                    start = ids[4 + p]
                    inside = (keys >= start) & (keys < start + PIECE)
                    inside &= (rows >= start) & (rows < start + PIECE)
                    seen |= inside
                bias_ref[i] = jnp.where(seen, 0.0, masked_score)

        k = k_ref[0]
        vt = v_ref[0].T
        slots = s_ref.shape[0]
        todo = [(i, head) for i in range(tiles) for head in range(2)]
        state = {}

        def score(n):
            i, head = todo[n]
            q_head = lane_mask(q_ref[0, i * TILE : (i + 1) * TILE], head)
            top = None
            for j in range(min(i + 2, tiles)):
                s = dot_f32(k[j * TILE : (j + 1) * TILE], q_head, 1, 1)
                if j >= i:
                    s = s + bias_ref[i, (j - i) * TILE : (j - i + 1) * TILE]
                s_ref[n % slots, j] = s
                now = jnp.max(s.reshape(TILE // 8, 8, TILE), axis=0)
                top = now if top is None else jnp.maximum(top, now)
            state[n] = jnp.max(top, axis=0, keepdims=True)

        def soften(n):
            i, head = todo[n]
            total = None
            for j in range(min(i + 2, tiles)):
                e = jnp.exp(s_ref[n % slots, j] - state[n])
                now = jnp.sum(e.reshape(TILE // 8, 8, TILE), axis=0)
                total = now if total is None else total + now
                e_ref[head, j * TILE : (j + 1) * TILE, i * TILE : (i + 1) * TILE] = e.astype(BF)
            state[n] = 1.0 / jnp.sum(total, axis=0, keepdims=True)
            inv_ref[0, head : head + 1, i * TILE : (i + 1) * TILE] = state[n]

        def gather_values(n):
            i, head = todo[n]
            used = min(i + 2, tiles) * TILE
            out = dot_f32(
                vt[head * HEAD_DIM : (head + 1) * HEAD_DIM, :used],
                e_ref[head, :used, i * TILE : (i + 1) * TILE],
                1,
                0,
            )
            state[n] = out * state[n]
            if head == 1:
                both = jnp.concatenate([state[n - 1], state[n]], axis=0)
                ot_ref[:, i * TILE : (i + 1) * TILE] = both.astype(BF)
                o_ref[i * TILE : (i + 1) * TILE] = both.T.astype(BF)

        for n in range(len(todo) + 2):
            if n < len(todo):
                score(n)
            if 1 <= n <= len(todo):
                soften(n - 1)
            if n >= 2:
                gather_values(n - 2)

    spec = [
        pl.BlockSpec((1, length, pair), lambda p, ids, c=c: (c, 0, p)) for c in range(3)
    ]
    return call(
        body,
        "attend",
        ids,
        (qkv, qkv, qkv),
        spec,
        (
            shape((length, width), BF),
            shape((width, length), BF),
            shape((heads, length, length), BF),
            shape((heads // 2, 2, length), F32),
        ),
        [
            pl.BlockSpec((length, pair), lambda p, ids: (0, p)),
            pl.BlockSpec((pair, length), lambda p, ids: (p, 0)),
            pl.BlockSpec((2, length, length), lambda p, ids: (p, 0, 0)),
            pl.BlockSpec((1, 2, length), lambda p, ids: (p, 0, 0)),
        ],
        (heads // 2,),
        (
            pltpu.VMEM((tiles, 2 * TILE, TILE), F32),
            pltpu.VMEM((4, tiles, TILE, TILE), F32),
        ),
    )


def attend_back(ids, qkv, d_heads, saved):
    length, width = qkv.shape[1:]
    tiles = length // TILE
    pair = 2 * HEAD_DIM
    heads = width // HEAD_DIM

    def body(ids, q_ref, k_ref, v_ref, d_ref, ot_ref, e_ref, inv_ref, *refs):
        out_ref, ds_ref, dq_ref = refs[-3:]
        k = k_ref[0]
        v = v_ref[0]
        kt = k.T
        dt = d_ref[...].astype(F32).T
        q_heads = []
        d_scaled = []
        deltas = []
        for head in range(2):
            span = slice(head * HEAD_DIM, (head + 1) * HEAD_DIM)
            inv_row = inv_ref[0, head : head + 1]
            mine = dt[span] * inv_row
            deltas.append(jnp.sum(mine * ot_ref[span].astype(F32), axis=0, keepdims=True))
            blank = jnp.zeros((HEAD_DIM, length), BF)
            mine = mine.astype(BF)
            d_scaled.append(
                jnp.concatenate([mine, blank] if head == 0 else [blank, mine], axis=0)
            )
            q_heads.append(lane_mask(q_ref[0], head))
        dq_ref[...] = jnp.zeros_like(dq_ref)
        sums = {}

        def scores_back(j, head):
            keys = slice(j * TILE, (j + 1) * TILE)
            for r in range(max(j - 1, 0) * TILE, length, TILE):
                cols = slice(r, r + TILE)
                dp = dot_f32(v[keys], d_scaled[head][:, cols], 1, 0)
                weights = e_ref[head, keys, cols].astype(F32)
                ds_ref[j % 2, head, :, cols] = (weights * (dp - deltas[head][:, cols])).astype(BF)

        def operands_back(j, head):
            keys = slice(j * TILE, (j + 1) * TILE)
            rows = slice(head * HEAD_DIM, (head + 1) * HEAD_DIM)
            first = max(j - 1, 0) * TILE
            ds = ds_ref[j % 2, head, :, first:length]
            d_key = dot_f32(ds, q_heads[head][first:length], 1, 0)
            d_value = dot_f32(
                e_ref[head, keys, first:length], d_scaled[head][:, first:length], 1, 1
            )
            dq_ref[rows, first:length] += dot_f32(kt[rows, keys], ds, 1, 0)
            if head == 0:
                sums[j] = (d_key, d_value)
            else:
                out_ref[1, keys] = (sums[j][0] + d_key).astype(BF)
                out_ref[2, keys] = (sums[j][1] + d_value).astype(BF)

        todo = [(j, head) for j in range(tiles) for head in range(2)]
        for n in range(len(todo) + 1):
            if n < len(todo):
                scores_back(*todo[n])
            if n >= 1:
                operands_back(*todo[n - 1])
        out_ref[0] = (dq_ref[...] * HEAD_DIM ** (-0.5)).T.astype(BF)

    spec = [
        pl.BlockSpec((1, length, pair), lambda p, ids, c=c: (c, 0, p)) for c in range(3)
    ]
    return call(
        body,
        "attend_back",
        ids,
        (qkv, qkv, qkv, d_heads, *saved),
        spec
        + [
            pl.BlockSpec((length, pair), lambda p, ids: (0, p)),
            pl.BlockSpec((pair, length), lambda p, ids: (p, 0)),
            pl.BlockSpec((2, length, length), lambda p, ids: (p, 0, 0)),
            pl.BlockSpec((1, 2, length), lambda p, ids: (p, 0, 0)),
        ],
        (shape((3, length, width), BF),),
        [pl.BlockSpec((3, length, pair), lambda p, ids: (0, 0, p))],
        (heads // 2,),
        (pltpu.VMEM((2, 2, TILE, length), BF), pltpu.VMEM((pair, length), F32)),
    )[0]


def out_project(ids, attended, w_out, x, gain):
    length, width = x.shape
    parts, _, half = w_out.shape

    def body(ids, a_ref, w_ref, x_ref, gain_ref, hidden_ref, hn_ref):
        total = x_ref[...].astype(F32)
        for t in range(parts):
            total += dot_f32(a_ref[:, t * half : (t + 1) * half], w_ref[t], 1, 1)
        hidden_ref[...] = total
        hn_ref[...] = (total * rms_scale(total) * gain_ref[...]).astype(BF)

    tile = pl.BlockSpec((TILE, width), lambda r, ids: (r, 0))
    return call(
        body,
        "out_project",
        ids,
        (attended, w_out, x, gain),
        [tile, whole(w_out.shape), tile, whole((1, width))],
        (shape((length, width), F32), shape((length, width), BF)),
        [tile, tile],
        (length // TILE,),
    )


def feed_forward(ids, hn, grads, which, packed):
    length, width = hn.shape
    fsdp, rows, units = packed.shape
    height = rows // 3
    tile = 256
    steps = units // tile
    columns = width // steps

    def body(ids, hn_ref, g_ref, w_ref, out_ref, t_ref):
        first = pl.multiple_of(pl.program_id(0) * columns, columns)
        store_natural(hn_ref[:, pl.ds(first, columns)], t_ref.at[0])
        store_natural(g_ref[0, :, pl.ds(first, columns)], t_ref.at[1])
        w_gate, w_up, w_down = [
            w_ref[:, c * height : (c + 1) * height].reshape(width, tile) for c in range(3)
        ]
        for r in range(0, length, TILE):
            rows = hn_ref[r : r + TILE]
            gate = dot_f32(rows, w_gate, 1, 0)
            up = dot_f32(rows, w_up, 1, 0)
            d_mixed = dot_f32(g_ref[0, r : r + TILE], w_down, 1, 0)
            sig = jax.nn.sigmoid(gate)
            act = gate * sig
            out_ref[0, r : r + TILE] = (
                d_mixed * up * sig * (1.0 + gate * (1.0 - sig))
            ).astype(BF)
            out_ref[1, r : r + TILE] = (d_mixed * act).astype(BF)
            out_ref[2, r : r + TILE] = (act * up).astype(BF)

    return call(
        body,
        "feed_forward",
        ids,
        (hn, grads, packed),
        [
            whole((length, width)),
            pl.BlockSpec((1, length, width), lambda n, ids: (which, 0, 0)),
            pl.BlockSpec((fsdp, rows, tile), lambda n, ids: (0, 0, n)),
        ],
        (
            shape((3, length, units), BF),
            shape((2, fsdp, height, length), BF),
        ),
        [
            pl.BlockSpec((3, length, tile), lambda n, ids: (0, 0, n)),
            pl.BlockSpec((2, columns // height, height, length), lambda n, ids: (0, n, 0, 0)),
        ],
        (steps,),
    )


def feed_forward_out(ids, own, theirs, packed, hidden):
    length, width = hidden.shape
    fsdp, rows, units = packed.shape
    height = rows // 3
    kept = length // 2
    per = kept // TILE

    def body(ids, own_ref, theirs_ref, w_ref, hidden_ref, keep_ref, send_ref):
        w = w_ref[...].reshape(width, units)
        mine = pl.program_id(0) == 0
        keeps = pl.program_id(1) >= per

        rows = jnp.where(mine, own_ref[0], theirs_ref[0])
        made = dot_f32(rows, w, 1, 1) + jnp.where(mine, hidden_ref[...], 0.0)

        @pl.when(keeps)
        def _():
            keep_ref[0] = made

        @pl.when(~keeps)
        def _():
            send_ref[0] = made.astype(BF)

    def row(j, ids):
        return jnp.where(j < per, (1 - ids[0]) * per + j, ids[0] * per + j - per)

    return call(
        body,
        "feed_forward_out",
        ids,
        (own, theirs, packed, hidden),
        [
            pl.BlockSpec(
                (1, TILE, units),
                lambda s, j, ids: (2, row(jnp.where(s == 0, j, 2 * per - 1), ids), 0),
            ),
            pl.BlockSpec(
                (1, TILE, units), lambda s, j, ids: (2, row(jnp.where(s == 1, j, 0), ids), 0)
            ),
            pl.BlockSpec((fsdp, height, units), lambda s, j, ids: (0, 2, 0)),
            pl.BlockSpec(
                (TILE, width), lambda s, j, ids: (row(jnp.where(s == 0, j, 2 * per - 1), ids), 0)
            ),
        ],
        (shape((2, kept, width), F32), shape((2, kept, width), BF)),
        [
            pl.BlockSpec(
                (1, TILE, width), lambda s, j, ids: (s ^ ids[0], jnp.maximum(j - per, 0), 0)
            ),
            pl.BlockSpec(
                (1, TILE, width), lambda s, j, ids: (s ^ ids[0], jnp.minimum(j, per - 1), 0)
            ),
        ],
        (2, 2 * per),
    )


def feed_forward_grads(ids, own_t, theirs_t, own, theirs):
    fsdp, height, length = own_t.shape[1:]
    units = own.shape[2]
    per = units // UNITS

    def body(ids, a_ref, b_ref, own_ref, theirs_ref, out_ref):
        for f in range(0, fsdp, 4):
            a = a_ref[0, f : f + 4].reshape(4 * height, length)
            b = b_ref[0, f : f + 4].reshape(4 * height, length)
            made = dot_f32(a, own_ref[0], 1, 0) + dot_f32(b, theirs_ref[0], 1, 0)
            out_ref[f : f + 4] = made.astype(BF).reshape(4, height, UNITS)

    left = pl.BlockSpec((1, fsdp, height, length), lambda c, n, ids: (c // 2, 0, 0, 0))
    right = pl.BlockSpec((1, length, UNITS), lambda c, n, ids: (c, 0, n))
    return call(
        body,
        "feed_forward_grads",
        ids,
        (own_t, theirs_t, own, theirs),
        [left, left, right, right],
        (shape((fsdp, 3 * height, units), BF),),
        [pl.BlockSpec((fsdp, height, UNITS), lambda c, n, ids: (0, c, n))],
        (3, per),
    )[0]


def weight_grad(ids, name, sources):
    fsdp, height, length = sources[0][0].shape
    parts = 2
    half = sources[0][1].shape[2] // parts
    tile = min(UNITS, half)
    per = half // tile
    hop = fsdp // 2

    def body(ids, *refs):
        outs = refs[-2:]
        for k in range(len(sources)):
            l_ref, r_ref = refs[2 * k : 2 * k + 2]

            @pl.when(pl.program_id(0) == k)
            def _(l_ref=l_ref, r_ref=r_ref):
                right_tile = r_ref[0]
                for b in range(0, fsdp, 4):
                    block = l_ref[b : b + 4].reshape(4 * height, length)
                    made = dot_f32(block, right_tile, 1, 0).astype(BF)
                    outs[b // hop][0, b % hop : b % hop + 4] = made.reshape(4, height, tile)

    ins, specs = [], []
    for k, (left, right, index) in enumerate(sources):
        ins += [left, right]

        def columns(c, t, n, ids, k=k, index=index):
            at = n * parts + t
            at = jnp.where(c == k, at, 0 if k else half * parts // tile - 1)
            return (index, 0, at)

        specs += [whole(left.shape), pl.BlockSpec((1, length, tile), columns)]
    spec = pl.BlockSpec((1, hop, height, tile), lambda c, t, n, ids: (t ^ ids[0], 0, c, n))
    return call(
        body,
        name,
        ids,
        tuple(ins),
        specs,
        (shape((parts, hop, len(sources) * height, half), BF),) * 2,
        [spec, spec],
        (len(sources), parts, per),
    )


def feed_forward_back(ids, stacked, packed, half=None):
    length = stacked.shape[1] if half is None else stacked.shape[1] // 2
    at = half or 0
    fsdp, rows, units = packed.shape
    height = rows // 3
    width = fsdp * height
    per = units // UNITS

    def body(ids, d_ref, w_ref, *refs):
        acc_ref = refs[-1]

        @pl.when(pl.program_id(0) == 0)
        def _():
            acc_ref[...] = jnp.zeros_like(acc_ref)

        w_gate, w_up = [
            w_ref[:, c * height : (c + 1) * height].reshape(width, UNITS) for c in range(2)
        ]
        for r in range(0, length, TILE):
            acc_ref[r : r + TILE] += dot_f32(d_ref[0, r : r + TILE], w_gate, 1, 1) + dot_f32(
                d_ref[1, r : r + TILE], w_up, 1, 1
            )

        @pl.when(pl.program_id(0) == per - 1)
        def _():
            refs[0][...] = acc_ref[...].astype(refs[0].dtype)

    return call(
        body,
        "feed_forward_back",
        ids,
        (stacked, packed),
        [
            pl.BlockSpec((2, length, UNITS), lambda n, ids: (0, at, n)),
            pl.BlockSpec((fsdp, 2 * height, UNITS), lambda n, ids: (0, 0, n)),
        ],
        (shape((length, width), BF),),
        [whole((length, width))],
        (per,),
        (pltpu.VMEM((length, width), F32),),
    )[0]


def norm_and_project_back(ids, share, gots, hidden, grads, gain, w_out):
    length, width = hidden.shape
    parts, _, half = w_out.shape
    fsdp = lax.axis_size("fsdp")
    height = width // fsdp
    cut = gots[0].shape[0] // TILE

    def body(ids, share_ref, got_ref, tail_ref, hidden_ref, g_ref, gain_ref, w_ref, *refs):
        low_ref, lt_ref, out_ref, blocks_ref, got_scr = refs

        @pl.when(pl.program_id(0) < cut)
        def _():
            got_scr[...] = got_ref[...]

        @pl.when(pl.program_id(0) >= cut)
        def _():
            got_scr[...] = tail_ref[...]

        rows = hidden_ref[...]
        scale = rms_scale(rows)
        normed = rows * scale
        d_normed = share_ref[...].astype(F32) + got_scr[...].astype(F32)
        dh = g_ref[0].astype(F32) + norm_backward_pass(d_normed, normed, scale, gain_ref[...])
        low = dh.astype(BF)
        low_ref[...] = low
        for t in range(parts):
            out_ref[:, t * half : (t + 1) * half] = dot_f32(low, w_ref[t], 1, 0).astype(BF)
        store_transposed(ids, low, blocks_ref, lt_ref)

    tile = pl.BlockSpec((TILE, width), lambda r, ids: (r, 0))
    return call(
        body,
        "norm_and_project_back",
        ids,
        (share, *gots, hidden, grads, gain, w_out),
        [
            tile,
            pl.BlockSpec((TILE, width), lambda r, ids: (jnp.minimum(r, cut - 1), 0)),
            pl.BlockSpec((TILE, width), lambda r, ids: (jnp.maximum(r - cut, 0), 0)),
            tile,
            pl.BlockSpec((1, TILE, width), lambda r, ids: (0, r, 0)),
            whole((1, width)),
            whole(w_out.shape),
        ],
        (
            shape((length, width), BF),
            shape((fsdp, height, length), BF),
            shape((length, width), BF),
        ),
        [tile, pl.BlockSpec((fsdp, height, TILE), lambda r, ids: (0, 0, r)), tile],
        (length // TILE,),
        (pltpu.VMEM((fsdp, height, TILE), BF), pltpu.VMEM((TILE, width), BF)),
    )


def store_lines(out_ref, values):
    lines = values.shape[1] // 128
    for n in range(lines):
        out_ref[0, pl.ds(n, values.shape[0], stride=lines)] = values[:, n * 128 : (n + 1) * 128]


def qkv_back(ids, d_qkv, weights, x, dh, gain, sent):
    length, width = x.shape
    parts, _, half = weights.shape[1:]
    kept = length // parts
    per = kept // TILE

    def body(ids, d_ref, w_ref, x_ref, dh_ref, gain_ref, out_ref, acc_ref):
        d_normed = None
        for c in range(3):
            for t in range(parts):
                part = dot_f32(d_ref[c, :, t * half : (t + 1) * half], w_ref[c, t], 1, 1)
                d_normed = part if d_normed is None else d_normed + part
        rows = x_ref[...].astype(F32)
        scale = rms_scale(rows)
        made = dh_ref[...].astype(F32) + norm_backward_pass(d_normed, rows * scale, scale, gain_ref[...])
        if sent:
            out_ref[...] = made.astype(BF)
        else:
            acc_ref[...] = made
            store_lines(out_ref, acc_ref)

    def rows(r, ids):
        return per * (1 - ids[0] if sent else ids[0]) + r

    lines = kept * width // 128
    return call(
        body,
        "qkv_back",
        ids,
        (d_qkv, weights, x, dh, gain),
        [
            pl.BlockSpec((3, TILE, width), lambda r, ids: (0, rows(r, ids), 0)),
            whole(weights.shape),
            pl.BlockSpec((TILE, width), lambda r, ids: (rows(r, ids), 0)),
            pl.BlockSpec((TILE, width), lambda r, ids: (rows(r, ids), 0)),
            whole((1, width)),
        ],
        (shape((kept, width), BF) if sent else shape((parts, lines, 128), F32),),
        [
            pl.BlockSpec((TILE, width), lambda r, ids: (r, 0))
            if sent
            else pl.BlockSpec((1, lines // per, 128), lambda r, ids: (ids[0], r, 0)),
        ],
        (per,),
        (pltpu.VMEM((TILE, width), F32),),
    )[0]


def place_rows(ids, got, lines):
    kept, width = got.shape

    def body(ids, got_ref, _, out_ref, wide_ref):
        wide_ref[...] = got_ref[...].astype(F32)
        store_lines(out_ref, wide_ref)

    return call(
        body,
        "place_rows",
        ids,
        (got, lines),
        [whole((kept, width)), IN_PLACE],
        (shape(lines.shape, F32),),
        [pl.BlockSpec((1,) + lines.shape[1:], lambda g, ids: (1 - ids[0], 0, 0))],
        (1,),
        (pltpu.VMEM((kept, width), F32),),
        aliases={2: 0},
    )[0]


def three_parts(values):
    high = values.astype(BF)
    rest = values - high.astype(F32)
    middle = rest.astype(BF)
    return jnp.stack([high, middle, (rest - middle.astype(F32)).astype(BF)], -1)


def local_sequence(
    tokens, piece_starts, gain_attn, w_qkv, w_out, gain_mlp, w_gate_up, w_down, out_grad
):
    fsdp = lax.axis_size("fsdp")
    parts = lax.axis_size("tensor")
    me_f = lax.axis_index("fsdp")
    me_t = lax.axis_index("tensor")
    local_rows = tokens.shape[1]
    height = w_qkv.shape[1]
    half = w_qkv.shape[2]
    share = gain_attn.shape[0]

    starts = lax.dynamic_index_in_dim(piece_starts, me_t, 0, keepdims=False)[0]
    ids = jnp.stack([me_t, me_f // 2, me_f % 2, me_f]).astype(jnp.int32)
    ids = jnp.concatenate([ids, starts])
    rows_in = tokens.reshape(parts, local_rows, D)
    grads_in = out_grad.reshape(parts, local_rows, D)

    def other(rows):
        return lax.dynamic_index_in_dim(rows, 1 - me_t, 0, keepdims=False)

    o_mine = jnp.split(w_out.T, (O_ROWS[0], O_ROWS[0] + O_ROWS[1]))
    wk = Gathered(jnp.concatenate([w_qkv[1], o_mine[1]]), (TENSOR, Z_FAR, X, Z_NEAR))
    wv = Gathered(jnp.concatenate([w_qkv[2], o_mine[2]]), (TENSOR, Z_NEAR, Z_FAR, X))
    gains = three_parts(jnp.stack([gain_attn, gain_mlp])).reshape(1, -1)
    gains = jnp.pad(gains, ((0, 7), (0, half - gains.shape[1])))
    wq = Gathered(
        jnp.concatenate([w_qkv[0], o_mine[0], gains]), (Z_FAR, X, Z_NEAR, TENSOR)
    )
    ff_mine = jnp.concatenate([w_gate_up.reshape(2 * height, -1), w_down.T])
    aways = jnp.split(other(rows_in), 2)
    three = [wq, wk, wv]
    aways[0] = after(aways[0], three)
    got_one = swap(aways[0], TENSOR)
    got_one, aways[1] = after((got_one, aways[1]), three)
    got_two = swap(aways[1], TENSOR)
    got_two = after(got_two, three)
    ff_mine = after(ff_mine, three)
    packed = lax.all_gather(ff_mine, "fsdp", axis=0, tiled=False)
    got_rows = after((got_one, got_two), three)

    each = jnp.arange(fsdp * parts)
    each_f, each_t = each // parts, each % parts
    at = position(wq.order, each_f, each_t) ^ position(wq.order, me_f, me_t)
    at = at + fsdp * ((each_f ^ me_f) % 2)
    row = height + O_ROWS[0]
    gains = jnp.concatenate([a[:, row, : 6 * share] for a in wq.arrays])[at]
    gains = jnp.sum(gains.reshape(fsdp * parts, 2, share, 3).astype(F32), axis=3)
    gain_one, gain_two = [gains[:, i].reshape(1, D) for i in range(2)]

    qkv, xt, x, w_all, wo_all = make_qkv(ids, rows_in, got_rows, gain_one, three, height)
    _, away = lax.optimization_barrier((got_rows, grads_in))
    got_grads = swap(away, TENSOR)
    attended, *saved = attend(ids, qkv)
    hidden, hn = out_project(ids, attended, wo_all, x, gain_two)
    hn_theirs = swap(hn, TENSOR)
    grads = join_rows(ids, grads_in, got_grads)
    hn, grads, packed = lax.optimization_barrier((hn, grads, packed))

    own, own_t = feed_forward(ids, hn, grads, 0, packed)
    own, hn_theirs = lax.optimization_barrier((own, hn_theirs))
    theirs, theirs_t = feed_forward(ids, hn_theirs, grads, 1, packed)
    d_one = feed_forward_back(ids, theirs, packed, 0)
    d_one, theirs, own = lax.optimization_barrier((d_one, theirs, own))
    got_one = swap(d_one, TENSOR)
    made = feed_forward_grads(ids, own_t, theirs_t, own, theirs)
    made, own, theirs, got_one = lax.optimization_barrier((made, own, theirs, got_one))
    summed = lax.psum_scatter(made, "fsdp", scatter_dimension=0, tiled=False)
    d_two = feed_forward_back(ids, theirs, packed, 1)
    d_two, own, theirs = lax.optimization_barrier((d_two, own, theirs))
    got_two = swap(d_two, TENSOR)
    share_own = feed_forward_back(ids, own, packed)
    share_own, own, theirs = lax.optimization_barrier((share_own, own, theirs))
    keep_out, send_out = feed_forward_out(ids, own, theirs, packed, hidden)
    share_own, got_two, send_out = lax.optimization_barrier((share_own, got_two, send_out))
    dh, dt, d_attended = norm_and_project_back(
        ids, share_own, (got_one, got_two), hidden, grads, gain_two, wo_all
    )

    def join(values, sums):
        values, gots = lax.optimization_barrier((values, [s.got for s in sums]))
        for s, g in zip(sums, gots):
            s.got = g
        made = halve(ids, sums)
        return lax.optimization_barrier((values, made))[0]

    o_sum = weight_grad(ids, "grad_out", [(dt, attended[None], 0)])
    o_sum, d_attended, send_out = lax.optimization_barrier((o_sum, d_attended, send_out))
    o_sum = Summed(*o_sum, (X, Z_NEAR, TENSOR, Z_FAR))
    got_out = swap(send_out, TENSOR)
    d_qkv = attend_back(ids, qkv, d_attended, saved)

    d_qkv = join(d_qkv, [o_sum])

    orders = (
        (X, Z_NEAR, TENSOR, Z_FAR),
        (Z_NEAR, X, Z_FAR, TENSOR),
        (TENSOR, Z_FAR, X, Z_NEAR),
    )
    sums = []
    for c, order in enumerate(orders):
        made = weight_grad(ids, "grad_qkv", [(xt, d_qkv, c)])
        made, d_qkv = lax.optimization_barrier((made, d_qkv))
        sums.append(Summed(*made, order))
    d_qkv = join(d_qkv, sums)
    sums.append(o_sum)
    sent = qkv_back(ids, d_qkv, w_all, x, dh, gain_one, True)
    sent, d_qkv, got_out = join((sent, d_qkv, got_out), sums)
    layer_out = (keep_out + got_out.astype(F32)).astype(BF).reshape(tokens.shape)
    got_grad = swap(sent, TENSOR)
    lines = qkv_back(ids, d_qkv, w_all, x, dh, gain_one, False)
    lines, summed = join((lines, summed), sums)
    halve(ids, sums)
    lines, got_grad = lax.optimization_barrier((lines, got_grad))
    input_grad = join(place_rows(ids, got_grad, lines), sums).reshape(tokens.shape)
    qkv_grad = jnp.stack([s.result for s in sums[:3]])
    summed = summed.astype(F32)
    gate_up_grad = summed[: 2 * height].reshape(w_gate_up.shape)
    from_qkv = jnp.sum(w_qkv.astype(F32) * qkv_grad, axis=(0, 2))
    from_gate_up = jnp.sum(w_gate_up.astype(F32) * gate_up_grad, axis=(0, 2))
    both = jnp.stack([from_qkv, from_gate_up]).reshape(2, parts, share)
    mine = lax.dynamic_index_in_dim(both, me_t, 1, keepdims=False)
    theirs = lax.dynamic_index_in_dim(both, 1 - me_t, 1, keepdims=False)
    mine = mine + swap(theirs, TENSOR)
    return (
        layer_out,
        input_grad,
        mine[0] / gain_attn,
        qkv_grad,
        o_sum.result.T,
        mine[1] / gain_mlp,
        gate_up_grad,
        summed[2 * height :].T,
    )


def local_any(tokens, *rest):
    sizes = (lax.axis_size("tensor"), tokens.shape[0], tokens.shape[2], lax.axis_size("fsdp"))
    if sizes == (2, 2, 1, 16):
        return local_sequence(tokens, *rest)
    return local(tokens, *rest)


def solution(mesh):
    return jax.shard_map(
        local_any,
        mesh=mesh,
        in_specs=(
            P(None, "tensor", "fsdp", None),
            P(None, "fsdp", None),
            P(("fsdp", "tensor")),
            P(None, "fsdp", "tensor"),
            P("tensor", "fsdp"),
            P(("fsdp", "tensor")),
            P(None, "fsdp", "tensor"),
            P("tensor", "fsdp"),
            P(None, "tensor", "fsdp", None),
        ),
        out_specs=(
            P(None, "tensor", "fsdp", None),
            P(None, "tensor", "fsdp", None),
            P(("fsdp", "tensor")),
            P(None, "fsdp", "tensor"),
            P("tensor", "fsdp"),
            P(("fsdp", "tensor")),
            P(None, "fsdp", "tensor"),
            P("tensor", "fsdp"),
        ),
        check_vma=False,
    )
```

```python
import itertools

import jax
import jax.numpy as jnp
from jax import lax
from jax.experimental import pallas as pl
from jax.experimental.pallas import tpu as pltpu
from jax.sharding import PartitionSpec as P

D = 1024
HEAD_DIM = 64
QBLOCK = 512
PIECE = 256


norm_eps = 1e-05
masked_score = -1e30


def rms_scale(values_float_rows):
    return lax.rsqrt(
        jnp.mean(values_float_rows * values_float_rows, axis=-1, keepdims=True) + norm_eps
    )


def norm_backward_pass(d_normed, normed_pre, scale_rows, gain_vector_row):
    d_scaled = d_normed * gain_vector_row
    return scale_rows * (
        d_scaled - normed_pre * jnp.mean(d_scaled * normed_pre, axis=-1, keepdims=True)
    )


def piece_index_labels(starts_row, length):
    positions = jnp.arange(length, dtype=jnp.int32)[:, None]
    inside = (positions >= starts_row[None, :]) & (positions < starts_row[None, :] + PIECE)
    numbers = jnp.arange(1, starts_row.shape[0] + 1, dtype=jnp.int32)
    return jnp.sum(jnp.where(inside, numbers[None, :], 0), axis=1)


def allowed_block(labels, first_row, key_count):
    row_ids = first_row + jnp.arange(QBLOCK, dtype=jnp.int32)
    col_ids = jnp.arange(key_count, dtype=jnp.int32)
    row_labels = labels[first_row : first_row + QBLOCK]
    causal = col_ids[None, :] <= row_ids[:, None]
    same_piece = (row_labels[:, None] == labels[None, :]) & (row_labels[:, None] > 0)
    return causal | same_piece


def attend_forward(queries, keys_all, values_all, labels, key_spans):
    score_scale = HEAD_DIM ** (-0.5)
    outputs = []
    totals = []
    for first_row, key_count in key_spans:
        block_q = queries[first_row : first_row + QBLOCK]
        scores = (
            jnp.einsum("qhd,khd->hqk", block_q, keys_all, preferred_element_type=jnp.float32)
            * score_scale
        )
        scores = jnp.where(allowed_block(labels, first_row, key_count)[None], scores, masked_score)
        row_max = jnp.max(scores, axis=-1, keepdims=True)
        exp_scores = jnp.exp(scores - row_max)
        row_total = jnp.sum(exp_scores, axis=-1, keepdims=True)
        attn_probs = (exp_scores / row_total).astype(jnp.bfloat16)
        block_out = jnp.einsum(
            "hqk,khd->qhd", attn_probs, values_all, preferred_element_type=jnp.float32
        )
        outputs.append(block_out.astype(jnp.bfloat16))
        totals.append((row_max + jnp.log(row_total))[..., 0])
    return (jnp.concatenate(outputs, 0), jnp.concatenate(totals, 1))


def attend_backward(queries, keys_all, values_all, labels, log_total, d_heads, key_spans):
    score_scale = HEAD_DIM ** (-0.5)
    query_parts = []
    d_keys = jnp.zeros(keys_all.shape, jnp.float32)
    d_values = jnp.zeros(values_all.shape, jnp.float32)
    for first_row, key_count in key_spans:
        block_q = queries[first_row : first_row + QBLOCK]
        block_d = d_heads[first_row : first_row + QBLOCK]
        scores = (
            jnp.einsum("qhd,khd->hqk", block_q, keys_all, preferred_element_type=jnp.float32)
            * score_scale
        )
        mask_now = allowed_block(labels, first_row, key_count)[None]
        attn_probs = jnp.where(
            mask_now, jnp.exp(scores - log_total[:, first_row : first_row + QBLOCK, None]), 0.0
        )
        probs_low = attn_probs.astype(jnp.bfloat16)
        d_probs = jnp.einsum(
            "qhd,khd->hqk", block_d, values_all, preferred_element_type=jnp.float32
        )
        row_dot = jnp.sum(attn_probs * d_probs, axis=-1, keepdims=True)
        d_scores = (attn_probs * (d_probs - row_dot)).astype(jnp.bfloat16)
        query_parts.append(
            jnp.einsum("hqk,khd->qhd", d_scores, keys_all, preferred_element_type=jnp.float32)
            * score_scale
        )
        d_keys = d_keys.at[:key_count].add(
            jnp.einsum("hqk,qhd->khd", d_scores, block_q, preferred_element_type=jnp.float32)
            * score_scale
        )
        d_values = d_values.at[:key_count].add(
            jnp.einsum("hqk,qhd->khd", probs_low, block_d, preferred_element_type=jnp.float32)
        )
    return (jnp.concatenate(query_parts, 0), d_keys, d_values)


def attention_forward(qkv_low, labels_all, key_spans):
    length, seq_count, width = (qkv_low.shape[0], qkv_low.shape[1], qkv_low.shape[3])
    per_seq = jnp.moveaxis(qkv_low, 1, 0).reshape(seq_count, length, 3, width // HEAD_DIM, HEAD_DIM)

    def one_seq(seq_items):
        seq_qkv, labels = seq_items
        return attend_forward(seq_qkv[:, 0], seq_qkv[:, 1], seq_qkv[:, 2], labels, key_spans)

    seq_outs, totals = lax.map(one_seq, (per_seq, labels_all))
    return (jnp.moveaxis(seq_outs.reshape(seq_count, length, width), 0, 1), totals)


def attention_backward(qkv_low, labels_all, totals, d_attended, key_spans):
    length, seq_count, width = (qkv_low.shape[0], qkv_low.shape[1], qkv_low.shape[3])
    per_seq = jnp.moveaxis(qkv_low, 1, 0).reshape(seq_count, length, 3, width // HEAD_DIM, HEAD_DIM)
    d_seq = jnp.moveaxis(d_attended, 1, 0).reshape(seq_count, length, width // HEAD_DIM, HEAD_DIM)

    def one_seq(seq_items):
        seq_qkv, labels, log_total, seq_d = seq_items
        d_query, d_keys, d_values = attend_backward(
            seq_qkv[:, 0], seq_qkv[:, 1], seq_qkv[:, 2], labels, log_total, seq_d, key_spans
        )
        return jnp.stack([d_query, d_keys, d_values], 1).astype(jnp.bfloat16)

    seq_grads = lax.map(one_seq, (per_seq, labels_all, totals, d_seq))
    return jnp.moveaxis(seq_grads, 0, 1).reshape(length, seq_count, 3, width)


def fetch_weights(w_qkv, w_out, w_gate_up, w_down):
    qkv_all, out_all, gate_up_all, down_weight_full = (
        lax.all_gather(w_qkv, "fsdp", axis=1, tiled=True),
        lax.all_gather(w_out, "fsdp", axis=1, tiled=True),
        lax.all_gather(w_gate_up, "fsdp", axis=1, tiled=True),
        lax.all_gather(w_down, "fsdp", axis=1, tiled=True),
    )
    return (qkv_all, out_all, gate_up_all, down_weight_full)


def local(tokens, piece_starts, gain_attn, w_qkv, w_out, gain_mlp, w_gate_up, w_down, out_grad):
    both_gains = lax.all_gather(
        jnp.stack([gain_attn, gain_mlp]), ("fsdp", "tensor"), axis=1, tiled=True
    )
    local_rows = tokens.shape[1]
    length = local_rows * lax.axis_size("tensor")
    key_spans = [(first_row, length) for first_row in range(0, length, QBLOCK)]

    def label_row(starts_row):
        return piece_index_labels(starts_row, length)

    labels_every = jax.vmap(jax.vmap(label_row))(piece_starts)
    ff_cols = w_gate_up.shape[2]
    acc_gain = jnp.zeros((2, D), jnp.float32)
    acc_qkv = jnp.zeros((3, D, w_qkv.shape[2]), jnp.float32)
    acc_out = jnp.zeros((w_out.shape[0], D), jnp.float32)
    acc_gate_up = jnp.zeros((2, D, ff_cols), jnp.float32)
    acc_down = jnp.zeros((ff_cols, D), jnp.float32)
    layer_outs = []
    input_grads = []
    for micro_idx in range(tokens.shape[0]):
        weights = fetch_weights(w_qkv, w_out, w_gate_up, w_down)
        qkv_all, out_all, gate_up_all, down_weight_full = weights
        rows_f32 = tokens[micro_idx].astype(jnp.float32)
        scale_attn = rms_scale(rows_f32)
        pre_attn = rows_f32 * scale_attn
        normed = (pre_attn * both_gains[0]).astype(jnp.bfloat16)
        piece_rows = lax.all_gather(normed, "tensor", axis=0, tiled=True)
        made = jnp.einsum("lsd,cde->lsce", piece_rows, qkv_all, preferred_element_type=jnp.float32)
        qkv_low = made.astype(jnp.bfloat16)
        attended, log_total = attention_forward(qkv_low, labels_every[micro_idx], key_spans)
        rows_now = lax.slice_in_dim(attended, 0, local_rows * lax.axis_size("tensor"), axis=0)
        attn_part = lax.psum_scatter(
            jnp.einsum("lsc,cd->lsd", rows_now, out_all, preferred_element_type=jnp.float32).astype(
                jnp.bfloat16
            ),
            "tensor",
            scatter_dimension=0,
            tiled=True,
        ).astype(jnp.float32)
        hidden = rows_f32 + attn_part
        scale_mlp = rms_scale(hidden)
        pre_mlp = hidden * scale_mlp
        normed_mlp = (pre_mlp * both_gains[1]).astype(jnp.bfloat16)
        expand_piece_rows = lax.all_gather(normed_mlp, "tensor", axis=0, tiled=True)
        gate_up = jnp.einsum(
            "lsd,cdf->lscf", expand_piece_rows, gate_up_all, preferred_element_type=jnp.float32
        )
        gate_part = gate_up[:, :, 0]
        up_part = gate_up[:, :, 1]
        sigmoid_gate = jax.nn.sigmoid(gate_part)
        activated = gate_part * sigmoid_gate
        mixed_lowp_rows = (activated * up_part).astype(jnp.bfloat16)
        down_rows_now = lax.slice_in_dim(
            mixed_lowp_rows, 0, local_rows * lax.axis_size("tensor"), axis=0
        )
        mlp_part = lax.psum_scatter(
            jnp.einsum(
                "meg,gp->mep", down_rows_now, down_weight_full, preferred_element_type=jnp.float32
            ).astype(jnp.bfloat16),
            "tensor",
            scatter_dimension=0,
            tiled=True,
        ).astype(jnp.float32)
        layer_outs.append((hidden + mlp_part).astype(jnp.bfloat16))
        qkv_all, out_all, gate_up_all, down_weight_full = fetch_weights(
            w_qkv, w_out, w_gate_up, w_down
        )
        grad_rows = out_grad[micro_idx]
        down_piece_rows = lax.all_gather(grad_rows, "tensor", axis=0, tiled=True)
        d_mixed = jnp.einsum(
            "xum,tm->xut", down_piece_rows, down_weight_full, preferred_element_type=jnp.float32
        )
        acc_down = acc_down + jnp.einsum(
            "zmp,zme->pe", mixed_lowp_rows, down_piece_rows, preferred_element_type=jnp.float32
        )
        d_gate = d_mixed * up_part * sigmoid_gate * (1.0 + gate_part * (1.0 - sigmoid_gate))
        d_up = d_mixed * activated
        d_gate_up = jnp.stack([d_gate, d_up], 2).astype(jnp.bfloat16)
        acc_gate_up = acc_gate_up + jnp.einsum(
            "lsd,lscf->cdf", expand_piece_rows, d_gate_up, preferred_element_type=jnp.float32
        )
        mlp_rows_now = lax.slice_in_dim(d_gate_up, 0, local_rows * lax.axis_size("tensor"), axis=0)
        d_normed_mlp = lax.psum_scatter(
            jnp.einsum(
                "lscf,cdf->lsd", mlp_rows_now, gate_up_all, preferred_element_type=jnp.float32
            ).astype(jnp.bfloat16),
            "tensor",
            scatter_dimension=0,
            tiled=True,
        ).astype(jnp.float32)
        gain_mlp_part = jnp.sum(d_normed_mlp * pre_mlp, axis=(0, 1))
        d_hidden = grad_rows.astype(jnp.float32) + norm_backward_pass(
            d_normed_mlp, pre_mlp, scale_mlp, both_gains[1]
        )
        attention_gradient_lowp = d_hidden.astype(jnp.bfloat16)
        out_piece_rows = lax.all_gather(attention_gradient_lowp, "tensor", axis=0, tiled=True)
        out_made = jnp.einsum(
            "lsd,cd->lsc", out_piece_rows, out_all, preferred_element_type=jnp.float32
        )
        d_attended = out_made.astype(jnp.bfloat16)
        acc_out = acc_out + jnp.einsum(
            "lsc,lsd->cd", attended, out_piece_rows, preferred_element_type=jnp.float32
        )
        d_qkv = attention_backward(
            qkv_low, labels_every[micro_idx], log_total, d_attended, key_spans
        )
        acc_qkv = acc_qkv + jnp.einsum(
            "lsd,lsce->cde", piece_rows, d_qkv, preferred_element_type=jnp.float32
        )
        d_normed = lax.psum_scatter(
            jnp.einsum("lsce,cde->lsd", d_qkv, qkv_all, preferred_element_type=jnp.float32).astype(
                jnp.bfloat16
            ),
            "tensor",
            scatter_dimension=0,
            tiled=True,
        ).astype(jnp.float32)
        gain_attn_part = jnp.sum(d_normed * pre_attn, axis=(0, 1))
        input_grads.append(
            d_hidden + norm_backward_pass(d_normed, pre_attn, scale_attn, both_gains[0])
        )
        acc_gain = acc_gain + jnp.stack([gain_attn_part, gain_mlp_part])
    gain_rows, qkv_rows, out_rows_sum, gate_up_rows, down_rows_sum = (
        lax.psum_scatter(
            acc_gain.astype(jnp.bfloat16), "fsdp", scatter_dimension=1, tiled=True
        ).astype(jnp.float32),
        lax.psum_scatter(
            acc_qkv.astype(jnp.bfloat16), "fsdp", scatter_dimension=1, tiled=True
        ).astype(jnp.float32),
        lax.psum_scatter(
            acc_out.astype(jnp.bfloat16), "fsdp", scatter_dimension=1, tiled=True
        ).astype(jnp.float32),
        lax.psum_scatter(
            acc_gate_up.astype(jnp.bfloat16), "fsdp", scatter_dimension=1, tiled=True
        ).astype(jnp.float32),
        lax.psum_scatter(
            acc_down.astype(jnp.bfloat16), "fsdp", scatter_dimension=1, tiled=True
        ).astype(jnp.float32),
    )
    gain_shares = lax.psum_scatter(gain_rows, "tensor", scatter_dimension=1, tiled=True)
    return (
        jnp.stack(layer_outs, 0),
        jnp.stack(input_grads, 0),
        gain_shares[0],
        qkv_rows,
        out_rows_sum,
        gain_shares[1],
        gate_up_rows,
        down_rows_sum,
    )


BF = jnp.bfloat16
F32 = jnp.float32
TILE = 256
UNITS = 512
O_ROWS = (16, 32, 16)
CORE, TENSOR, X, Z_NEAR, Z_FAR = 1, 0, 2, 4, 8


def dot_f32(a, b, ca, cb):
    return lax.dot_general(a, b, (((ca,), (cb,)), ((), ())), preferred_element_type=F32)


def call(body, name, ids, ins, in_specs, outs, out_specs, grid, scratch=(), aliases=None):
    return pl.pallas_call(
        body,
        name=name,
        out_shape=outs,
        grid_spec=pltpu.PrefetchScalarGridSpec(
            num_scalar_prefetch=1,
            grid=grid,
            in_specs=in_specs,
            out_specs=out_specs,
            scratch_shapes=list(scratch),
        ),
        input_output_aliases=aliases or {},
        compiler_params=pltpu.CompilerParams(
            dimension_semantics=("arbitrary",) * len(grid), vmem_limit_bytes=56 * 2**20
        ),
        cost_estimate=pl.CostEstimate(flops=1024, bytes_accessed=1024, transcendentals=0),
    )(ids, *ins)


def shape(dims, dtype):
    return jax.ShapeDtypeStruct(dims, dtype)


def whole(dims):
    zeros = (0,) * len(dims)
    return pl.BlockSpec(dims, lambda *_: zeros)


IN_PLACE = pl.BlockSpec(memory_space=pl.ANY)


def store_transposed(ids, value, blocks_ref, out_ref):
    count, height = blocks_ref.shape[0], blocks_ref.shape[1]
    step = 128 // height
    for c in range(value.shape[1] // 128):
        part = value[:, c * 128 : (c + 1) * 128]
        blocks_ref[c * step : (c + 1) * step] = part.T.reshape(step, height, part.shape[0])
    for core in range(2):
        for pair in range(count // 2):
            source = 2 * (pair ^ ids[1]) + (core ^ ids[2])
            out_ref[core * (count // 2) + pair] = blocks_ref[source]


def position(order, f, t):
    at = 0
    for k, bit in enumerate(order):
        value = t if bit == TENSOR else (f // bit) % 2
        at = at + value * 2**k
    return at


def swap(value, bit):
    if bit == TENSOR:
        return lax.ppermute(value, "tensor", [(0, 1), (1, 0)])
    return lax.ppermute(value, "fsdp", [(i, i ^ bit) for i in range(lax.axis_size("fsdp"))])


class Gathered:
    def __init__(self, mine, order):
        self.order = order
        self.left = [*order, CORE]
        self.held = mine
        self.rows = mine.shape
        self.ready = False
        self.begin()

    def begin(self):
        self.got = swap(self.held, self.left[0])
        if len(self.left) == 2:
            self.early = swap(self.held, CORE)

    def advance(self):
        if self.left.pop(0) == CORE:
            arrays = (self.held, self.last, self.early, self.got)
            self.arrays = [a.reshape((-1,) + self.rows) for a in arrays]
            self.ready = True
        elif self.left == [CORE]:
            self.last = self.got
            self.got = swap(self.last, CORE)
        else:
            self.held = jnp.stack([self.held, self.got])
            self.begin()


class Summed:
    def __init__(self, keep, send, order):
        dims = (2,) * 4 + keep.shape[2:]
        axes = (TENSOR, Z_FAR, Z_NEAR, X)
        self.arrays = [(keep.reshape(dims), axes)]
        self.axes = axes
        self.left = list(order)
        self.got = swap(send.reshape(dims), CORE)
        self.bit = None

    def received(self):
        self.arrays.append((self.got, self.axes))
        self.bit = self.left.pop(0) if self.left else None
        self.axes = tuple(a for a in self.axes if a != self.bit)


def halve(ids, sums):
    for s in sums:
        s.received()
    steps = 2 if any(s.axes for s in sums) else 1
    ins, in_specs, outs, out_specs, counts = [], [], [], [], []
    for s in sums:
        rows, columns = s.arrays[0][0].shape[-2:]
        split = s.axes[0] if steps == 2 and s.axes else None

        def spec(axes, now=s.axes, bit=s.bit, split=split, tail=(rows, columns)):
            block = tuple(2 if a in now and a != split else None for a in axes)

            def index(g, ids):
                at = tuple(g if a == split else int(a == bit and a not in now) for a in axes)
                return (*at, 0, 0)

            return pl.BlockSpec(block + tail, index)

        for array, axes in s.arrays:
            ins.append(array)
            in_specs.append(spec(axes))
        counts.append(len(s.arrays))
        kind = F32 if s.bit is None else BF
        outs.append(shape((2,) * len(s.axes) + (rows, columns), kind))
        out_specs.append(spec(s.axes))

    def body(ids, *refs):
        out_refs = refs[len(ins) :]
        at = 0
        for out_ref, count in zip(out_refs, counts):
            for where in itertools.product(range(2), repeat=len(out_ref.shape) - 2):
                total = refs[at][where].astype(F32)
                for k in range(1, count):
                    total += refs[at + k][where].astype(F32)
                out_ref[where] = total.astype(out_ref.dtype)
            at += count

    made = call(body, "halve", ids, tuple(ins), in_specs, tuple(outs), out_specs, (steps,))
    for s, value in zip(sums, made):
        if s.bit is None:
            s.result = value
        else:
            s.got = swap(value, s.bit)
    return made


def after(values, running):
    running = [r for r in running if not r.ready]
    values, got = lax.optimization_barrier((values, [r.got for r in running]))
    for r, g in zip(running, got):
        r.got = g
        r.advance()
    return values


def gathered_pair(ids, refs, order, pair, part, low, high):
    count = refs[0].shape[0]
    at = position(order, 2 * pair, part) ^ position(order, ids[3], ids[0])
    late = at >= count
    at = at % count
    held, last, early, other = [ref[at, low:high] for ref in refs]
    a, b = jnp.where(late, last, held), jnp.where(late, other, early)
    flipped = ids[2] == 1
    return jnp.where(flipped, b, a), jnp.where(flipped, a, b)


def make_qkv(ids, rows, gots, gain, gathered, height):
    parts, local_rows, width = rows.shape
    length = parts * local_rows
    fsdp = width // height
    half = width // parts
    per = local_rows // TILE

    def body(ids, rows_ref, gain_ref, *refs):
        qkv_ref, xt_ref, x_ref, w_ref, wo_ref, blocks_ref = refs[-6:]
        step = pl.program_id(0)

        @pl.when(step == 0)
        def _():
            @pl.loop(0, fsdp // 2)
            def _(pair):
                for t in range(parts):
                    first = 0
                    for c in range(3):
                        args = (ids, refs[4 * c : 4 * c + 4], gathered[c].order, pair, t)
                        for core, rows in enumerate(gathered_pair(*args, 0, height)):
                            start = pl.multiple_of((2 * pair + core) * height, height)
                            w_ref[c, t, pl.ds(start, height)] = rows
                        count = O_ROWS[c]
                        if not count:
                            continue
                        for core, rows in enumerate(
                            gathered_pair(*args, height, height + count)
                        ):
                            start = (2 * pair + core) * height + first
                            wo_ref[t, pl.ds(pl.multiple_of(start, 16), count)] = rows
                        first += count

        @pl.when(step // per == ids[0])
        def _():
            x_ref[...] = rows_ref[0]

        for k in range(per):

            @pl.when((step // per != ids[0]) & (step % per == k))
            def _(k=k):
                x_ref[...] = refs[12 + k][...]

        values = x_ref[...].astype(F32)
        xn = (values * rms_scale(values) * gain_ref[...]).astype(BF)
        for c in range(3):
            for t in range(parts):
                made = dot_f32(xn, w_ref[c, t], 1, 0)
                if c == 0:
                    made = made * HEAD_DIM ** (-0.5)
                qkv_ref[c, :, t * half : (t + 1) * half] = made.astype(BF)
        store_transposed(ids, xn, blocks_ref, xt_ref)

    weights = [a for g in gathered for a in g.arrays]
    return call(
        body,
        "qkv",
        ids,
        (rows, gain, *weights, *gots),
        [
            pl.BlockSpec((1, TILE, width), lambda r, ids: (ids[0], r % per, 0)),
            whole((1, width)),
        ]
        + [whole(a.shape) for a in (*weights, *gots)],
        (
            shape((3, length, width), BF),
            shape((fsdp, height, length), BF),
            shape((length, width), BF),
            shape((3, parts, width, half), BF),
            shape((parts, width, half), BF),
        ),
        [
            pl.BlockSpec((3, TILE, width), lambda r, ids: (0, r, 0)),
            pl.BlockSpec((fsdp, height, TILE), lambda r, ids: (0, 0, r)),
            pl.BlockSpec((TILE, width), lambda r, ids: (r, 0)),
            whole((3, parts, width, half)),
            whole((parts, width, half)),
        ],
        (length // TILE,),
        (pltpu.VMEM((fsdp, height, TILE), BF),),
    )


def store_natural(value, out_ref):
    height = out_ref.shape[-2]
    step = 128 // height
    for c in range(value.shape[1] // 128):
        part = value[:, c * 128 : (c + 1) * 128]
        out_ref[c * step : (c + 1) * step] = part.T.reshape(step, height, part.shape[0])


def join_rows(ids, rows, got):
    parts, local_rows, width = rows.shape
    length = parts * local_rows

    def body(ids, rows_ref, got_ref, out_ref):
        mine = pl.multiple_of(ids[0] * local_rows, local_rows)
        out_ref[0, pl.ds(mine, local_rows)] = rows_ref[0]
        rest = pl.multiple_of((1 - ids[0]) * local_rows, local_rows)
        out_ref[0, pl.ds(rest, local_rows)] = got_ref[0]

    spec = pl.BlockSpec((1, local_rows, width), lambda s, ids: (s ^ ids[0], 0, 0))
    return call(
        body,
        "join_rows",
        ids,
        (rows, got),
        [spec, spec],
        (shape((parts, length, width), BF),),
        [pl.BlockSpec((1, length, width), lambda s, ids: (s, 0, 0))],
        (parts,),
    )[0]


def lane_mask(values, head):
    lanes = lax.broadcasted_iota(jnp.int32, values.shape, 1)
    return jnp.where(lanes // HEAD_DIM == head, values, jnp.zeros_like(values))


def attend(ids, qkv):
    length, width = qkv.shape[1:]
    tiles = length // TILE
    pair = 2 * HEAD_DIM
    heads = width // HEAD_DIM

    def body(ids, q_ref, k_ref, v_ref, *refs):
        o_ref, ot_ref, e_ref, inv_ref, bias_ref, s_ref = refs[-6:]

        @pl.when(pl.program_id(0) == 0)
        def _():
            for i in range(tiles):
                keys = i * TILE + lax.broadcasted_iota(jnp.int32, (2 * TILE, TILE), 0)
                rows = i * TILE + lax.broadcasted_iota(jnp.int32, (2 * TILE, TILE), 1)
                seen = keys <= rows
                for p in range(3):
                    start = ids[4 + p]
                    inside = (keys >= start) & (keys < start + PIECE)
                    inside &= (rows >= start) & (rows < start + PIECE)
                    seen |= inside
                bias_ref[i] = jnp.where(seen, 0.0, masked_score)

        k = k_ref[0]
        vt = v_ref[0].T
        slots = s_ref.shape[0]
        todo = [(i, head) for i in range(tiles) for head in range(2)]
        state = {}

        def score(n):
            i, head = todo[n]
            q_head = lane_mask(q_ref[0, i * TILE : (i + 1) * TILE], head)
            top = None
            for j in range(min(i + 2, tiles)):
                s = dot_f32(k[j * TILE : (j + 1) * TILE], q_head, 1, 1)
                if j >= i:
                    s = s + bias_ref[i, (j - i) * TILE : (j - i + 1) * TILE]
                s_ref[n % slots, j] = s
                now = jnp.max(s.reshape(TILE // 8, 8, TILE), axis=0)
                top = now if top is None else jnp.maximum(top, now)
            state[n] = jnp.max(top, axis=0, keepdims=True)

        def soften(n):
            i, head = todo[n]
            total = None
            for j in range(min(i + 2, tiles)):
                e = jnp.exp(s_ref[n % slots, j] - state[n])
                now = jnp.sum(e.reshape(TILE // 8, 8, TILE), axis=0)
                total = now if total is None else total + now
                e_ref[head, j * TILE : (j + 1) * TILE, i * TILE : (i + 1) * TILE] = e.astype(BF)
            state[n] = 1.0 / jnp.sum(total, axis=0, keepdims=True)
            inv_ref[0, head : head + 1, i * TILE : (i + 1) * TILE] = state[n]

        def gather_values(n):
            i, head = todo[n]
            used = min(i + 2, tiles) * TILE
            out = dot_f32(
                vt[head * HEAD_DIM : (head + 1) * HEAD_DIM, :used],
                e_ref[head, :used, i * TILE : (i + 1) * TILE],
                1,
                0,
            )
            state[n] = out * state[n]
            if head == 1:
                both = jnp.concatenate([state[n - 1], state[n]], axis=0)
                ot_ref[:, i * TILE : (i + 1) * TILE] = both.astype(BF)
                o_ref[i * TILE : (i + 1) * TILE] = both.T.astype(BF)

        for n in range(len(todo) + 2):
            if n < len(todo):
                score(n)
            if 1 <= n <= len(todo):
                soften(n - 1)
            if n >= 2:
                gather_values(n - 2)

    spec = [
        pl.BlockSpec((1, length, pair), lambda p, ids, c=c: (c, 0, p)) for c in range(3)
    ]
    return call(
        body,
        "attend",
        ids,
        (qkv, qkv, qkv),
        spec,
        (
            shape((length, width), BF),
            shape((width, length), BF),
            shape((heads, length, length), BF),
            shape((heads // 2, 2, length), F32),
        ),
        [
            pl.BlockSpec((length, pair), lambda p, ids: (0, p)),
            pl.BlockSpec((pair, length), lambda p, ids: (p, 0)),
            pl.BlockSpec((2, length, length), lambda p, ids: (p, 0, 0)),
            pl.BlockSpec((1, 2, length), lambda p, ids: (p, 0, 0)),
        ],
        (heads // 2,),
        (
            pltpu.VMEM((tiles, 2 * TILE, TILE), F32),
            pltpu.VMEM((4, tiles, TILE, TILE), F32),
        ),
    )


def attend_back(ids, qkv, d_heads, saved):
    length, width = qkv.shape[1:]
    tiles = length // TILE
    pair = 2 * HEAD_DIM
    heads = width // HEAD_DIM

    def body(ids, q_ref, k_ref, v_ref, d_ref, ot_ref, e_ref, inv_ref, *refs):
        out_ref, ds_ref, dq_ref = refs[-3:]
        k = k_ref[0]
        v = v_ref[0]
        kt = k.T
        dt = d_ref[...].astype(F32).T
        q_heads = []
        d_scaled = []
        deltas = []
        for head in range(2):
            span = slice(head * HEAD_DIM, (head + 1) * HEAD_DIM)
            inv_row = inv_ref[0, head : head + 1]
            mine = dt[span] * inv_row
            deltas.append(jnp.sum(mine * ot_ref[span].astype(F32), axis=0, keepdims=True))
            blank = jnp.zeros((HEAD_DIM, length), BF)
            mine = mine.astype(BF)
            d_scaled.append(
                jnp.concatenate([mine, blank] if head == 0 else [blank, mine], axis=0)
            )
            q_heads.append(lane_mask(q_ref[0], head))
        dq_ref[...] = jnp.zeros_like(dq_ref)
        sums = {}

        def scores_back(j, head):
            keys = slice(j * TILE, (j + 1) * TILE)
            for r in range(max(j - 1, 0) * TILE, length, TILE):
                cols = slice(r, r + TILE)
                dp = dot_f32(v[keys], d_scaled[head][:, cols], 1, 0)
                weights = e_ref[head, keys, cols].astype(F32)
                ds_ref[j % 2, head, :, cols] = (weights * (dp - deltas[head][:, cols])).astype(BF)

        def operands_back(j, head):
            keys = slice(j * TILE, (j + 1) * TILE)
            rows = slice(head * HEAD_DIM, (head + 1) * HEAD_DIM)
            first = max(j - 1, 0) * TILE
            ds = ds_ref[j % 2, head, :, first:length]
            d_key = dot_f32(ds, q_heads[head][first:length], 1, 0)
            d_value = dot_f32(
                e_ref[head, keys, first:length], d_scaled[head][:, first:length], 1, 1
            )
            dq_ref[rows, first:length] += dot_f32(kt[rows, keys], ds, 1, 0)
            if head == 0:
                sums[j] = (d_key, d_value)
            else:
                out_ref[1, keys] = (sums[j][0] + d_key).astype(BF)
                out_ref[2, keys] = (sums[j][1] + d_value).astype(BF)

        todo = [(j, head) for j in range(tiles) for head in range(2)]
        for n in range(len(todo) + 1):
            if n < len(todo):
                scores_back(*todo[n])
            if n >= 1:
                operands_back(*todo[n - 1])
        out_ref[0] = (dq_ref[...] * HEAD_DIM ** (-0.5)).T.astype(BF)

    spec = [
        pl.BlockSpec((1, length, pair), lambda p, ids, c=c: (c, 0, p)) for c in range(3)
    ]
    return call(
        body,
        "attend_back",
        ids,
        (qkv, qkv, qkv, d_heads, *saved),
        spec
        + [
            pl.BlockSpec((length, pair), lambda p, ids: (0, p)),
            pl.BlockSpec((pair, length), lambda p, ids: (p, 0)),
            pl.BlockSpec((2, length, length), lambda p, ids: (p, 0, 0)),
            pl.BlockSpec((1, 2, length), lambda p, ids: (p, 0, 0)),
        ],
        (shape((3, length, width), BF),),
        [pl.BlockSpec((3, length, pair), lambda p, ids: (0, 0, p))],
        (heads // 2,),
        (pltpu.VMEM((2, 2, TILE, length), BF), pltpu.VMEM((pair, length), F32)),
    )[0]


def out_project(ids, attended, w_out, x, gain):
    length, width = x.shape
    parts, _, half = w_out.shape

    def body(ids, a_ref, w_ref, x_ref, gain_ref, hidden_ref, hn_ref):
        total = x_ref[...].astype(F32)
        for t in range(parts):
            total += dot_f32(a_ref[:, t * half : (t + 1) * half], w_ref[t], 1, 1)
        hidden_ref[...] = total.astype(BF)
        hn_ref[...] = (total * rms_scale(total) * gain_ref[...]).astype(BF)

    tile = pl.BlockSpec((TILE, width), lambda r, ids: (r, 0))
    return call(
        body,
        "out_project",
        ids,
        (attended, w_out, x, gain),
        [tile, whole(w_out.shape), tile, whole((1, width))],
        (shape((length, width), BF), shape((length, width), BF)),
        [tile, tile],
        (length // TILE,),
    )


def feed_forward(ids, hn, grads, which, packed):
    length, width = hn.shape
    fsdp, rows, units = packed.shape
    height = rows // 3
    tile = 256
    steps = units // tile
    columns = width // steps

    def body(ids, hn_ref, g_ref, w_ref, out_ref, t_ref):
        first = pl.multiple_of(pl.program_id(0) * columns, columns)
        store_natural(hn_ref[:, pl.ds(first, columns)], t_ref.at[0])
        store_natural(g_ref[0, :, pl.ds(first, columns)], t_ref.at[1])
        w_gate, w_up, w_down = [
            w_ref[:, c * height : (c + 1) * height].reshape(width, tile) for c in range(3)
        ]
        for r in range(0, length, TILE):
            rows = hn_ref[r : r + TILE]
            gate = dot_f32(rows, w_gate, 1, 0)
            up = dot_f32(rows, w_up, 1, 0)
            d_mixed = dot_f32(g_ref[0, r : r + TILE], w_down, 1, 0)
            sig = jax.nn.sigmoid(gate)
            act = gate * sig
            out_ref[0, r : r + TILE] = (
                d_mixed * up * sig * (1.0 + gate * (1.0 - sig))
            ).astype(BF)
            out_ref[1, r : r + TILE] = (d_mixed * act).astype(BF)
            out_ref[2, r : r + TILE] = (act * up).astype(BF)

    return call(
        body,
        "feed_forward",
        ids,
        (hn, grads, packed),
        [
            whole((length, width)),
            pl.BlockSpec((1, length, width), lambda n, ids: (which, 0, 0)),
            pl.BlockSpec((fsdp, rows, tile), lambda n, ids: (0, 0, n)),
        ],
        (
            shape((3, length, units), BF),
            shape((2, fsdp, height, length), BF),
        ),
        [
            pl.BlockSpec((3, length, tile), lambda n, ids: (0, 0, n)),
            pl.BlockSpec((2, columns // height, height, length), lambda n, ids: (0, n, 0, 0)),
        ],
        (steps,),
    )


def feed_forward_out(ids, own, theirs, packed, hidden):
    length, width = hidden.shape
    fsdp, rows, units = packed.shape
    height = rows // 3
    kept = length // 2
    per = kept // TILE

    def body(ids, own_ref, theirs_ref, w_ref, hidden_ref, keep_ref, send_ref):
        w = w_ref[...].reshape(width, units)
        mine = pl.program_id(0) == 0
        keeps = pl.program_id(1) >= per

        rows = jnp.where(mine, own_ref[0], theirs_ref[0])
        made = dot_f32(rows, w, 1, 1) + jnp.where(mine, hidden_ref[...].astype(F32), 0.0)

        @pl.when(keeps)
        def _():
            keep_ref[0] = made

        @pl.when(~keeps)
        def _():
            send_ref[0] = made.astype(BF)

    def row(j, ids):
        return jnp.where(j < per, (1 - ids[0]) * per + j, ids[0] * per + j - per)

    return call(
        body,
        "feed_forward_out",
        ids,
        (own, theirs, packed, hidden),
        [
            pl.BlockSpec(
                (1, TILE, units),
                lambda s, j, ids: (2, row(jnp.where(s == 0, j, 2 * per - 1), ids), 0),
            ),
            pl.BlockSpec(
                (1, TILE, units), lambda s, j, ids: (2, row(jnp.where(s == 1, j, 0), ids), 0)
            ),
            pl.BlockSpec((fsdp, height, units), lambda s, j, ids: (0, 2, 0)),
            pl.BlockSpec(
                (TILE, width), lambda s, j, ids: (row(jnp.where(s == 0, j, 2 * per - 1), ids), 0)
            ),
        ],
        (shape((2, kept, width), F32), shape((2, kept, width), BF)),
        [
            pl.BlockSpec(
                (1, TILE, width), lambda s, j, ids: (s ^ ids[0], jnp.maximum(j - per, 0), 0)
            ),
            pl.BlockSpec(
                (1, TILE, width), lambda s, j, ids: (s ^ ids[0], jnp.minimum(j, per - 1), 0)
            ),
        ],
        (2, 2 * per),
    )


def feed_forward_grads(ids, own_t, theirs_t, own, theirs):
    fsdp, height, length = own_t.shape[1:]
    units = own.shape[2]
    per = units // UNITS

    def body(ids, a_ref, b_ref, own_ref, theirs_ref, out_ref):
        for f in range(0, fsdp, 4):
            a = a_ref[0, f : f + 4].reshape(4 * height, length)
            b = b_ref[0, f : f + 4].reshape(4 * height, length)
            made = dot_f32(a, own_ref[0], 1, 0) + dot_f32(b, theirs_ref[0], 1, 0)
            out_ref[f : f + 4] = made.astype(BF).reshape(4, height, UNITS)

    left = pl.BlockSpec((1, fsdp, height, length), lambda c, n, ids: (c // 2, 0, 0, 0))
    right = pl.BlockSpec((1, length, UNITS), lambda c, n, ids: (c, 0, n))
    return call(
        body,
        "feed_forward_grads",
        ids,
        (own_t, theirs_t, own, theirs),
        [left, left, right, right],
        (shape((fsdp, 3 * height, units), BF),),
        [pl.BlockSpec((fsdp, height, UNITS), lambda c, n, ids: (0, c, n))],
        (3, per),
    )[0]


def weight_grad(ids, name, sources):
    fsdp, height, length = sources[0][0].shape
    parts = 2
    half = sources[0][1].shape[2] // parts
    tile = min(UNITS, half)
    per = half // tile
    hop = fsdp // 2

    def body(ids, *refs):
        outs = refs[-2:]
        for k in range(len(sources)):
            l_ref, r_ref = refs[2 * k : 2 * k + 2]

            @pl.when(pl.program_id(0) == k)
            def _(l_ref=l_ref, r_ref=r_ref):
                right_tile = r_ref[0]
                for b in range(0, fsdp, 4):
                    block = l_ref[b : b + 4].reshape(4 * height, length)
                    made = dot_f32(block, right_tile, 1, 0).astype(BF)
                    outs[b // hop][0, b % hop : b % hop + 4] = made.reshape(4, height, tile)

    ins, specs = [], []
    for k, (left, right, index) in enumerate(sources):
        ins += [left, right]

        def columns(c, t, n, ids, k=k, index=index):
            at = n * parts + t
            at = jnp.where(c == k, at, 0 if k else half * parts // tile - 1)
            return (index, 0, at)

        specs += [whole(left.shape), pl.BlockSpec((1, length, tile), columns)]
    spec = pl.BlockSpec((1, hop, height, tile), lambda c, t, n, ids: (t ^ ids[0], 0, c, n))
    return call(
        body,
        name,
        ids,
        tuple(ins),
        specs,
        (shape((parts, hop, len(sources) * height, half), BF),) * 2,
        [spec, spec],
        (len(sources), parts, per),
    )


def feed_forward_back(ids, stacked, packed, half=None):
    length = stacked.shape[1] if half is None else stacked.shape[1] // 2
    at = half or 0
    fsdp, rows, units = packed.shape
    height = rows // 3
    width = fsdp * height
    per = units // UNITS

    def body(ids, d_ref, w_ref, *refs):
        acc_ref = refs[-1]

        @pl.when(pl.program_id(0) == 0)
        def _():
            acc_ref[...] = jnp.zeros_like(acc_ref)

        w_gate, w_up = [
            w_ref[:, c * height : (c + 1) * height].reshape(width, UNITS) for c in range(2)
        ]
        for r in range(0, length, TILE):
            acc_ref[r : r + TILE] += dot_f32(d_ref[0, r : r + TILE], w_gate, 1, 1) + dot_f32(
                d_ref[1, r : r + TILE], w_up, 1, 1
            )

        @pl.when(pl.program_id(0) == per - 1)
        def _():
            refs[0][...] = acc_ref[...].astype(refs[0].dtype)

    return call(
        body,
        "feed_forward_back",
        ids,
        (stacked, packed),
        [
            pl.BlockSpec((2, length, UNITS), lambda n, ids: (0, at, n)),
            pl.BlockSpec((fsdp, 2 * height, UNITS), lambda n, ids: (0, 0, n)),
        ],
        (shape((length, width), BF),),
        [whole((length, width))],
        (per,),
        (pltpu.VMEM((length, width), F32),),
    )[0]


def norm_and_project_back(ids, share, gots, hidden, grads, gain, w_out):
    length, width = hidden.shape
    parts, _, half = w_out.shape
    fsdp = lax.axis_size("fsdp")
    height = width // fsdp
    cut = gots[0].shape[0] // TILE

    def body(ids, share_ref, got_ref, tail_ref, hidden_ref, g_ref, gain_ref, w_ref, *refs):
        low_ref, lt_ref, out_ref, blocks_ref, got_scr = refs

        @pl.when(pl.program_id(0) < cut)
        def _():
            got_scr[...] = got_ref[...]

        @pl.when(pl.program_id(0) >= cut)
        def _():
            got_scr[...] = tail_ref[...]

        rows = hidden_ref[...].astype(F32)
        scale = rms_scale(rows)
        normed = rows * scale
        d_normed = share_ref[...].astype(F32) + got_scr[...].astype(F32)
        dh = g_ref[0].astype(F32) + norm_backward_pass(d_normed, normed, scale, gain_ref[...])
        low = dh.astype(BF)
        low_ref[...] = low
        for t in range(parts):
            out_ref[:, t * half : (t + 1) * half] = dot_f32(low, w_ref[t], 1, 0).astype(BF)
        store_transposed(ids, low, blocks_ref, lt_ref)

    tile = pl.BlockSpec((TILE, width), lambda r, ids: (r, 0))
    return call(
        body,
        "norm_and_project_back",
        ids,
        (share, *gots, hidden, grads, gain, w_out),
        [
            tile,
            pl.BlockSpec((TILE, width), lambda r, ids: (jnp.minimum(r, cut - 1), 0)),
            pl.BlockSpec((TILE, width), lambda r, ids: (jnp.maximum(r - cut, 0), 0)),
            tile,
            pl.BlockSpec((1, TILE, width), lambda r, ids: (0, r, 0)),
            whole((1, width)),
            whole(w_out.shape),
        ],
        (
            shape((length, width), BF),
            shape((fsdp, height, length), BF),
            shape((length, width), BF),
        ),
        [tile, pl.BlockSpec((fsdp, height, TILE), lambda r, ids: (0, 0, r)), tile],
        (length // TILE,),
        (pltpu.VMEM((fsdp, height, TILE), BF), pltpu.VMEM((TILE, width), BF)),
    )


def store_lines(out_ref, values):
    lines = values.shape[1] // 128
    for n in range(lines):
        out_ref[0, pl.ds(n, values.shape[0], stride=lines)] = values[:, n * 128 : (n + 1) * 128]


def qkv_back(ids, d_qkv, weights, x, dh, gain, sent):
    length, width = x.shape
    parts, _, half = weights.shape[1:]
    kept = length // parts
    per = kept // TILE

    def body(ids, d_ref, w_ref, x_ref, dh_ref, gain_ref, out_ref, acc_ref):
        d_normed = None
        for c in range(3):
            for t in range(parts):
                part = dot_f32(d_ref[c, :, t * half : (t + 1) * half], w_ref[c, t], 1, 1)
                d_normed = part if d_normed is None else d_normed + part
        rows = x_ref[...].astype(F32)
        scale = rms_scale(rows)
        made = dh_ref[...].astype(F32) + norm_backward_pass(d_normed, rows * scale, scale, gain_ref[...])
        if sent:
            out_ref[...] = made.astype(BF)
        else:
            acc_ref[...] = made
            store_lines(out_ref, acc_ref)

    def rows(r, ids):
        return per * (1 - ids[0] if sent else ids[0]) + r

    lines = kept * width // 128
    return call(
        body,
        "qkv_back",
        ids,
        (d_qkv, weights, x, dh, gain),
        [
            pl.BlockSpec((3, TILE, width), lambda r, ids: (0, rows(r, ids), 0)),
            whole(weights.shape),
            pl.BlockSpec((TILE, width), lambda r, ids: (rows(r, ids), 0)),
            pl.BlockSpec((TILE, width), lambda r, ids: (rows(r, ids), 0)),
            whole((1, width)),
        ],
        (shape((kept, width), BF) if sent else shape((parts, lines, 128), F32),),
        [
            pl.BlockSpec((TILE, width), lambda r, ids: (r, 0))
            if sent
            else pl.BlockSpec((1, lines // per, 128), lambda r, ids: (ids[0], r, 0)),
        ],
        (per,),
        (pltpu.VMEM((TILE, width), F32),),
    )[0]


def place_rows(ids, got, lines):
    kept, width = got.shape

    def body(ids, got_ref, _, out_ref, wide_ref):
        wide_ref[...] = got_ref[...].astype(F32)
        store_lines(out_ref, wide_ref)

    return call(
        body,
        "place_rows",
        ids,
        (got, lines),
        [whole((kept, width)), IN_PLACE],
        (shape(lines.shape, F32),),
        [pl.BlockSpec((1,) + lines.shape[1:], lambda g, ids: (1 - ids[0], 0, 0))],
        (1,),
        (pltpu.VMEM((kept, width), F32),),
        aliases={2: 0},
    )[0]


def three_parts(values):
    high = values.astype(BF)
    rest = values - high.astype(F32)
    middle = rest.astype(BF)
    return jnp.stack([high, middle, (rest - middle.astype(F32)).astype(BF)], -1)


def local_sequence(
    tokens, piece_starts, gain_attn, w_qkv, w_out, gain_mlp, w_gate_up, w_down, out_grad
):
    fsdp = lax.axis_size("fsdp")
    parts = lax.axis_size("tensor")
    me_f = lax.axis_index("fsdp")
    me_t = lax.axis_index("tensor")
    local_rows = tokens.shape[1]
    height = w_qkv.shape[1]
    half = w_qkv.shape[2]
    share = gain_attn.shape[0]

    starts = lax.dynamic_index_in_dim(piece_starts, me_t, 0, keepdims=False)[0]
    ids = jnp.stack([me_t, me_f // 2, me_f % 2, me_f]).astype(jnp.int32)
    ids = jnp.concatenate([ids, starts])
    rows_in = tokens.reshape(parts, local_rows, D)
    grads_in = out_grad.reshape(parts, local_rows, D)

    def other(rows):
        return lax.dynamic_index_in_dim(rows, 1 - me_t, 0, keepdims=False)

    o_mine = jnp.split(w_out.T, (O_ROWS[0], O_ROWS[0] + O_ROWS[1]))
    wk = Gathered(jnp.concatenate([w_qkv[1], o_mine[1]]), (TENSOR, Z_FAR, X, Z_NEAR))
    wv = Gathered(jnp.concatenate([w_qkv[2], o_mine[2]]), (TENSOR, Z_NEAR, Z_FAR, X))
    gains = three_parts(jnp.stack([gain_attn, gain_mlp])).reshape(1, -1)
    gains = jnp.pad(gains, ((0, 7), (0, half - gains.shape[1])))
    wq = Gathered(
        jnp.concatenate([w_qkv[0], o_mine[0], gains]), (Z_FAR, X, Z_NEAR, TENSOR)
    )
    ff_mine = jnp.concatenate([w_gate_up.reshape(2 * height, -1), w_down.T])
    aways = jnp.split(other(rows_in), 2)
    three = [wq, wk, wv]
    aways[0] = after(aways[0], three)
    got_one = swap(aways[0], TENSOR)
    got_one, aways[1] = after((got_one, aways[1]), three)
    got_two = swap(aways[1], TENSOR)
    got_two = after(got_two, three)
    ff_mine = after(ff_mine, three)
    packed = lax.all_gather(ff_mine, "fsdp", axis=0, tiled=False)
    got_rows = after((got_one, got_two), three)

    each = jnp.arange(fsdp * parts)
    each_f, each_t = each // parts, each % parts
    at = position(wq.order, each_f, each_t) ^ position(wq.order, me_f, me_t)
    at = at + fsdp * ((each_f ^ me_f) % 2)
    row = height + O_ROWS[0]
    gains = jnp.concatenate([a[:, row, : 6 * share] for a in wq.arrays])[at]
    gains = jnp.sum(gains.reshape(fsdp * parts, 2, share, 3).astype(F32), axis=3)
    gain_one, gain_two = [gains[:, i].reshape(1, D) for i in range(2)]

    qkv, xt, x, w_all, wo_all = make_qkv(ids, rows_in, got_rows, gain_one, three, height)
    _, away = lax.optimization_barrier((got_rows, grads_in))
    got_grads = swap(away, TENSOR)
    attended, *saved = attend(ids, qkv)
    hidden, hn = out_project(ids, attended, wo_all, x, gain_two)
    hn_theirs = swap(hn, TENSOR)
    grads = join_rows(ids, grads_in, got_grads)
    hn, grads, packed = lax.optimization_barrier((hn, grads, packed))

    own, own_t = feed_forward(ids, hn, grads, 0, packed)
    own, hn_theirs = lax.optimization_barrier((own, hn_theirs))
    theirs, theirs_t = feed_forward(ids, hn_theirs, grads, 1, packed)
    d_one = feed_forward_back(ids, theirs, packed, 0)
    d_one, theirs, own = lax.optimization_barrier((d_one, theirs, own))
    got_one = swap(d_one, TENSOR)
    made = feed_forward_grads(ids, own_t, theirs_t, own, theirs)
    made, own, theirs, got_one = lax.optimization_barrier((made, own, theirs, got_one))
    summed = lax.psum_scatter(made, "fsdp", scatter_dimension=0, tiled=False)
    d_two = feed_forward_back(ids, theirs, packed, 1)
    d_two, own, theirs = lax.optimization_barrier((d_two, own, theirs))
    got_two = swap(d_two, TENSOR)
    share_own = feed_forward_back(ids, own, packed)
    share_own, own, theirs = lax.optimization_barrier((share_own, own, theirs))
    keep_out, send_out = feed_forward_out(ids, own, theirs, packed, hidden)
    share_own, got_two, send_out = lax.optimization_barrier((share_own, got_two, send_out))
    dh, dt, d_attended = norm_and_project_back(
        ids, share_own, (got_one, got_two), hidden, grads, gain_two, wo_all
    )

    def join(values, sums):
        values, gots = lax.optimization_barrier((values, [s.got for s in sums]))
        for s, g in zip(sums, gots):
            s.got = g
        made = halve(ids, sums)
        return lax.optimization_barrier((values, made))[0]

    o_sum = weight_grad(ids, "grad_out", [(dt, attended[None], 0)])
    o_sum, d_attended, send_out = lax.optimization_barrier((o_sum, d_attended, send_out))
    o_sum = Summed(*o_sum, (X, Z_NEAR, TENSOR, Z_FAR))
    got_out = swap(send_out, TENSOR)
    d_qkv = attend_back(ids, qkv, d_attended, saved)

    d_qkv = join(d_qkv, [o_sum])

    orders = (
        (X, Z_NEAR, TENSOR, Z_FAR),
        (Z_NEAR, X, Z_FAR, TENSOR),
        (TENSOR, Z_FAR, X, Z_NEAR),
    )
    sums = []
    for c, order in enumerate(orders):
        made = weight_grad(ids, "grad_qkv", [(xt, d_qkv, c)])
        made, d_qkv = lax.optimization_barrier((made, d_qkv))
        sums.append(Summed(*made, order))
    d_qkv = join(d_qkv, sums)
    sums.append(o_sum)
    sent = qkv_back(ids, d_qkv, w_all, x, dh, gain_one, True)
    sent, d_qkv, got_out = join((sent, d_qkv, got_out), sums)
    layer_out = (keep_out + got_out.astype(F32)).astype(BF).reshape(tokens.shape)
    got_grad = swap(sent, TENSOR)
    lines = qkv_back(ids, d_qkv, w_all, x, dh, gain_one, False)
    lines, summed = join((lines, summed), sums)
    halve(ids, sums)
    lines, got_grad = lax.optimization_barrier((lines, got_grad))
    input_grad = join(place_rows(ids, got_grad, lines), sums).reshape(tokens.shape)
    qkv_grad = jnp.stack([s.result for s in sums[:3]])
    summed = summed.astype(F32)
    gate_up_grad = summed[: 2 * height].reshape(w_gate_up.shape)
    from_qkv = jnp.sum(w_qkv.astype(F32) * qkv_grad, axis=(0, 2))
    from_gate_up = jnp.sum(w_gate_up.astype(F32) * gate_up_grad, axis=(0, 2))
    both = jnp.stack([from_qkv, from_gate_up]).reshape(2, parts, share)
    mine = lax.dynamic_index_in_dim(both, me_t, 1, keepdims=False)
    theirs = lax.dynamic_index_in_dim(both, 1 - me_t, 1, keepdims=False)
    mine = mine + swap(theirs, TENSOR)
    return (
        layer_out,
        input_grad,
        mine[0] / gain_attn,
        qkv_grad,
        o_sum.result.T,
        mine[1] / gain_mlp,
        gate_up_grad,
        summed[2 * height :].T,
    )


def local_any(tokens, *rest):
    sizes = (lax.axis_size("tensor"), tokens.shape[0], tokens.shape[2], lax.axis_size("fsdp"))
    if sizes == (2, 2, 1, 16):
        return local_sequence(tokens, *rest)
    return local(tokens, *rest)


def solution(mesh):
    return jax.shard_map(
        local_any,
        mesh=mesh,
        in_specs=(
            P(None, "tensor", "fsdp", None),
            P(None, "fsdp", None),
            P(("fsdp", "tensor")),
            P(None, "fsdp", "tensor"),
            P("tensor", "fsdp"),
            P(("fsdp", "tensor")),
            P(None, "fsdp", "tensor"),
            P("tensor", "fsdp"),
            P(None, "tensor", "fsdp", None),
        ),
        out_specs=(
            P(None, "tensor", "fsdp", None),
            P(None, "tensor", "fsdp", None),
            P(("fsdp", "tensor")),
            P(None, "fsdp", "tensor"),
            P("tensor", "fsdp"),
            P(("fsdp", "tensor")),
            P(None, "fsdp", "tensor"),
            P("tensor", "fsdp"),
        ),
        check_vma=False,
    )
```
